512 devices in a mesh: lead: 4 (over x_hi, core), lat: 32 (over x_lo, z), lon: 4 (over y).
Axes of the slice: x: 4 (x_hi: 2, x_lo: 2; x = x_hi * 2 + x_lo), y: 4, z: 16, core: 2. Of those that a mesh axis runs over, the one named last changes fastest.
Arguments:
- head_grads: bfloat16 [8, 8, 128, 128, 128], P('lead', None, 'lat', 'lon'), may hold values from -6 to 6
- head_weights: bfloat16 [8, 9, 256, 128], P('lead'), may hold values from -0.0625 to 0.0625
- encoder_input: bfloat16 [8, 128, 128, 128], P('lead', 'lat', 'lon'), may hold values from -6 to 6
- pre_first: bfloat16 [8, 128, 128, 256], P('lead', 'lat', 'lon'), may hold values from -8 to 8
- pre_second: bfloat16 [8, 128, 128, 256], P('lead', 'lat', 'lon'), may hold values from -8 to 8
- w_first: bfloat16 [9, 128, 256], replicated, may hold values from -0.1875 to 0.1875
- w_second: bfloat16 [9, 256, 256], replicated, may hold values from -0.125 to 0.125
Outputs:
- input_grad: bfloat16 [8, 128, 128, 128], P('lead', 'lat', 'lon')
- weight_grad_first: float32 [294912], P(('lat', 'lon'))
- weight_grad_second: float32 [589824], P(('lat', 'lon'))
The draws below stay inside these ranges and needn't reach their ends.
All inputs are finite; a program needn't handle non-finite values.
Results may differ from the reference program's by a relative error of at most 0.022.
Values may be sent and summed in bfloat16 or wider, within the bound.
A program may use at most 64 MiB of HBM per device.

```python
import jax
import jax.numpy as jnp
from jax import lax

D = 256
HC = 128
C_IN = 128
HEAD_DEV = 2
HEADS = 8
BATCH = 8
ROWS = 128
COLS = 128
N_LEAD = 4


def level_of(key, dims, cuts, smallest, high):
    def one(dim, blocks):
        draws = jax.random.uniform(jax.random.fold_in(jax.random.fold_in(key, 6), dim), (blocks,), jnp.float32, smallest / len(cuts), high / len(cuts))
        return jnp.repeat(jnp.exp(draws), dims[dim] // blocks).reshape((-1,) + (1,) * (len(dims) - dim - 1))

    loudness = one(*cuts[0])
    for cut in cuts[1:]:
        loudness = loudness * one(*cut)
    return loudness


def bell_draw(rng, shape, spread, reach, cuts=(), dtype=jnp.bfloat16):
    factor_of = level_of(rng, shape, cuts, -0.22, 0.18) if cuts else 1.0
    values = jax.random.normal(rng, shape, jnp.float32) * spread * factor_of
    return jnp.minimum(jnp.maximum(values, -reach), reach).astype(dtype)


def setup_inputs(seed: int = 0) -> dict:
    splits = jax.random.split(jax.random.key(seed), 8)
    head_grads = bell_draw(splits[0], (HEADS, BATCH, ROWS, COLS, HC), 1.0, 6.0, ((0, 4), (2, 32), (3, 4)))
    head_weights = bell_draw(splits[1], (HEADS, 9, D, HC), (9 * HC * HEADS) ** -0.5, 0.0625, ((0, 4),))
    encoder_input = bell_draw(splits[2], (BATCH, ROWS, COLS, C_IN), 1.0, 6.0, ((0, 4), (1, 32), (2, 4)))
    pre_first = bell_draw(splits[3], (BATCH, ROWS, COLS, D), 1.5, 8.0, ((0, 4), (1, 32), (2, 4)))
    pre_second = bell_draw(splits[4], (BATCH, ROWS, COLS, D), 1.5, 8.0, ((0, 4), (1, 32), (2, 4)))
    w_first = bell_draw(splits[5], (9, C_IN, D), (9 * C_IN) ** -0.5, 0.1875)
    w_second = bell_draw(splits[6], (9, D, D), (9 * D) ** -0.5, 0.125)
    return {"head_grads": head_grads, "head_weights": head_weights, "encoder_input": encoder_input, "pre_first": pre_first, "pre_second": pre_second, "w_first": w_first, "w_second": w_second}


OFFSETS = [(-1, -1), (-1, 0), (-1, 1), (0, -1), (0, 0), (0, 1), (1, -1), (1, 0), (1, 1)]

def gelu_value(values):
    return 0.5 * values * (1.0 + lax.erf(values * 0.7071067811865476))

def gelu_slope(values):
    return 0.5 * (1.0 + lax.erf(values * 0.7071067811865476)) + values * jnp.exp(-0.5 * values * values) * 0.3989422804014327

def shifted(source, step_row, step_col):
    rolled = jnp.roll(source, -step_col, axis=source.ndim - 2)
    widths = [(0, 0)] * (source.ndim - 3) + [(1, 1), (0, 0), (0, 0)]
    padded = jnp.pad(rolled, widths)
    return lax.slice_in_dim(padded, 1 + step_row, 1 + step_row + ROWS, axis=source.ndim - 3)

def reference(head_grads, head_weights, encoder_input, pre_first, pre_second, w_first, w_second):
    grouped_grads = head_grads.reshape(N_LEAD, HEAD_DEV, BATCH, ROWS, COLS, HC)
    grouped_weights = head_weights.reshape(N_LEAD, HEAD_DEV, 9, D, HC)

    def add_group(carry, pair):
        grads_group, weights_group = pair
        summed = jnp.zeros((BATCH, ROWS, COLS, D), jnp.float32)
        for offset, (step_row, step_col) in enumerate(OFFSETS):
            moved = shifted(grads_group, -step_row, -step_col).astype(jnp.float32)
            summed = summed + jnp.einsum('hbrcj,hdj->brcd', moved, weights_group[:, offset].astype(jnp.float32))
        rounded = lax.optimization_barrier(summed.astype(jnp.bfloat16))
        return (carry + rounded.astype(jnp.float32), None)
    latent_grad, _ = lax.scan(add_group, jnp.zeros((BATCH, ROWS, COLS, D), jnp.float32), (grouped_grads, grouped_weights))
    pre_two = pre_second.astype(jnp.float32)
    pre_one = pre_first.astype(jnp.float32)
    da_second = (latent_grad * gelu_slope(pre_two)).astype(jnp.bfloat16)
    act_first = gelu_value(pre_one).astype(jnp.bfloat16)
    grad_second = []
    linear_first = jnp.zeros((BATCH, ROWS, COLS, D), jnp.float32)
    for offset, (step_row, step_col) in enumerate(OFFSETS):
        grad_second.append(jnp.einsum('brci,brcd->id', shifted(act_first, step_row, step_col).astype(jnp.float32), da_second.astype(jnp.float32)))
        linear_first = linear_first + jnp.einsum('brcd,id->brci', shifted(da_second, -step_row, -step_col).astype(jnp.float32), w_second[offset].astype(jnp.float32))
    da_first = (linear_first * gelu_slope(pre_one)).astype(jnp.bfloat16)
    grad_first = []
    input_sum = jnp.zeros((BATCH, ROWS, COLS, C_IN), jnp.float32)
    for offset, (step_row, step_col) in enumerate(OFFSETS):
        grad_first.append(jnp.einsum('brcj,brcd->jd', shifted(encoder_input, step_row, step_col).astype(jnp.float32), da_first.astype(jnp.float32)))
        input_sum = input_sum + jnp.einsum('brcd,jd->brcj', shifted(da_first, -step_row, -step_col).astype(jnp.float32), w_first[offset].astype(jnp.float32))
    input_grad = input_sum.astype(jnp.bfloat16)
    norm_factor = 1.0 / jnp.sqrt(jnp.float32(BATCH * ROWS * COLS))
    weight_grad_first = (jnp.stack(grad_first) * norm_factor).reshape(-1)
    weight_grad_second = (jnp.stack(grad_second) * norm_factor).reshape(-1)
    return (input_grad, weight_grad_first, weight_grad_second)
```

```python
import functools
import math

import jax
import jax.numpy as jnp
from jax import lax
from jax.experimental import pallas as pl
from jax.experimental.pallas import tpu as pltpu
from jax.sharding import PartitionSpec as P

OFFSETS = [(-1, -1), (-1, 0), (-1, 1), (0, -1), (0, 0), (0, 1), (1, -1), (1, 0), (1, 1)]
MESH = pl.DeviceIdType.MESH
BF = jnp.bfloat16
F32 = jnp.float32
NT = (((1,), (1,)), ((), ()))
NN = (((1,), (0,)), ((), ()))
UNIT = 8


def gelu_value(values):
    return 0.5 * values * (1.0 + lax.erf(values * 0.7071067811865476))


def gelu_slope(values):
    return (
        0.5 * (1.0 + lax.erf(values * 0.7071067811865476))
        + values * jnp.exp(-0.5 * values * values) * 0.3989422804014327
    )


def matmul(a, b, dims):
    return lax.dot_general(a, b, dims, preferred_element_type=F32)


class Place:
    def __init__(self):
        self.lead = lax.axis_index("lead")
        self.lat = lax.axis_index("lat")
        self.lon = lax.axis_index("lon")
        self.n_lead = lax.axis_size("lead")
        self.n_lat = lax.axis_size("lat")
        self.n_lon = lax.axis_size("lon")
        self.planes = self.n_lead * self.n_lon
        self.fold = self.n_lat // self.planes
        self.x = self.lat // self.planes
        self.z = self.lat % self.planes
        self.seat = self.x * self.planes + self.lon * self.n_lead + self.lead
        self.has_low = self.lat > 0
        self.has_high = self.lat < self.n_lat - 1

    def seat_device(self, seat):
        rest = seat % self.planes
        lat = (seat // self.planes) * self.planes + self.z
        return (rest % self.n_lead, lat, rest // self.n_lead)

    def near(self, rows, cols):
        return (self.lead, self.lat + rows, (self.lon + cols + self.n_lon) % self.n_lon)


class Halo:
    def __init__(self, here, rows_out, rows_in, field, edge, ring, send, recv):
        self.here, self.field, self.edge, self.ring = here, field, edge, ring
        self.units = edge.shape[1]
        self.rows = field.shape[0] - 2
        self.batch = field.shape[1]
        self.cols = field.shape[2]
        copies = []
        slot = 0
        for high in (0, 1):
            step = 1 if high == 0 else -1
            sends = here.has_high if high == 0 else here.has_low
            takes = here.has_low if high == 0 else here.has_high
            for source, target in zip(rows_out[high], rows_in[high]):
                copies.append((sends, takes, source, target, here.near(step, 0), slot))
                slot += 1
        self.row_count = slot
        body = pl.ds(1, self.units)
        for right in (0, 1):
            step = 1 if right == 0 else -1
            source = edge.at[1 - right]
            copies.append((None, None, source, ring.at[right, body], here.near(0, step), slot))
            slot += 1
        for high in (0, 1):
            for right in (0, 1):
                row_step = 1 if high == 0 else -1
                col_step = 1 if right == 0 else -1
                sends = here.has_high if high == 0 else here.has_low
                takes = here.has_low if high == 0 else here.has_high
                source = edge.at[1 - right, self.units - 1 if high == 0 else 0]
                target = ring.at[right, 0 if high == 0 else self.units + 1]
                copies.append((sends, takes, source, target, here.near(row_step, col_step), slot))
                slot += 1
        self.copies = [
            (
                sends,
                takes,
                pltpu.make_async_remote_copy(
                    src_ref=source,
                    dst_ref=target,
                    send_sem=send.at[number],
                    recv_sem=recv.at[number],
                    device_id=device,
                    device_id_type=MESH,
                ),
            )
            for sends, takes, source, target, device, number in copies
        ]

    def run(self, items, which, name):
        for item in items:
            if item[which] is None:
                getattr(item[2], name)()
            else:
                pl.when(item[which])(getattr(item[2], name))

    def start_rows(self):
        self.run(self.copies[: self.row_count], 0, "start")

    def start_columns(self):
        self.run(self.copies[self.row_count :], 0, "start")

    def wait_recv(self):
        self.run(self.copies, 1, "wait_recv")

    def wait_send(self):
        self.run(self.copies, 0, "wait_send")

    def clear(self):
        def low():
            self.field[0] = jnp.zeros(self.field.shape[1:], self.field.dtype)
            for side in (0, 1):
                self.ring[side, 0] = jnp.zeros(self.ring.shape[2:], F32)

        def high():
            self.field[self.rows + 1] = jnp.zeros(self.field.shape[1:], self.field.dtype)
            for side in (0, 1):
                self.ring[side, self.units + 1] = jnp.zeros(self.ring.shape[2:], F32)

        pl.when(jnp.logical_not(self.here.has_low))(low)
        pl.when(jnp.logical_not(self.here.has_high))(high)

    def place(self, row, b):
        flat = row * self.batch + b
        return flat // UNIT, flat % UNIT

    def take_edges(self):
        for row in range(self.rows):
            for b in range(self.batch):
                unit, sub = self.place(row, b)
                block = self.field[1 + row, b].astype(F32)
                self.edge[0, unit, sub : sub + 1] = block[0:1]
                self.edge[1, unit, sub : sub + 1] = block[self.cols - 1 : self.cols]

    def ring_row(self, side, ext, b):
        if ext == 0:
            unit, sub = self.place(self.rows - 1, b)
            unit = 0
        elif ext == self.rows + 1:
            unit, sub = self.place(0, b)
            unit = self.units + 1
        else:
            unit, sub = self.place(ext - 1, b)
            unit = unit + 1
        return self.ring[side, unit, sub : sub + 1]

    def spread(self, base, out):
        for ext in range(self.rows + 2):
            for b in range(self.batch):
                block = base[ext, b].astype(F32)
                column = lax.broadcasted_iota(jnp.int32, block.shape, 0)
                behind = jnp.where(
                    column == 0, self.ring_row(0, ext, b), pltpu.roll(block, 1, 0)
                )
                ahead = jnp.where(
                    column == self.cols - 1,
                    self.ring_row(1, ext, b),
                    pltpu.roll(block, self.cols - 1, 0),
                )
                out[0, ext, b] = behind.astype(BF)
                out[1, ext, b] = ahead.astype(BF)


def window(base, spread, step_row, step_col, rows, batch=None):
    row = pl.ds(1 + step_row, rows)
    if step_col == 0:
        view = base[row] if batch is None else base[row, batch]
    else:
        side = 0 if step_col < 0 else 1
        view = spread[side, row] if batch is None else spread[side, row, batch]
    return view.reshape(-1, view.shape[-1])


def kernel(
    norm,
    heads_hbm, head_w_hbm, input_hbm, first_hbm, second_hbm, w_first_hbm, w_second_hbm,
    grad_out, first_out, second_out,
    xh, xh2, eh, rh, head_w,
    xp, xa, xa2, ep, rp,
    xe, xe2, ee, re,
    x2, x22, e2, r2,
    x1, x12, e1, r1,
    pre_two, slope_two, slope_one, w_one, w_two,
    part, parts_in,
    act_t, input_t,
    s1b, q1b, s2b, q2b, s1a, q1a, s2a, q2a,
    grad_stage,
    load_sem, halo_send, halo_recv, lead_send, lead_recv,
    p1_send, p1_recv, p2_send, p2_recv,
):
    here = Place()
    n_lead, planes, n_lon = here.n_lead, here.planes, here.n_lon
    seats = here.fold * planes
    heads, batch_all, rows, cols, head_width = heads_hbm.shape
    samples = input_hbm.shape[0]
    cells = samples * rows * cols

    loads = {}
    count = 0

    def load(key, source, target):
        nonlocal count
        copy = pltpu.make_async_copy(source, target, load_sem.at[count])
        copy.start()
        loads.setdefault(key, []).append(copy)
        count += 1

    for row in range(rows):
        for h in range(heads):
            lanes = pl.ds(h * head_width, head_width)
            load("heads", heads_hbm.at[h, :, row], xh.at[1 + row, :, :, lanes])
    for row in range(rows):
        load("first", first_hbm.at[:, row], xp.at[1 + row])
        load("input", input_hbm.at[:, row], xe.at[1 + row])
    for h in range(heads):
        load("head_w", head_w_hbm.at[h], head_w.at[:, :, pl.ds(h * head_width, head_width)])
    for row in range(rows):
        load("second", second_hbm.at[:, row], pre_two.at[row])
    load("w_two", w_second_hbm, w_two)
    load("w_one", w_first_hbm, w_one)

    def ready(key):
        for copy in loads[key]:
            copy.wait()

    lane = [pl.ds(h * head_width, head_width) for h in range(heads)]
    halo_h = Halo(
        here,
        [[heads_hbm.at[h, :, rows - 1] for h in range(heads)], [heads_hbm.at[h, :, 0] for h in range(heads)]],
        [[xh.at[0, :, :, lane[h]] for h in range(heads)], [xh.at[rows + 1, :, :, lane[h]] for h in range(heads)]],
        xh, eh, rh, halo_send.at[0], halo_recv.at[0],
    )
    halo_p = Halo(
        here,
        [[first_hbm.at[:, rows - 1]], [first_hbm.at[:, 0]]],
        [[xp.at[0]], [xp.at[rows + 1]]],
        xp, ep, rp, halo_send.at[1], halo_recv.at[1],
    )
    halo_e = Halo(
        here,
        [[input_hbm.at[:, rows - 1]], [input_hbm.at[:, 0]]],
        [[xe.at[0]], [xe.at[rows + 1]]],
        xe, ee, re, halo_send.at[2], halo_recv.at[2],
    )
    halo_2 = Halo(
        here, [[x2.at[rows]], [x2.at[1]]], [[x2.at[0]], [x2.at[rows + 1]]],
        x2, e2, r2, halo_send.at[3], halo_recv.at[3],
    )
    halo_1 = Halo(
        here, [[x1.at[rows]], [x1.at[1]]], [[x1.at[0]], [x1.at[rows + 1]]],
        x1, e1, r1, halo_send.at[4], halo_recv.at[4],
    )

    barrier = pltpu.get_barrier_semaphore()

    def greet(device):
        pl.semaphore_signal(barrier, inc=1, device_id=device, device_id_type=MESH)

    for has, step in ((here.has_low, -1), (here.has_high, 1)):

        def greet_rows(step=step):
            for col in (-1, 0, 1):
                greet(here.near(step, col))

        pl.when(has)(greet_rows)

    @pl.loop(1, seats)
    def _(j):
        greet(here.seat_device((here.seat + j) % seats))

    feeder_lon = here.z // n_lead
    feeder_lead = here.z % n_lead
    target_z = here.lon * n_lead + here.lead
    own_feed = jnp.logical_and(here.lon == feeder_lon, here.lead == feeder_lead)

    @pl.loop(0, planes)
    def _(z):
        @pl.when(jnp.logical_not(jnp.logical_and(own_feed, z == here.z)))
        def _():
            greet((feeder_lead, here.x * planes + z, feeder_lon))

    greetings = (
        seats - 1
        + jnp.where(here.has_low, 3, 0)
        + jnp.where(here.has_high, 3, 0)
        + planes
        - jnp.where(here.z == target_z, 1, 0)
    )

    halo_h.clear()
    halo_p.clear()
    halo_e.clear()
    halo_2.clear()
    halo_1.clear()
    ready("heads")
    halo_h.take_edges()
    pl.semaphore_wait(barrier, greetings)
    halo_h.start_rows()
    halo_h.start_columns()
    ready("first")
    halo_p.take_edges()
    halo_p.start_rows()
    halo_p.start_columns()
    ready("input")
    halo_e.take_edges()
    halo_e.start_rows()
    halo_e.start_columns()
    ready("head_w")

    halo_h.wait_recv()
    halo_h.spread(xh, xh2)

    def lead_copy(owner):
        return pltpu.make_async_remote_copy(
            src_ref=part.at[owner],
            dst_ref=parts_in.at[here.lead],
            send_sem=lead_send.at[owner],
            recv_sem=lead_recv.at[here.lead],
            device_id=(owner, here.lat, here.lon),
            device_id_type=MESH,
        )

    @pl.loop(0, n_lead)
    def _(j):
        owner = (here.lead + n_lead - 1 - j) % n_lead
        batch = pl.ds(owner * samples, samples)
        total = jnp.zeros((cells, head_w.shape[1]), F32)
        for k, (u, v) in enumerate(OFFSETS):
            total += matmul(window(xh, xh2, -u, -v, rows, batch), head_w[k], NT)
        part[owner] = total.astype(BF).reshape(part.shape[1:])

        @pl.when(owner != here.lead)
        def _():
            lead_copy(owner).start()

    ready("second")
    for row in range(rows):
        slope_two[row] = gelu_slope(pre_two[row].astype(F32))
        slope_one[row] = gelu_slope(xp[1 + row].astype(F32))
    halo_p.wait_recv()
    for row in range(rows + 2):
        xa[row] = gelu_value(xp[row].astype(F32)).astype(BF)
    for side in (0, 1):
        for unit in range(rp.shape[1]):
            rp[side, unit] = gelu_value(rp[side, unit])
    halo_p.spread(xa, xa2)
    halo_e.wait_recv()
    halo_e.spread(xe, xe2)
    for k, (u, v) in enumerate(OFFSETS):
        block = window(xa, xa2, u, v, rows)
        act_t[pl.ds(k * block.shape[1], block.shape[1])] = block.T
        block = window(xe, xe2, u, v, rows)
        input_t[pl.ds(k * block.shape[1], block.shape[1])] = block.T

    @pl.loop(1, n_lead)
    def _(j):
        owner = (here.lead + j) % n_lead
        pltpu.make_async_remote_copy(
            src_ref=part.at[owner],
            dst_ref=parts_in.at[owner],
            send_sem=lead_send.at[owner],
            recv_sem=lead_recv.at[owner],
            device_id=(owner, here.lat, here.lon),
            device_id_type=MESH,
        ).wait_recv()

    parts_in[here.lead] = part[here.lead]
    for row in range(rows):
        total = parts_in[0, row].astype(F32)
        for a in range(1, n_lead):
            total += parts_in[a, row].astype(F32)
        x2[1 + row] = (total * slope_two[row]).astype(BF)
    halo_2.start_rows()
    halo_2.take_edges()
    halo_2.start_columns()

    def share_copy(stage, sent, taken, send_seat, recv_seat):
        return pltpu.make_async_remote_copy(
            src_ref=sent.at[send_seat],
            dst_ref=taken.at[recv_seat],
            send_sem=p1_send.at[stage, send_seat],
            recv_sem=p1_recv.at[stage, recv_seat],
            device_id=here.seat_device(send_seat),
            device_id_type=MESH,
        )

    def weight_grad(stage, turned, da, sent, taken):
        share = sent.shape[1]
        groups = UNIT
        per = seats // groups
        block = share * per

        @pl.loop(0, groups)
        def _(j):
            group = (here.seat // per + j) % groups
            begin = pl.multiple_of(group * block, block)
            product = matmul(turned[pl.ds(begin, block)], da, NN)
            for t in range(per):
                seat = group * per + t
                sent[seat] = product[t * share : (t + 1) * share].astype(BF)

                @pl.when(seat != here.seat)
                def _():
                    share_copy(stage, sent, taken, seat, here.seat).start()

    def plane_sum(stage, sent, taken):
        taken[here.seat] = sent[here.seat]

        @pl.loop(1, seats)
        def _(j):
            seat = (here.seat + j) % seats
            share_copy(stage, sent, taken, seat, seat).wait_recv()

        return lax.fori_loop(
            0,
            seats,
            lambda seat, total: total + taken[seat].astype(F32),
            jnp.zeros(taken.shape[1:], F32),
        )

    def final_copy(stage, sent, taken, lon, lead):
        return pltpu.make_async_remote_copy(
            src_ref=sent.at[lon],
            dst_ref=taken.at[here.z],
            send_sem=p2_send.at[stage, lon * n_lead + lead],
            recv_sem=p2_recv.at[stage, here.z],
            device_id=(lead, here.x * planes + target_z, lon),
            device_id_type=MESH,
        )

    def not_me(lon, lead):
        same = jnp.logical_and(lon == here.lon, lead == here.lead)
        return jnp.logical_not(jnp.logical_and(same, here.z == target_z))

    def spread_sums(stage, total, sent, taken):
        share = sent.shape[1]
        for lon in range(n_lon):
            sent[lon] = total[lon * share : (lon + 1) * share].astype(BF)

        @pl.loop(0, planes)
        def _(j):
            lon, lead = j // n_lead, j % n_lead

            @pl.when(not_me(lon, lead))
            def _():
                final_copy(stage, sent, taken, lon, lead).start()

        @pl.when(here.z == target_z)
        def _():
            taken[here.z] = sent[here.lon]

    def final_sum(stage, sent, taken, out):
        @pl.loop(0, planes)
        def _(z):
            @pl.when(jnp.logical_not(jnp.logical_and(own_feed, z == here.z)))
            def _():
                pltpu.make_async_remote_copy(
                    src_ref=sent.at[0],
                    dst_ref=taken.at[z],
                    send_sem=p2_send.at[stage, 0],
                    recv_sem=p2_recv.at[stage, z],
                    device_id=(feeder_lead, here.x * planes + z, feeder_lon),
                    device_id_type=MESH,
                ).wait_recv()

        total = taken[0].astype(F32)
        for z in range(1, planes):
            total += taken[z].astype(F32)
        out[...] = total * norm

    def tile(field):
        return field[pl.ds(1, rows)].reshape(cells, field.shape[-1])

    weight_grad(1, act_t, tile(x2), s1b, q1b)

    ready("w_two")
    halo_2.wait_recv()
    halo_2.spread(x2, x22)
    total = jnp.zeros((cells, w_two.shape[1]), F32)
    for k, (u, v) in enumerate(OFFSETS):
        total += matmul(window(x2, x22, -u, -v, rows), w_two[k], NT)
    da_first = total.reshape(slope_one.shape) * slope_one[...]
    x1[pl.ds(1, rows)] = da_first.astype(BF)
    halo_1.start_rows()
    halo_1.take_edges()
    halo_1.start_columns()
    weight_grad(0, input_t, tile(x1), s1a, q1a)

    spread_sums(1, plane_sum(1, s1b, q1b), s2b, q2b)

    ready("w_one")
    halo_1.wait_recv()
    halo_1.spread(x1, x12)
    total = jnp.zeros((cells, w_one.shape[1]), F32)
    for k, (u, v) in enumerate(OFFSETS):
        total += matmul(window(x1, x12, -u, -v, rows), w_one[k], NT)
    grad_stage[...] = total.astype(BF).reshape(grad_stage.shape)
    stores = [
        pltpu.make_async_copy(grad_stage.at[row], grad_out.at[:, row], load_sem.at[row])
        for row in range(rows)
    ]
    for copy in stores:
        copy.start()

    spread_sums(0, plane_sum(0, s1a, q1a), s2a, q2a)
    final_sum(1, s2b, q2b, second_out)
    final_sum(0, s2a, q2a, first_out)

    for copy in stores:
        copy.wait()
    for halo in (halo_h, halo_p, halo_e, halo_2, halo_1):
        halo.wait_send()

    @pl.loop(1, n_lead)
    def _(j):
        lead_copy((here.lead + j) % n_lead).wait_send()

    for stage, sent, taken in ((1, s1b, q1b), (0, s1a, q1a)):

        @pl.loop(1, seats)
        def _(j):
            seat = (here.seat + j) % seats
            share_copy(stage, sent, taken, seat, here.seat).wait_send()

    for stage, sent, taken in ((1, s2b, q2b), (0, s2a, q2a)):

        @pl.loop(0, planes)
        def _(j):
            lon, lead = j // n_lead, j % n_lead

            @pl.when(not_me(lon, lead))
            def _():
                final_copy(stage, sent, taken, lon, lead).wait_send()


def per_device(head_grads, head_weights, encoder_input, pre_first, pre_second, w_first, w_second):
    heads, batch_all, rows, cols, head_width = head_grads.shape
    samples, _, _, in_width = encoder_input.shape
    width = head_weights.shape[2]
    taps = len(OFFSETS)
    n_lead, n_lat, n_lon = lax.axis_size("lead"), lax.axis_size("lat"), lax.axis_size("lon")
    planes = n_lead * n_lon
    seats = n_lat
    lanes = heads * head_width
    cells = samples * rows * cols
    cells_total = cells * n_lead * n_lat * n_lon
    rows_two, rows_one = taps * width, taps * in_width
    share_two, share_one = rows_two // seats, rows_one // seats
    last_two, last_one = share_two // n_lon, share_one // n_lon

    def field(batch, lane):
        full = (rows + 2, batch, cols, lane)
        units = rows * batch // UNIT
        return (
            pltpu.VMEM(full, BF),
            pltpu.VMEM((2,) + full, BF),
            pltpu.VMEM((2, units, UNIT, lane), F32),
            pltpu.VMEM((2, units + 2, UNIT, lane), F32),
        )

    own = (rows, samples, cols, width)
    act_field = field(samples, width)
    scratch = [
        *field(batch_all, lanes),
        pltpu.VMEM((taps, width, lanes), BF),
        act_field[0], *act_field,
        *field(samples, in_width),
        *field(samples, width),
        *field(samples, width),
        pltpu.VMEM(own, BF),
        pltpu.VMEM(own, F32),
        pltpu.VMEM(own, F32),
        pltpu.VMEM(w_first.shape, BF),
        pltpu.VMEM(w_second.shape, BF),
        pltpu.VMEM((n_lead,) + own, BF),
        pltpu.VMEM((n_lead,) + own, BF),
        pltpu.VMEM((rows_two, cells), BF),
        pltpu.VMEM((rows_one, cells), BF),
        pltpu.VMEM((seats, share_two, width), BF),
        pltpu.VMEM((seats, share_two, width), BF),
        pltpu.VMEM((n_lon, last_two, width), BF),
        pltpu.VMEM((planes, last_two, width), BF),
        pltpu.VMEM((seats, share_one, width), BF),
        pltpu.VMEM((seats, share_one, width), BF),
        pltpu.VMEM((n_lon, last_one, width), BF),
        pltpu.VMEM((planes, last_one, width), BF),
        pltpu.VMEM((rows, samples, cols, in_width), BF),
        pltpu.SemaphoreType.DMA((64,)),
        pltpu.SemaphoreType.DMA((5, 16)),
        pltpu.SemaphoreType.DMA((5, 16)),
        pltpu.SemaphoreType.DMA((n_lead,)),
        pltpu.SemaphoreType.DMA((n_lead,)),
        pltpu.SemaphoreType.DMA((2, seats)),
        pltpu.SemaphoreType.DMA((2, seats)),
        pltpu.SemaphoreType.DMA((2, planes)),
        pltpu.SemaphoreType.DMA((2, planes)),
    ]
    anywhere = pl.BlockSpec(memory_space=pl.ANY)
    vmem = pl.BlockSpec(memory_space=pltpu.VMEM)
    input_grad, grad_first, grad_second = pl.pallas_call(
        functools.partial(kernel, 1.0 / math.sqrt(cells_total)),
        out_shape=(
            jax.ShapeDtypeStruct(encoder_input.shape, BF),
            jax.ShapeDtypeStruct((last_one, width), F32),
            jax.ShapeDtypeStruct((last_two, width), F32),
        ),
        in_specs=[anywhere] * 7,
        out_specs=(anywhere, vmem, vmem),
        scratch_shapes=scratch,
        compiler_params=pltpu.CompilerParams(
            collective_id=0, has_side_effects=True, vmem_limit_bytes=48 * 2**20
        ),
    )(head_grads, head_weights, encoder_input, pre_first, pre_second, w_first, w_second)
    return input_grad, grad_first.reshape(-1), grad_second.reshape(-1)


def solution(mesh):
    tile = P("lead", "lat", "lon", None)
    in_specs = (P("lead", None, "lat", "lon", None), P("lead", None, None, None), tile, tile, tile, P(), P())
    out_specs = (tile, P(("lat", "lon")), P(("lat", "lon")))
    return jax.shard_map(
        per_device, mesh=mesh, in_specs=in_specs, out_specs=out_specs, check_vma=False
    )
```

```python
import functools
import math

import jax
import jax.numpy as jnp
from jax import lax
from jax.experimental import pallas as pl
from jax.experimental.pallas import tpu as pltpu
from jax.sharding import PartitionSpec as P

OFFSETS = [(-1, -1), (-1, 0), (-1, 1), (0, -1), (0, 0), (0, 1), (1, -1), (1, 0), (1, 1)]
MESH = pl.DeviceIdType.MESH
BF = jnp.bfloat16
F32 = jnp.float32
NT = (((1,), (1,)), ((), ()))
NN = (((1,), (0,)), ((), ()))
UNIT = 8


def gelu_value(values):
    return 0.5 * values * (1.0 + lax.erf(values * 0.7071067811865476))


def gelu_slope(values):
    return (
        0.5 * (1.0 + lax.erf(values * 0.7071067811865476))
        + values * jnp.exp(-0.5 * values * values) * 0.3989422804014327
    )


def matmul(a, b, dims):
    return lax.dot_general(a, b, dims, preferred_element_type=F32)


class Place:
    def __init__(self):
        self.lead = lax.axis_index("lead")
        self.lat = lax.axis_index("lat")
        self.lon = lax.axis_index("lon")
        self.n_lead = lax.axis_size("lead")
        self.n_lat = lax.axis_size("lat")
        self.n_lon = lax.axis_size("lon")
        self.planes = self.n_lat // 2
        self.side = self.lat // self.planes
        self.z = self.lat % self.planes
        self.far = self.lead // 2
        self.core = self.lead % 2
        self.seats = 4 * self.n_lon
        self.seat = self.seat_of(self.side, self.lon, self.far)
        self.has_low = self.lat > 0
        self.has_high = self.lat < self.n_lat - 1

    def seat_of(self, side, lon, far):
        return (side * self.n_lon + lon) * 2 + far

    def seat_device(self, seat):
        far, lon, side = seat % 2, seat // 2 % self.n_lon, seat // (2 * self.n_lon)
        return (2 * far + self.core, side * self.planes + self.z, lon)

    def lead_device(self, lead):
        return (lead, self.lat, self.lon)

    def plane_device(self, z):
        return (self.lead, self.side * self.planes + z, self.lon)

    def near(self, rows, cols):
        return (self.lead, self.lat + rows, (self.lon + cols + self.n_lon) % self.n_lon)


class Halo:
    def __init__(self, here, rows_out, rows_in, field, edge, ring, send, recv):
        self.here, self.field, self.edge, self.ring = here, field, edge, ring
        self.units = edge.shape[1]
        self.rows = field.shape[0] - 2
        self.batch = field.shape[1]
        self.cols = field.shape[2]
        copies = []
        slot = 0
        for high in (0, 1):
            step = 1 if high == 0 else -1
            sends = here.has_high if high == 0 else here.has_low
            takes = here.has_low if high == 0 else here.has_high
            for source, target in zip(rows_out[high], rows_in[high]):
                copies.append((sends, takes, source, target, here.near(step, 0), slot))
                slot += 1
        self.row_count = slot
        body = pl.ds(1, self.units)
        for right in (0, 1):
            step = 1 if right == 0 else -1
            source = edge.at[1 - right]
            copies.append((None, None, source, ring.at[right, body], here.near(0, step), slot))
            slot += 1
        for high in (0, 1):
            for right in (0, 1):
                row_step = 1 if high == 0 else -1
                col_step = 1 if right == 0 else -1
                sends = here.has_high if high == 0 else here.has_low
                takes = here.has_low if high == 0 else here.has_high
                source = edge.at[1 - right, self.units - 1 if high == 0 else 0]
                target = ring.at[right, 0 if high == 0 else self.units + 1]
                copies.append((sends, takes, source, target, here.near(row_step, col_step), slot))
                slot += 1
        self.copies = [
            (
                sends,
                takes,
                pltpu.make_async_remote_copy(
                    src_ref=source,
                    dst_ref=target,
                    send_sem=send.at[number],
                    recv_sem=recv.at[number],
                    device_id=device,
                    device_id_type=MESH,
                ),
            )
            for sends, takes, source, target, device, number in copies
        ]

    def run(self, items, which, name):
        for item in items:
            if item[which] is None:
                getattr(item[2], name)()
            else:
                pl.when(item[which])(getattr(item[2], name))

    def start_rows(self):
        self.run(self.copies[: self.row_count], 0, "start")

    def start_columns(self):
        self.run(self.copies[self.row_count :], 0, "start")

    def wait_recv(self):
        self.run(self.copies, 1, "wait_recv")

    def wait_send(self):
        self.run(self.copies, 0, "wait_send")

    def clear(self):
        def low():
            self.field[0] = jnp.zeros(self.field.shape[1:], self.field.dtype)
            for side in (0, 1):
                self.ring[side, 0] = jnp.zeros(self.ring.shape[2:], F32)

        def high():
            self.field[self.rows + 1] = jnp.zeros(self.field.shape[1:], self.field.dtype)
            for side in (0, 1):
                self.ring[side, self.units + 1] = jnp.zeros(self.ring.shape[2:], F32)

        pl.when(jnp.logical_not(self.here.has_low))(low)
        pl.when(jnp.logical_not(self.here.has_high))(high)

    def place(self, row, b):
        flat = row * self.batch + b
        return flat // UNIT, flat % UNIT

    def take_edges(self):
        for row in range(self.rows):
            for b in range(self.batch):
                unit, sub = self.place(row, b)
                block = self.field[1 + row, b].astype(F32)
                self.edge[0, unit, sub : sub + 1] = block[0:1]
                self.edge[1, unit, sub : sub + 1] = block[self.cols - 1 : self.cols]

    def ring_row(self, side, ext, b):
        if ext == 0:
            unit, sub = self.place(self.rows - 1, b)
            unit = 0
        elif ext == self.rows + 1:
            unit, sub = self.place(0, b)
            unit = self.units + 1
        else:
            unit, sub = self.place(ext - 1, b)
            unit = unit + 1
        return self.ring[side, unit, sub : sub + 1]

    def spread(self, base, out):
        for ext in range(self.rows + 2):
            for b in range(self.batch):
                block = base[ext, b].astype(F32)
                column = lax.broadcasted_iota(jnp.int32, block.shape, 0)
                behind = jnp.where(
                    column == 0, self.ring_row(0, ext, b), pltpu.roll(block, 1, 0)
                )
                ahead = jnp.where(
                    column == self.cols - 1,
                    self.ring_row(1, ext, b),
                    pltpu.roll(block, self.cols - 1, 0),
                )
                out[0, ext, b] = behind.astype(BF)
                out[1, ext, b] = ahead.astype(BF)


def window(base, spread, step_row, step_col, rows, batch=None):
    row = pl.ds(1 + step_row, rows)
    if step_col == 0:
        view = base[row] if batch is None else base[row, batch]
    else:
        side = 0 if step_col < 0 else 1
        view = spread[side, row] if batch is None else spread[side, row, batch]
    return view.reshape(-1, view.shape[-1])


def kernel(
    norm,
    heads_hbm, head_w_hbm, input_hbm, first_hbm, second_hbm, w_first_hbm, w_second_hbm,
    grad_out, first_out, second_out,
    xh, xh2, eh, rh, head_w,
    xp, xa, xa2, ep, rp,
    xe, xe2, ee, re,
    x2, x22, e2, r2,
    x1, x12, e1, r1,
    pre_two, slope_two, slope_one, w_one, w_two,
    part, parts_in,
    act_t, input_t, act_mate, input_mate, da2_mate, da1_mate,
    s1b, q1b, s2b, q2b, s3b, q3b, s1a, q1a, s2a, q2a, s3a, q3a,
    grad_stage,
    load_sem, halo_send, halo_recv, lead_send, lead_recv, mate_send, mate_recv,
    p1_send, p1_recv, p2_send, p2_recv, p3_send, p3_recv,
):
    here = Place()
    n_lead, planes, n_lon, seats = here.n_lead, here.planes, here.n_lon, here.seats
    half = planes // 2
    heads, batch_all, rows, cols, head_width = heads_hbm.shape
    samples = input_hbm.shape[0]
    cells = samples * rows * cols

    barrier = pltpu.get_barrier_semaphore()

    def greet(device):
        pl.semaphore_signal(barrier, inc=1, device_id=device, device_id_type=MESH)

    for has, step in ((here.has_low, -1), (here.has_high, 1)):

        def greet_rows(step=step):
            for col in (-1, 0, 1):
                greet(here.near(step, col))

        pl.when(has)(greet_rows)

    for col in (-1, 1):
        greet(here.near(0, col))
    for j in range(1, n_lead):
        greet(here.lead_device((here.lead + j) % n_lead))

    @pl.loop(1, seats)
    def _(j):
        greet(here.seat_device((here.seat + j) % seats))

    gathers = here.z // half == here.core
    first_source = (here.z + here.far) % 2
    first_target = here.core * half + first_source

    @pl.when(gathers)
    def _():
        @pl.loop(0, half)
        def _(j):
            z = 2 * j + first_source

            @pl.when(z != here.z)
            def _():
                greet(here.plane_device(z))

    own_share = jnp.logical_and(gathers, here.far == 0)
    greetings = (
        2 + (n_lead - 1) + (seats - 1) + half // 2
        + jnp.where(here.has_low, 3, 0)
        + jnp.where(here.has_high, 3, 0)
        - jnp.where(own_share, 1, 0)
    )

    loads = {}
    count = 0

    def load(key, source, target):
        nonlocal count
        copy = pltpu.make_async_copy(source, target, load_sem.at[count])
        copy.start()
        loads.setdefault(key, []).append(copy)
        count += 1

    for row in range(rows):
        for h in range(heads):
            lanes = pl.ds(h * head_width, head_width)
            load("heads", heads_hbm.at[h, :, row], xh.at[1 + row, :, :, lanes])
    for row in range(rows):
        load("first", first_hbm.at[:, row], xp.at[1 + row])
        load("input", input_hbm.at[:, row], xe.at[1 + row])
    for h in range(heads):
        load("head_w", head_w_hbm.at[h], head_w.at[:, :, pl.ds(h * head_width, head_width)])
    for row in range(rows):
        load("second", second_hbm.at[:, row], pre_two.at[row])
    load("w_two", w_second_hbm, w_two)
    load("w_one", w_first_hbm, w_one)

    def ready(key):
        for copy in loads[key]:
            copy.wait()

    lane = [pl.ds(h * head_width, head_width) for h in range(heads)]
    halo_h = Halo(
        here,
        [[heads_hbm.at[h, :, rows - 1] for h in range(heads)], [heads_hbm.at[h, :, 0] for h in range(heads)]],
        [[xh.at[0, :, :, lane[h]] for h in range(heads)], [xh.at[rows + 1, :, :, lane[h]] for h in range(heads)]],
        xh, eh, rh, halo_send.at[0], halo_recv.at[0],
    )
    halo_p = Halo(
        here,
        [[first_hbm.at[:, rows - 1]], [first_hbm.at[:, 0]]],
        [[xp.at[0]], [xp.at[rows + 1]]],
        xp, ep, rp, halo_send.at[1], halo_recv.at[1],
    )
    halo_e = Halo(
        here,
        [[input_hbm.at[:, rows - 1]], [input_hbm.at[:, 0]]],
        [[xe.at[0]], [xe.at[rows + 1]]],
        xe, ee, re, halo_send.at[2], halo_recv.at[2],
    )
    halo_2 = Halo(
        here, [[x2.at[rows]], [x2.at[1]]], [[x2.at[0]], [x2.at[rows + 1]]],
        x2, e2, r2, halo_send.at[3], halo_recv.at[3],
    )
    halo_1 = Halo(
        here, [[x1.at[rows]], [x1.at[1]]], [[x1.at[0]], [x1.at[rows + 1]]],
        x1, e1, r1, halo_send.at[4], halo_recv.at[4],
    )

    halo_h.clear()
    halo_p.clear()
    halo_e.clear()
    halo_2.clear()
    halo_1.clear()
    ready("heads")
    halo_h.take_edges()
    pl.semaphore_wait(barrier, greetings)
    halo_h.start_rows()
    halo_h.start_columns()
    ready("first")
    halo_p.take_edges()
    halo_p.start_rows()
    halo_p.start_columns()
    ready("input")
    halo_e.take_edges()
    halo_e.start_rows()
    halo_e.start_columns()
    ready("head_w")

    halo_h.wait_recv()
    halo_h.spread(xh, xh2)

    def lead_copy(owner):
        return pltpu.make_async_remote_copy(
            src_ref=part.at[owner],
            dst_ref=parts_in.at[here.lead],
            send_sem=lead_send.at[owner],
            recv_sem=lead_recv.at[here.lead],
            device_id=(owner, here.lat, here.lon),
            device_id_type=MESH,
        )

    @pl.loop(0, n_lead)
    def _(j):
        owner = (here.lead + n_lead - 1 - j) % n_lead
        batch = pl.ds(owner * samples, samples)
        total = jnp.zeros((cells, head_w.shape[1]), F32)
        for k, (u, v) in enumerate(OFFSETS):
            total += matmul(window(xh, xh2, -u, -v, rows, batch), head_w[k], NT)
        part[owner] = total.astype(BF).reshape(part.shape[1:])

        @pl.when(owner != here.lead)
        def _():
            lead_copy(owner).start()

    ready("second")
    for row in range(rows):
        slope_two[row] = gelu_slope(pre_two[row].astype(F32))
        slope_one[row] = gelu_slope(xp[1 + row].astype(F32))
    halo_p.wait_recv()
    for row in range(rows + 2):
        xa[row] = gelu_value(xp[row].astype(F32)).astype(BF)
    for side in (0, 1):
        for unit in range(rp.shape[1]):
            rp[side, unit] = gelu_value(rp[side, unit])
    halo_p.spread(xa, xa2)
    halo_e.wait_recv()
    halo_e.spread(xe, xe2)
    for k, (u, v) in enumerate(OFFSETS):
        block = window(xa, xa2, u, v, rows)
        act_t[pl.ds(k * block.shape[1], block.shape[1])] = block.T
        block = window(xe, xe2, u, v, rows)
        input_t[pl.ds(k * block.shape[1], block.shape[1])] = block.T

    mate = here.lead + 1 - 2 * here.core

    def mate_copy(number, source, target):
        return pltpu.make_async_remote_copy(
            src_ref=source,
            dst_ref=target,
            send_sem=mate_send.at[number],
            recv_sem=mate_recv.at[number],
            device_id=here.lead_device(mate),
            device_id_type=MESH,
        )

    def turned_rows(turned, side, core):
        block = turned.shape[0] // 4
        return pl.ds(pl.multiple_of((2 * side + core) * block, block), block)

    mates = [
        mate_copy(2 * stage + side, turned.at[turned_rows(turned, side, 1 - here.core)], taken.at[side])
        for stage, turned, taken in ((1, act_t, act_mate), (0, input_t, input_mate))
        for side in (0, 1)
    ]
    mates.append(mate_copy(4, x2.at[pl.ds(1, rows)], da2_mate))
    mates.append(mate_copy(5, x1.at[pl.ds(1, rows)], da1_mate))
    for copy in mates[:4]:
        copy.start()

    @pl.loop(1, n_lead)
    def _(j):
        owner = (here.lead + j) % n_lead
        pltpu.make_async_remote_copy(
            src_ref=part.at[owner],
            dst_ref=parts_in.at[owner],
            send_sem=lead_send.at[owner],
            recv_sem=lead_recv.at[owner],
            device_id=(owner, here.lat, here.lon),
            device_id_type=MESH,
        ).wait_recv()

    parts_in[here.lead] = part[here.lead]
    for row in range(rows):
        total = parts_in[0, row].astype(F32)
        for a in range(1, n_lead):
            total += parts_in[a, row].astype(F32)
        x2[1 + row] = (total * slope_two[row]).astype(BF)
    halo_2.start_rows()
    halo_2.take_edges()
    halo_2.start_columns()
    mates[4].start()

    def share_copy(stage, sent, taken, send_seat, recv_seat):
        return pltpu.make_async_remote_copy(
            src_ref=sent.at[send_seat],
            dst_ref=taken.at[recv_seat],
            send_sem=p1_send.at[stage, send_seat],
            recv_sem=p1_recv.at[stage, recv_seat],
            device_id=here.seat_device(send_seat),
            device_id_type=MESH,
        )

    def weight_grad(stage, turned, turned_mate, da, da_mate, sent, taken):
        share = sent.shape[1] * 2 // half
        da_mate = da_mate[...].reshape(da.shape)

        @pl.loop(0, 2)
        def _(j):
            side = (here.side + 1 + j) % 2
            product = matmul(turned[turned_rows(turned, side, here.core)], da, NN)
            product += matmul(turned_mate[side], da_mate, NN)
            for lon in range(n_lon):
                for odd in (0, 1):
                    far = (odd + here.z) % 2
                    seat = here.seat_of(side, lon, far)
                    for t in range(half // 2):
                        begin = ((2 * t + odd) * n_lon + lon) * share
                        piece = product[begin : begin + share].astype(BF)
                        sent[seat, t * share : (t + 1) * share] = piece

            @pl.loop(0, 2 * n_lon)
            def _(i):
                seat = 2 * n_lon * side + (here.seat + 2 + i) % (2 * n_lon)

                @pl.when(seat != here.seat)
                def _():
                    share_copy(stage, sent, taken, seat, here.seat).start()

    def plane_sum(stage, sent, taken):
        taken[here.seat] = sent[here.seat]

        @pl.loop(1, seats)
        def _(j):
            seat = (here.seat + j) % seats
            share_copy(stage, sent, taken, seat, seat).wait_recv()

        total = taken[0].astype(F32)
        for seat in range(1, seats):
            total += taken[seat].astype(F32)
        return total

    def plane_copy(stage, sent, taken, t, slot, z):
        return pltpu.make_async_remote_copy(
            src_ref=sent.at[t],
            dst_ref=taken.at[slot],
            send_sem=p2_send.at[stage, t],
            recv_sem=p2_recv.at[stage, slot],
            device_id=here.plane_device(z),
            device_id_type=MESH,
        )

    def send_planes(stage, total, sent, taken):
        share = sent.shape[1]
        for t in range(half // 2):
            sent[t] = total[t * share : (t + 1) * share].astype(BF)
        for t in range(half // 2):
            z = first_target + 2 * t
            copy = plane_copy(stage, sent, taken, t, here.z // 2, z)
            pl.when(z != here.z)(copy.start)

        @pl.when(own_share)
        def _():
            taken[here.z // 2] = sent[here.z % half // 2]

    def last_copy(stage, sent, taken, lead, slot):
        return pltpu.make_async_remote_copy(
            src_ref=sent,
            dst_ref=taken.at[slot],
            send_sem=p3_send.at[stage, lead],
            recv_sem=p3_recv.at[stage, slot],
            device_id=here.lead_device(lead),
            device_id_type=MESH,
        )

    def send_last(stage, sent, taken, last, last_taken):
        @pl.when(gathers)
        def _():
            for j in range(half):
                z = 2 * j + first_source
                copy = plane_copy(stage, sent, taken, 0, j, z)
                pl.when(z != here.z)(copy.wait_recv)
            total = taken[0].astype(F32)
            for j in range(1, half):
                total += taken[j].astype(F32)
            last[...] = total
            for j in range(1, n_lead):
                last_copy(stage, last, last_taken, (here.lead + j) % n_lead, here.far).start()
            last_taken[here.far] = total

    def final_sum(stage, last, last_taken, out):
        for far in (0, 1):
            source = 2 * far + here.z // half
            copy = last_copy(stage, last, last_taken, source, far)
            pl.when(source != here.lead)(copy.wait_recv)
        out[...] = (last_taken[0] + last_taken[1]) * norm

    def tile(field):
        return field[pl.ds(1, rows)].reshape(cells, field.shape[-1])

    for number in (0, 1, 4):
        mates[number].wait_recv()
    weight_grad(1, act_t, act_mate, tile(x2), da2_mate, s1b, q1b)

    ready("w_two")
    halo_2.wait_recv()
    halo_2.spread(x2, x22)
    total = jnp.zeros((cells, w_two.shape[1]), F32)
    for k, (u, v) in enumerate(OFFSETS):
        total += matmul(window(x2, x22, -u, -v, rows), w_two[k], NT)
    da_first = total.reshape(slope_one.shape) * slope_one[...]
    x1[pl.ds(1, rows)] = da_first.astype(BF)
    halo_1.start_rows()
    halo_1.take_edges()
    halo_1.start_columns()
    mates[5].start()
    for number in (2, 3, 5):
        mates[number].wait_recv()
    weight_grad(0, input_t, input_mate, tile(x1), da1_mate, s1a, q1a)

    send_planes(1, plane_sum(1, s1b, q1b), s2b, q2b)

    ready("w_one")
    halo_1.wait_recv()
    halo_1.spread(x1, x12)
    total = jnp.zeros((cells, w_one.shape[1]), F32)
    for k, (u, v) in enumerate(OFFSETS):
        total += matmul(window(x1, x12, -u, -v, rows), w_one[k], NT)
    grad_stage[...] = total.astype(BF).reshape(grad_stage.shape)
    stores = [
        pltpu.make_async_copy(grad_stage.at[row], grad_out.at[:, row], load_sem.at[row])
        for row in range(rows)
    ]
    for copy in stores:
        copy.start()

    send_planes(0, plane_sum(0, s1a, q1a), s2a, q2a)
    send_last(1, s2b, q2b, s3b, q3b)
    send_last(0, s2a, q2a, s3a, q3a)
    final_sum(1, s3b, q3b, second_out)
    final_sum(0, s3a, q3a, first_out)
    for copy in stores:
        copy.wait()
    for halo in (halo_h, halo_p, halo_e, halo_2, halo_1):
        halo.wait_send()

    for copy in mates:
        copy.wait_send()
    for j in range(1, n_lead):
        lead_copy((here.lead + j) % n_lead).wait_send()

    for stage, sent, taken in ((1, s1b, q1b), (0, s1a, q1a)):

        @pl.loop(1, seats)
        def _(j):
            seat = (here.seat + j) % seats
            share_copy(stage, sent, taken, seat, here.seat).wait_send()

    for stage, sent, taken in ((1, s2b, q2b), (0, s2a, q2a)):
        for t in range(half // 2):
            z = first_target + 2 * t
            copy = plane_copy(stage, sent, taken, t, here.z // 2, z)
            pl.when(z != here.z)(copy.wait_send)

    @pl.when(gathers)
    def _():
        for stage, last, last_taken in ((1, s3b, q3b), (0, s3a, q3a)):
            for j in range(1, n_lead):
                last_copy(stage, last, last_taken, (here.lead + j) % n_lead, here.far).wait_send()


def per_device(head_grads, head_weights, encoder_input, pre_first, pre_second, w_first, w_second):
    heads, batch_all, rows, cols, head_width = head_grads.shape
    samples, _, _, in_width = encoder_input.shape
    width = head_weights.shape[2]
    taps = len(OFFSETS)
    n_lead, n_lat, n_lon = lax.axis_size("lead"), lax.axis_size("lat"), lax.axis_size("lon")
    half = n_lat // 4
    seats = 4 * n_lon
    lanes = heads * head_width
    cells = samples * rows * cols
    cells_total = cells * n_lead * n_lat * n_lon
    rows_two, rows_one = taps * width, taps * in_width
    last_two, last_one = rows_two // (n_lat * n_lon), rows_one // (n_lat * n_lon)

    def field(batch, lane):
        full = (rows + 2, batch, cols, lane)
        units = rows * batch // UNIT
        return (
            pltpu.VMEM(full, BF),
            pltpu.VMEM((2,) + full, BF),
            pltpu.VMEM((2, units, UNIT, lane), F32),
            pltpu.VMEM((2, units + 2, UNIT, lane), F32),
        )

    def reduce_buffers(share):
        return (
            pltpu.VMEM((seats, share * half // 2, width), BF),
            pltpu.VMEM((seats, share * half // 2, width), BF),
            pltpu.VMEM((half // 2, share, width), BF),
            pltpu.VMEM((half, share, width), BF),
            pltpu.VMEM((share, width), F32),
            pltpu.VMEM((2, share, width), F32),
        )

    own = (rows, samples, cols, width)
    act_field = field(samples, width)
    scratch = [
        *field(batch_all, lanes),
        pltpu.VMEM((taps, width, lanes), BF),
        act_field[0], *act_field,
        *field(samples, in_width),
        *field(samples, width),
        *field(samples, width),
        pltpu.VMEM(own, BF),
        pltpu.VMEM(own, F32),
        pltpu.VMEM(own, F32),
        pltpu.VMEM(w_first.shape, BF),
        pltpu.VMEM(w_second.shape, BF),
        pltpu.VMEM((n_lead,) + own, BF),
        pltpu.VMEM((n_lead,) + own, BF),
        pltpu.VMEM((rows_two, cells), BF),
        pltpu.VMEM((rows_one, cells), BF),
        pltpu.VMEM((2, rows_two // 4, cells), BF),
        pltpu.VMEM((2, rows_one // 4, cells), BF),
        pltpu.VMEM(own, BF),
        pltpu.VMEM(own, BF),
        *reduce_buffers(last_two),
        *reduce_buffers(last_one),
        pltpu.VMEM((rows, samples, cols, in_width), BF),
        pltpu.SemaphoreType.DMA((64,)),
        pltpu.SemaphoreType.DMA((5, 16)),
        pltpu.SemaphoreType.DMA((5, 16)),
        pltpu.SemaphoreType.DMA((n_lead,)),
        pltpu.SemaphoreType.DMA((n_lead,)),
        pltpu.SemaphoreType.DMA((6,)),
        pltpu.SemaphoreType.DMA((6,)),
        pltpu.SemaphoreType.DMA((2, seats)),
        pltpu.SemaphoreType.DMA((2, seats)),
        pltpu.SemaphoreType.DMA((2, half // 2)),
        pltpu.SemaphoreType.DMA((2, half)),
        pltpu.SemaphoreType.DMA((2, n_lead)),
        pltpu.SemaphoreType.DMA((2, 2)),
    ]
    anywhere = pl.BlockSpec(memory_space=pl.ANY)
    vmem = pl.BlockSpec(memory_space=pltpu.VMEM)
    input_grad, grad_first, grad_second = pl.pallas_call(
        functools.partial(kernel, 1.0 / math.sqrt(cells_total)),
        out_shape=(
            jax.ShapeDtypeStruct(encoder_input.shape, BF),
            jax.ShapeDtypeStruct((last_one, width), F32),
            jax.ShapeDtypeStruct((last_two, width), F32),
        ),
        in_specs=[anywhere] * 7,
        out_specs=(anywhere, vmem, vmem),
        scratch_shapes=scratch,
        compiler_params=pltpu.CompilerParams(
            collective_id=0, has_side_effects=True, vmem_limit_bytes=48 * 2**20
        ),
    )(head_grads, head_weights, encoder_input, pre_first, pre_second, w_first, w_second)
    return input_grad, grad_first.reshape(-1), grad_second.reshape(-1)


def solution(mesh):
    tile = P("lead", "lat", "lon", None)
    in_specs = (P("lead", None, "lat", "lon", None), P("lead", None, None, None), tile, tile, tile, P(), P())
    out_specs = (tile, P(("lat", "lon")), P(("lat", "lon")))
    return jax.shard_map(
        per_device, mesh=mesh, in_specs=in_specs, out_specs=out_specs, check_vma=False
    )
```

```python
import functools
import math

import jax
import jax.numpy as jnp
from jax import lax
from jax.experimental import pallas as pl
from jax.experimental.pallas import tpu as pltpu
from jax.sharding import PartitionSpec as P

OFFSETS = [(-1, -1), (-1, 0), (-1, 1), (0, -1), (0, 0), (0, 1), (1, -1), (1, 0), (1, 1)]
MESH = pl.DeviceIdType.MESH
BF = jnp.bfloat16
F32 = jnp.float32
NT = (((1,), (1,)), ((), ()))
NN = (((1,), (0,)), ((), ()))
UNIT = 8


def gelu_value(values):
    return 0.5 * values * (1.0 + lax.erf(values * 0.7071067811865476))


def gelu_slope(values):
    return (
        0.5 * (1.0 + lax.erf(values * 0.7071067811865476))
        + values * jnp.exp(-0.5 * values * values) * 0.3989422804014327
    )


def matmul(a, b, dims):
    return lax.dot_general(a, b, dims, preferred_element_type=F32)


class Place:
    def __init__(self):
        self.lead = lax.axis_index("lead")
        self.lat = lax.axis_index("lat")
        self.lon = lax.axis_index("lon")
        self.n_lead = lax.axis_size("lead")
        self.n_lat = lax.axis_size("lat")
        self.n_lon = lax.axis_size("lon")
        self.planes = self.n_lat // 2
        self.side = self.lat // self.planes
        self.z = self.lat % self.planes
        self.far = self.lead // 2
        self.core = self.lead % 2
        self.seats = 4 * self.n_lon
        self.seat = self.seat_of(self.side, self.lon, self.far)
        self.has_low = self.lat > 0
        self.has_high = self.lat < self.n_lat - 1

    def seat_of(self, side, lon, far):
        return (side * self.n_lon + lon) * 2 + far

    def seat_device(self, seat):
        far, lon, side = seat % 2, seat // 2 % self.n_lon, seat // (2 * self.n_lon)
        return (2 * far + self.core, side * self.planes + self.z, lon)

    def lead_device(self, lead):
        return (lead, self.lat, self.lon)

    def plane_device(self, z):
        return (self.lead, self.side * self.planes + z, self.lon)

    def near(self, rows, cols):
        return (self.lead, self.lat + rows, (self.lon + cols + self.n_lon) % self.n_lon)


class Halo:
    def __init__(self, here, rows_out, rows_in, field, edge, ring, send, recv):
        self.here, self.field, self.edge, self.ring = here, field, edge, ring
        self.units = edge.shape[1]
        self.rows = field.shape[0] - 2
        self.batch = field.shape[1]
        self.cols = field.shape[2]
        copies = []
        slot = 0
        for high in (0, 1):
            step = 1 if high == 0 else -1
            sends = here.has_high if high == 0 else here.has_low
            takes = here.has_low if high == 0 else here.has_high
            for source, target in zip(rows_out[high], rows_in[high]):
                copies.append((sends, takes, source, target, here.near(step, 0), slot))
                slot += 1
        self.row_count = slot
        body = pl.ds(1, self.units)
        for right in (0, 1):
            step = 1 if right == 0 else -1
            source = edge.at[1 - right]
            copies.append((None, None, source, ring.at[right, body], here.near(0, step), slot))
            slot += 1
        for high in (0, 1):
            for right in (0, 1):
                row_step = 1 if high == 0 else -1
                col_step = 1 if right == 0 else -1
                sends = here.has_high if high == 0 else here.has_low
                takes = here.has_low if high == 0 else here.has_high
                source = edge.at[1 - right, self.units - 1 if high == 0 else 0]
                target = ring.at[right, 0 if high == 0 else self.units + 1]
                copies.append((sends, takes, source, target, here.near(row_step, col_step), slot))
                slot += 1
        self.copies = [
            (
                sends,
                takes,
                pltpu.make_async_remote_copy(
                    src_ref=source,
                    dst_ref=target,
                    send_sem=send.at[number],
                    recv_sem=recv.at[number],
                    device_id=device,
                    device_id_type=MESH,
                ),
            )
            for sends, takes, source, target, device, number in copies
        ]

    def run(self, items, which, name):
        for item in items:
            if item[which] is None:
                getattr(item[2], name)()
            else:
                pl.when(item[which])(getattr(item[2], name))

    def start_rows(self):
        self.run(self.copies[: self.row_count], 0, "start")

    def start_columns(self):
        self.run(self.copies[self.row_count :], 0, "start")

    def wait_columns(self):
        self.run(self.copies[self.row_count : self.row_count + 2], 1, "wait_recv")

    def wait_side(self, high):
        each = self.row_count // 2
        corner = self.row_count + 2 + 2 * high
        items = self.copies[high * each : (high + 1) * each] + self.copies[corner : corner + 2]
        self.run(items, 1, "wait_recv")

    def wait_recv(self):
        self.wait_columns()
        self.wait_side(0)
        self.wait_side(1)

    def wait_send(self):
        self.run(self.copies, 0, "wait_send")

    def clear(self):
        def low():
            self.field[0] = jnp.zeros(self.field.shape[1:], self.field.dtype)
            for side in (0, 1):
                self.ring[side, 0] = jnp.zeros(self.ring.shape[2:], F32)

        def high():
            self.field[self.rows + 1] = jnp.zeros(self.field.shape[1:], self.field.dtype)
            for side in (0, 1):
                self.ring[side, self.units + 1] = jnp.zeros(self.ring.shape[2:], F32)

        pl.when(jnp.logical_not(self.here.has_low))(low)
        pl.when(jnp.logical_not(self.here.has_high))(high)

    def place(self, row, b):
        flat = row * self.batch + b
        return flat // UNIT, flat % UNIT

    def take_edges(self):
        for row in range(self.rows):
            for b in range(self.batch):
                unit, sub = self.place(row, b)
                block = self.field[1 + row, b].astype(F32)
                self.edge[0, unit, sub : sub + 1] = block[0:1]
                self.edge[1, unit, sub : sub + 1] = block[self.cols - 1 : self.cols]

    def ring_row(self, side, ext, b):
        if ext == 0:
            unit, sub = self.place(self.rows - 1, b)
            unit = 0
        elif ext == self.rows + 1:
            unit, sub = self.place(0, b)
            unit = self.units + 1
        else:
            unit, sub = self.place(ext - 1, b)
            unit = unit + 1
        return self.ring[side, unit, sub : sub + 1]

    def spread(self, base, out, rows=None):
        for ext in range(self.rows + 2) if rows is None else rows:
            for b in range(self.batch):
                block = base[ext, b].astype(F32)
                column = lax.broadcasted_iota(jnp.int32, block.shape, 0)
                behind = jnp.where(
                    column == 0, self.ring_row(0, ext, b), pltpu.roll(block, 1, 0)
                )
                ahead = jnp.where(
                    column == self.cols - 1,
                    self.ring_row(1, ext, b),
                    pltpu.roll(block, self.cols - 1, 0),
                )
                out[0, ext, b] = behind.astype(BF)
                out[1, ext, b] = ahead.astype(BF)


def window(base, spread, step_row, step_col, rows, batch=None, first=0):
    row = pl.ds(1 + first + step_row, rows)
    if step_col == 0:
        view = base[row] if batch is None else base[row, batch]
    else:
        side = 0 if step_col < 0 else 1
        view = spread[side, row] if batch is None else spread[side, row, batch]
    return view.reshape(-1, view.shape[-1])


def kernel(
    norm,
    heads_hbm, head_w_hbm, input_hbm, first_hbm, second_hbm, w_first_hbm, w_second_hbm,
    grad_out, first_out, second_out,
    xh, xh2, eh, rh, head_w,
    xp, xa, xa2, ep, rp,
    xe, xe2, ee, re,
    x2, x22, e2, r2,
    x1, x12, e1, r1,
    pre_two, slope_two, slope_one, w_one, w_two,
    part, parts_in,
    act_t, input_t, act_mate, input_mate, da2_mate, da1_mate,
    s1b, q1b, s2b, q2b, s3b, q3b, s1a, q1a, s2a, q2a, s3a, q3a,
    grad_stage,
    load_sem, halo_send, halo_recv, lead_send, lead_recv, mate_send, mate_recv,
    p1_send, p1_recv, p2_send, p2_recv, p3_send, p3_recv,
):
    here = Place()
    n_lead, planes, n_lon, seats = here.n_lead, here.planes, here.n_lon, here.seats
    half = planes // 2
    heads, batch_all, rows, cols, head_width = heads_hbm.shape
    samples = input_hbm.shape[0]
    cells = samples * rows * cols

    barrier = pltpu.get_barrier_semaphore()

    def greet(device):
        pl.semaphore_signal(barrier, inc=1, device_id=device, device_id_type=MESH)

    for has, step in ((here.has_low, -1), (here.has_high, 1)):

        def greet_rows(step=step):
            for col in (-1, 0, 1):
                greet(here.near(step, col))

        pl.when(has)(greet_rows)

    for col in (-1, 1):
        greet(here.near(0, col))
    for j in range(1, n_lead):
        greet(here.lead_device((here.lead + j) % n_lead))

    @pl.loop(1, seats)
    def _(j):
        greet(here.seat_device((here.seat + j) % seats))

    gathers = here.z // half == here.core
    first_source = (here.z + here.far) % 2
    first_target = here.core * half + first_source

    @pl.when(gathers)
    def _():
        @pl.loop(0, half)
        def _(j):
            z = 2 * j + first_source

            @pl.when(z != here.z)
            def _():
                greet(here.plane_device(z))

    own_share = jnp.logical_and(gathers, here.far == 0)
    greetings = (
        2 + (n_lead - 1) + (seats - 1) + half // 2
        + jnp.where(here.has_low, 3, 0)
        + jnp.where(here.has_high, 3, 0)
        - jnp.where(own_share, 1, 0)
    )

    loads = {}
    count = 0

    def load(key, source, target):
        nonlocal count
        copy = pltpu.make_async_copy(source, target, load_sem.at[count])
        copy.start()
        loads.setdefault(key, []).append(copy)
        count += 1

    for row in range(rows):
        for h in range(heads):
            lanes = pl.ds(h * head_width, head_width)
            load("heads", heads_hbm.at[h, :, row], xh.at[1 + row, :, :, lanes])
    for row in range(rows):
        load("first", first_hbm.at[:, row], xp.at[1 + row])
        load("input", input_hbm.at[:, row], xe.at[1 + row])
    for h in range(heads):
        load("head_w", head_w_hbm.at[h], head_w.at[:, :, pl.ds(h * head_width, head_width)])
    for row in range(rows):
        load("second", second_hbm.at[:, row], pre_two.at[row])
    load("w_two", w_second_hbm, w_two)
    load("w_one", w_first_hbm, w_one)

    def ready(key):
        for copy in loads[key]:
            copy.wait()

    lane = [pl.ds(h * head_width, head_width) for h in range(heads)]
    halo_h = Halo(
        here,
        [[heads_hbm.at[h, :, rows - 1] for h in range(heads)], [heads_hbm.at[h, :, 0] for h in range(heads)]],
        [[xh.at[0, :, :, lane[h]] for h in range(heads)], [xh.at[rows + 1, :, :, lane[h]] for h in range(heads)]],
        xh, eh, rh, halo_send.at[0], halo_recv.at[0],
    )
    halo_p = Halo(
        here,
        [[first_hbm.at[:, rows - 1]], [first_hbm.at[:, 0]]],
        [[xp.at[0]], [xp.at[rows + 1]]],
        xp, ep, rp, halo_send.at[1], halo_recv.at[1],
    )
    halo_e = Halo(
        here,
        [[input_hbm.at[:, rows - 1]], [input_hbm.at[:, 0]]],
        [[xe.at[0]], [xe.at[rows + 1]]],
        xe, ee, re, halo_send.at[2], halo_recv.at[2],
    )
    halo_2 = Halo(
        here, [[x2.at[rows]], [x2.at[1]]], [[x2.at[0]], [x2.at[rows + 1]]],
        x2, e2, r2, halo_send.at[3], halo_recv.at[3],
    )
    halo_1 = Halo(
        here, [[x1.at[rows]], [x1.at[1]]], [[x1.at[0]], [x1.at[rows + 1]]],
        x1, e1, r1, halo_send.at[4], halo_recv.at[4],
    )

    halo_h.clear()
    halo_p.clear()
    halo_e.clear()
    halo_2.clear()
    halo_1.clear()
    pl.semaphore_wait(barrier, greetings)
    halo_h.start_rows()
    ready("heads")
    halo_h.take_edges()
    halo_h.start_columns()
    ready("first")
    halo_p.take_edges()
    halo_p.start_rows()
    halo_p.start_columns()
    ready("input")
    halo_e.take_edges()
    halo_e.start_rows()
    halo_e.start_columns()
    ready("head_w")

    pieces = (pl.ds(1, rows - 2), pl.ds(0, 1), pl.ds(rows - 1, 1))

    def lead_copy(source, owner, piece):
        return pltpu.make_async_remote_copy(
            src_ref=part.at[owner, pieces[piece]],
            dst_ref=parts_in.at[source, pieces[piece]],
            send_sem=lead_send.at[owner, piece],
            recv_sem=lead_recv.at[source, piece],
            device_id=here.lead_device(owner),
            device_id_type=MESH,
        )

    def convolve(first, count, batch):
        total = None
        for k, (u, v) in enumerate(OFFSETS):
            term = matmul(window(xh, xh2, -u, -v, count, batch, first), head_w[k], NT)
            total = term if total is None else total + term
        return total.astype(BF)

    halo_h.wait_columns()
    halo_h.spread(xh, xh2, range(1, rows + 1))
    @pl.loop(0, 2)
    def _(j):
        far = (here.far + 1 + j) % 2
        block = convolve(1, rows - 2, pl.ds(far * 2 * samples, 2 * samples))
        block = block.reshape((rows - 2, 2 * samples) + part.shape[3:])
        for core in (0, 1):
            owner = 2 * far + core
            part[owner, pieces[0]] = block[:, core * samples : (core + 1) * samples]
            copy = lead_copy(here.lead, owner, 0)
            pl.when(owner != here.lead)(copy.start)

    for high in (0, 1):
        halo_h.wait_side(high)
        halo_h.spread(xh, xh2, [(rows + 1) * high])
        block = convolve((rows - 1) * high, 1, pl.ds(0, batch_all)).reshape((batch_all,) + part.shape[3:])
        for owner in range(n_lead):
            part[owner, (rows - 1) * high] = block[owner * samples : (owner + 1) * samples]
        for j in (2, 3, 1):
            lead_copy(here.lead, (here.lead + j) % n_lead, 1 + high).start()

    ready("second")
    for row in range(rows):
        slope_two[row] = gelu_slope(pre_two[row].astype(F32))
        slope_one[row] = gelu_slope(xp[1 + row].astype(F32))
    halo_p.wait_recv()
    for row in range(rows + 2):
        xa[row] = gelu_value(xp[row].astype(F32)).astype(BF)
    for side in (0, 1):
        for unit in range(rp.shape[1]):
            rp[side, unit] = gelu_value(rp[side, unit])
    halo_p.spread(xa, xa2)
    halo_e.wait_recv()
    halo_e.spread(xe, xe2)
    for k, (u, v) in enumerate(OFFSETS):
        block = window(xa, xa2, u, v, rows)
        act_t[pl.ds(k * block.shape[1], block.shape[1])] = block.T
        block = window(xe, xe2, u, v, rows)
        input_t[pl.ds(k * block.shape[1], block.shape[1])] = block.T

    mate = here.lead + 1 - 2 * here.core

    def mate_copy(number, source, target):
        return pltpu.make_async_remote_copy(
            src_ref=source,
            dst_ref=target,
            send_sem=mate_send.at[number],
            recv_sem=mate_recv.at[number],
            device_id=here.lead_device(mate),
            device_id_type=MESH,
        )

    def turned_rows(turned, side, core):
        block = turned.shape[0] // 4
        return pl.ds(pl.multiple_of((2 * side + core) * block, block), block)

    mates = [
        mate_copy(2 * stage + side, turned.at[turned_rows(turned, side, 1 - here.core)], taken.at[side])
        for stage, turned, taken in ((1, act_t, act_mate), (0, input_t, input_mate))
        for side in (0, 1)
    ]
    mates.append(mate_copy(4, x2.at[pl.ds(1, rows)], da2_mate))
    mates.append(mate_copy(5, x1.at[pl.ds(1, rows)], da1_mate))
    for copy in mates[:4]:
        copy.start()

    for j in range(1, n_lead):
        source = (here.lead + j) % n_lead
        for piece in range(len(pieces)):
            lead_copy(source, source, piece).wait_recv()
    parts_in[here.lead] = part[here.lead]
    for row in range(rows):
        total = parts_in[0, row].astype(F32)
        for a in range(1, n_lead):
            total += parts_in[a, row].astype(F32)
        x2[1 + row] = (total * slope_two[row]).astype(BF)
    halo_2.start_rows()
    halo_2.take_edges()
    halo_2.start_columns()
    mates[4].start()

    def share_copy(stage, sent, taken, send_seat, recv_seat):
        return pltpu.make_async_remote_copy(
            src_ref=sent.at[send_seat],
            dst_ref=taken.at[recv_seat],
            send_sem=p1_send.at[stage, send_seat],
            recv_sem=p1_recv.at[stage, recv_seat],
            device_id=here.seat_device(send_seat),
            device_id_type=MESH,
        )

    def weight_grad(stage, turned, turned_mate, da, da_mate, sent, taken, waits):
        share = sent.shape[1] * 2 // half

        @pl.loop(0, 2)
        def _(j):
            side = (here.side + 1 + j) % 2
            product = matmul(turned[turned_rows(turned, side, here.core)], da, NN)

            @pl.when(j == 0)
            def _():
                for number in waits:
                    mates[number].wait_recv()

            product += matmul(turned_mate[side], da_mate[...].reshape(da.shape), NN)
            for lon in range(n_lon):
                for odd in (0, 1):
                    far = (odd + here.z) % 2
                    seat = here.seat_of(side, lon, far)
                    for t in range(half // 2):
                        begin = ((2 * t + odd) * n_lon + lon) * share
                        piece = product[begin : begin + share].astype(BF)
                        sent[seat, t * share : (t + 1) * share] = piece

            @pl.loop(0, 2 * n_lon)
            def _(i):
                seat = 2 * n_lon * side + (here.seat + 2 + i) % (2 * n_lon)

                @pl.when(seat != here.seat)
                def _():
                    share_copy(stage, sent, taken, seat, here.seat).start()

    def plane_sum(stage, sent, taken):
        taken[here.seat] = sent[here.seat]

        @pl.loop(1, seats)
        def _(j):
            seat = (here.seat + j) % seats
            share_copy(stage, sent, taken, seat, seat).wait_recv()

        total = taken[0].astype(F32)
        for seat in range(1, seats):
            total += taken[seat].astype(F32)
        return total

    def plane_copy(stage, sent, taken, t, slot, z):
        return pltpu.make_async_remote_copy(
            src_ref=sent.at[t],
            dst_ref=taken.at[slot],
            send_sem=p2_send.at[stage, t],
            recv_sem=p2_recv.at[stage, slot],
            device_id=here.plane_device(z),
            device_id_type=MESH,
        )

    def send_planes(stage, total, sent, taken):
        share = sent.shape[1]
        for t in range(half // 2):
            sent[t] = total[t * share : (t + 1) * share].astype(BF)
        for t in range(half // 2):
            z = first_target + 2 * t
            copy = plane_copy(stage, sent, taken, t, here.z // 2, z)
            pl.when(z != here.z)(copy.start)

        @pl.when(own_share)
        def _():
            taken[here.z // 2] = sent[here.z % half // 2]

    def last_copy(stage, sent, taken, lead, slot):
        return pltpu.make_async_remote_copy(
            src_ref=sent,
            dst_ref=taken.at[slot],
            send_sem=p3_send.at[stage, lead],
            recv_sem=p3_recv.at[stage, slot],
            device_id=here.lead_device(lead),
            device_id_type=MESH,
        )

    def send_last(stage, sent, taken, last, last_taken):
        @pl.when(gathers)
        def _():
            for j in range(half):
                z = 2 * j + first_source
                copy = plane_copy(stage, sent, taken, 0, j, z)
                pl.when(z != here.z)(copy.wait_recv)
            total = taken[0].astype(F32)
            for j in range(1, half):
                total += taken[j].astype(F32)
            last[...] = total
            for j in range(1, n_lead):
                last_copy(stage, last, last_taken, (here.lead + j) % n_lead, here.far).start()
            last_taken[here.far] = total

    def final_sum(stage, last, last_taken, out):
        for far in (0, 1):
            source = 2 * far + here.z // half
            copy = last_copy(stage, last, last_taken, source, far)
            pl.when(source != here.lead)(copy.wait_recv)
        out[...] = (last_taken[0] + last_taken[1]) * norm

    def tile(field):
        return field[pl.ds(1, rows)].reshape(cells, field.shape[-1])

    weight_grad(1, act_t, act_mate, tile(x2), da2_mate, s1b, q1b, (0, 1, 4))

    ready("w_two")
    halo_2.wait_recv()
    halo_2.spread(x2, x22)
    total = jnp.zeros((cells, w_two.shape[1]), F32)
    for k, (u, v) in enumerate(OFFSETS):
        total += matmul(window(x2, x22, -u, -v, rows), w_two[k], NT)
    da_first = total.reshape(slope_one.shape) * slope_one[...]
    x1[pl.ds(1, rows)] = da_first.astype(BF)
    halo_1.start_rows()
    halo_1.take_edges()
    halo_1.start_columns()
    mates[5].start()
    weight_grad(0, input_t, input_mate, tile(x1), da1_mate, s1a, q1a, (2, 3, 5))

    send_planes(1, plane_sum(1, s1b, q1b), s2b, q2b)

    ready("w_one")
    halo_1.wait_recv()
    halo_1.spread(x1, x12)
    total = jnp.zeros((cells, w_one.shape[1]), F32)
    for k, (u, v) in enumerate(OFFSETS):
        total += matmul(window(x1, x12, -u, -v, rows), w_one[k], NT)
    grad_stage[...] = total.astype(BF).reshape(grad_stage.shape)
    stores = [
        pltpu.make_async_copy(grad_stage.at[row], grad_out.at[:, row], load_sem.at[row])
        for row in range(rows)
    ]
    for copy in stores:
        copy.start()

    send_planes(0, plane_sum(0, s1a, q1a), s2a, q2a)
    send_last(1, s2b, q2b, s3b, q3b)
    send_last(0, s2a, q2a, s3a, q3a)
    for copy in stores:
        copy.wait()
    for halo in (halo_h, halo_p, halo_e, halo_2, halo_1):
        halo.wait_send()

    for copy in mates:
        copy.wait_send()
    for j in range(1, n_lead):
        for piece in range(len(pieces)):
            lead_copy(here.lead, (here.lead + j) % n_lead, piece).wait_send()

    for stage, sent, taken in ((1, s1b, q1b), (0, s1a, q1a)):

        @pl.loop(1, seats)
        def _(j):
            seat = (here.seat + j) % seats
            share_copy(stage, sent, taken, seat, here.seat).wait_send()

    final_sum(1, s3b, q3b, second_out)
    final_sum(0, s3a, q3a, first_out)
    for stage, sent, taken in ((1, s2b, q2b), (0, s2a, q2a)):
        for t in range(half // 2):
            z = first_target + 2 * t
            copy = plane_copy(stage, sent, taken, t, here.z // 2, z)
            pl.when(z != here.z)(copy.wait_send)

    @pl.when(gathers)
    def _():
        for stage, last, last_taken in ((1, s3b, q3b), (0, s3a, q3a)):
            for j in range(1, n_lead):
                last_copy(stage, last, last_taken, (here.lead + j) % n_lead, here.far).wait_send()


def per_device(head_grads, head_weights, encoder_input, pre_first, pre_second, w_first, w_second):
    heads, batch_all, rows, cols, head_width = head_grads.shape
    samples, _, _, in_width = encoder_input.shape
    width = head_weights.shape[2]
    taps = len(OFFSETS)
    n_lead, n_lat, n_lon = lax.axis_size("lead"), lax.axis_size("lat"), lax.axis_size("lon")
    half = n_lat // 4
    seats = 4 * n_lon
    lanes = heads * head_width
    cells = samples * rows * cols
    cells_total = cells * n_lead * n_lat * n_lon
    rows_two, rows_one = taps * width, taps * in_width
    last_two, last_one = rows_two // (n_lat * n_lon), rows_one // (n_lat * n_lon)

    def field(batch, lane):
        full = (rows + 2, batch, cols, lane)
        units = rows * batch // UNIT
        return (
            pltpu.VMEM(full, BF),
            pltpu.VMEM((2,) + full, BF),
            pltpu.VMEM((2, units, UNIT, lane), F32),
            pltpu.VMEM((2, units + 2, UNIT, lane), F32),
        )

    def reduce_buffers(share):
        return (
            pltpu.VMEM((seats, share * half // 2, width), BF),
            pltpu.VMEM((seats, share * half // 2, width), BF),
            pltpu.VMEM((half // 2, share, width), BF),
            pltpu.VMEM((half, share, width), BF),
            pltpu.VMEM((share, width), F32),
            pltpu.VMEM((2, share, width), F32),
        )

    own = (rows, samples, cols, width)
    act_field = field(samples, width)
    scratch = [
        *field(batch_all, lanes),
        pltpu.VMEM((taps, width, lanes), BF),
        act_field[0], *act_field,
        *field(samples, in_width),
        *field(samples, width),
        *field(samples, width),
        pltpu.VMEM(own, BF),
        pltpu.VMEM(own, F32),
        pltpu.VMEM(own, F32),
        pltpu.VMEM(w_first.shape, BF),
        pltpu.VMEM(w_second.shape, BF),
        pltpu.VMEM((n_lead,) + own, BF),
        pltpu.VMEM((n_lead,) + own, BF),
        pltpu.VMEM((rows_two, cells), BF),
        pltpu.VMEM((rows_one, cells), BF),
        pltpu.VMEM((2, rows_two // 4, cells), BF),
        pltpu.VMEM((2, rows_one // 4, cells), BF),
        pltpu.VMEM(own, BF),
        pltpu.VMEM(own, BF),
        *reduce_buffers(last_two),
        *reduce_buffers(last_one),
        pltpu.VMEM((rows, samples, cols, in_width), BF),
        pltpu.SemaphoreType.DMA((64,)),
        pltpu.SemaphoreType.DMA((5, 16)),
        pltpu.SemaphoreType.DMA((5, 16)),
        pltpu.SemaphoreType.DMA((n_lead, 3)),
        pltpu.SemaphoreType.DMA((n_lead, 3)),
        pltpu.SemaphoreType.DMA((6,)),
        pltpu.SemaphoreType.DMA((6,)),
        pltpu.SemaphoreType.DMA((2, seats)),
        pltpu.SemaphoreType.DMA((2, seats)),
        pltpu.SemaphoreType.DMA((2, half // 2)),
        pltpu.SemaphoreType.DMA((2, half)),
        pltpu.SemaphoreType.DMA((2, n_lead)),
        pltpu.SemaphoreType.DMA((2, 2)),
    ]
    anywhere = pl.BlockSpec(memory_space=pl.ANY)
    vmem = pl.BlockSpec(memory_space=pltpu.VMEM)
    input_grad, grad_first, grad_second = pl.pallas_call(
        functools.partial(kernel, 1.0 / math.sqrt(cells_total)),
        out_shape=(
            jax.ShapeDtypeStruct(encoder_input.shape, BF),
            jax.ShapeDtypeStruct((last_one, width), F32),
            jax.ShapeDtypeStruct((last_two, width), F32),
        ),
        in_specs=[anywhere] * 7,
        out_specs=(anywhere, vmem, vmem),
        scratch_shapes=scratch,
        compiler_params=pltpu.CompilerParams(
            collective_id=0, has_side_effects=True, vmem_limit_bytes=56 * 2**20
        ),
    )(head_grads, head_weights, encoder_input, pre_first, pre_second, w_first, w_second)
    return input_grad, grad_first.reshape(-1), grad_second.reshape(-1)


def solution(mesh):
    tile = P("lead", "lat", "lon", None)
    in_specs = (P("lead", None, "lat", "lon", None), P("lead", None, None, None), tile, tile, tile, P(), P())
    out_specs = (tile, P(("lat", "lon")), P(("lat", "lon")))
    return jax.shard_map(
        per_device, mesh=mesh, in_specs=in_specs, out_specs=out_specs, check_vma=False
    )
```

```python
import functools
import math

import jax
import jax.numpy as jnp
from jax import lax
from jax.experimental import pallas as pl
from jax.experimental.pallas import tpu as pltpu
from jax.sharding import PartitionSpec as P

OFFSETS = [(-1, -1), (-1, 0), (-1, 1), (0, -1), (0, 0), (0, 1), (1, -1), (1, 0), (1, 1)]
MESH = pl.DeviceIdType.MESH
BF = jnp.bfloat16
F32 = jnp.float32
NT = (((1,), (1,)), ((), ()))
NN = (((1,), (0,)), ((), ()))
UNIT = 8


def gelu_value(values):
    return 0.5 * values * (1.0 + lax.erf(values * 0.7071067811865476))


def gelu_slope(values):
    return (
        0.5 * (1.0 + lax.erf(values * 0.7071067811865476))
        + values * jnp.exp(-0.5 * values * values) * 0.3989422804014327
    )


def matmul(a, b, dims):
    return lax.dot_general(a, b, dims, preferred_element_type=F32)


class Place:
    def __init__(self):
        self.lead = lax.axis_index("lead")
        self.lat = lax.axis_index("lat")
        self.lon = lax.axis_index("lon")
        self.n_lead = lax.axis_size("lead")
        self.n_lat = lax.axis_size("lat")
        self.n_lon = lax.axis_size("lon")
        self.planes = self.n_lat // 2
        self.side = self.lat // self.planes
        self.z = self.lat % self.planes
        self.far = self.lead // 2
        self.core = self.lead % 2
        self.seats = 4 * self.n_lon
        self.seat = self.seat_of(self.side, self.lon, self.far)
        self.has_low = self.lat > 0
        self.has_high = self.lat < self.n_lat - 1

    def seat_of(self, side, lon, far):
        return (side * self.n_lon + lon) * 2 + far

    def seat_device(self, seat):
        far, lon, side = seat % 2, seat // 2 % self.n_lon, seat // (2 * self.n_lon)
        return (2 * far + self.core, side * self.planes + self.z, lon)

    def lead_device(self, lead):
        return (lead, self.lat, self.lon)

    def plane_device(self, z):
        return (self.lead, self.side * self.planes + z, self.lon)

    def near(self, rows, cols):
        return (self.lead, self.lat + rows, (self.lon + cols + self.n_lon) % self.n_lon)


class Halo:
    def __init__(self, here, rows_out, rows_in, field, edge, ring, send, recv):
        self.here, self.field, self.edge, self.ring = here, field, edge, ring
        self.units = edge.shape[1]
        self.rows = field.shape[0] - 2
        self.batch = field.shape[1]
        self.cols = field.shape[2]
        copies = []
        for high in (0, 1):
            step = 1 if high == 0 else -1
            sends = here.has_high if high == 0 else here.has_low
            for source, target in zip(rows_out[high], rows_in[high]):
                copies.append((sends, source, target, here.near(step, 0), 1 + high))
        self.row_count = len(copies)
        body = pl.ds(1, self.units)
        for right in (0, 1):
            step = 1 if right == 0 else -1
            copies.append((None, edge.at[1 - right], ring.at[right, body], here.near(0, step), 0))
        for high in (0, 1):
            for right in (0, 1):
                row_step = 1 if high == 0 else -1
                col_step = 1 if right == 0 else -1
                sends = here.has_high if high == 0 else here.has_low
                source = edge.at[1 - right, self.units - 1 if high == 0 else 0]
                target = ring.at[right, 0 if high == 0 else self.units + 1]
                copies.append((sends, source, target, here.near(row_step, col_step), 3 + high))

        def remote(source, target, device, number):
            return pltpu.make_async_remote_copy(
                src_ref=source,
                dst_ref=target,
                send_sem=send.at[number],
                recv_sem=recv.at[number],
                device_id=device,
                device_id_type=MESH,
            )

        self.copies = [
            (sends, remote(source, target, device, number))
            for sends, source, target, device, number in copies
        ]
        far_rows = (0, self.rows + 1)
        far_units = (0, self.units + 1)
        self.columns = remote(edge, ring.at[:, body], here.near(0, 1), 0)
        self.row_groups = [
            remote(field.at[far_rows[high]], field.at[far_rows[high]], here.near(0, 1), 1 + high)
            for high in (0, 1)
        ]
        self.corner_groups = [
            remote(edge.at[:, 0], ring.at[:, far_units[high]], here.near(0, 1), 3 + high)
            for high in (0, 1)
        ]

    def start(self, items):
        for sends, copy in items:
            if sends is None:
                copy.start()
            else:
                pl.when(sends)(copy.start)

    def start_rows(self):
        self.start(self.copies[: self.row_count])

    def start_columns(self):
        self.start(self.copies[self.row_count :])

    def wait_columns(self):
        self.columns.wait_recv()

    def wait_side(self, high):
        takes = self.here.has_high if high else self.here.has_low

        @pl.when(takes)
        def _():
            self.row_groups[high].wait_recv()
            self.corner_groups[high].wait_recv()

    def wait_recv(self):
        self.wait_columns()
        self.wait_side(0)
        self.wait_side(1)

    def wait_send(self):
        self.columns.wait_send()
        for high in (0, 1):
            sends = self.here.has_low if high else self.here.has_high

            @pl.when(sends)
            def _(high=high):
                self.row_groups[high].wait_send()
                self.corner_groups[high].wait_send()

    def clear(self):
        def low():
            self.field[0] = jnp.zeros(self.field.shape[1:], self.field.dtype)
            for side in (0, 1):
                self.ring[side, 0] = jnp.zeros(self.ring.shape[2:], F32)

        def high():
            self.field[self.rows + 1] = jnp.zeros(self.field.shape[1:], self.field.dtype)
            for side in (0, 1):
                self.ring[side, self.units + 1] = jnp.zeros(self.ring.shape[2:], F32)

        pl.when(jnp.logical_not(self.here.has_low))(low)
        pl.when(jnp.logical_not(self.here.has_high))(high)

    def place(self, row, b):
        flat = row * self.batch + b
        return flat // UNIT, flat % UNIT

    def take_edges(self):
        for row in range(self.rows):
            for b in range(self.batch):
                unit, sub = self.place(row, b)
                block = self.field[1 + row, b].astype(F32)
                self.edge[0, unit, sub : sub + 1] = block[0:1]
                self.edge[1, unit, sub : sub + 1] = block[self.cols - 1 : self.cols]

    def ring_row(self, side, ext, b):
        if ext == 0:
            unit, sub = self.place(self.rows - 1, b)
            unit = 0
        elif ext == self.rows + 1:
            unit, sub = self.place(0, b)
            unit = self.units + 1
        else:
            unit, sub = self.place(ext - 1, b)
            unit = unit + 1
        return self.ring[side, unit, sub : sub + 1]

    def spread(self, base, out, rows=None):
        for ext in range(self.rows + 2) if rows is None else rows:
            for b in range(self.batch):
                block = base[ext, b].astype(F32)
                column = lax.broadcasted_iota(jnp.int32, block.shape, 0)
                behind = jnp.where(
                    column == 0, self.ring_row(0, ext, b), pltpu.roll(block, 1, 0)
                )
                ahead = jnp.where(
                    column == self.cols - 1,
                    self.ring_row(1, ext, b),
                    pltpu.roll(block, self.cols - 1, 0),
                )
                out[0, ext, b] = behind.astype(BF)
                out[1, ext, b] = ahead.astype(BF)


def window(base, spread, step_row, step_col, rows, batch=None, first=0):
    row = pl.ds(1 + first + step_row, rows)
    if step_col == 0:
        view = base[row] if batch is None else base[row, batch]
    else:
        side = 0 if step_col < 0 else 1
        view = spread[side, row] if batch is None else spread[side, row, batch]
    return view.reshape(-1, view.shape[-1])


def kernel(
    norm,
    heads_hbm, head_w_hbm, input_hbm, first_hbm, second_hbm, w_first_hbm, w_second_hbm,
    grad_out, first_out, second_out,
    xh, xh2, eh, rh, head_w,
    xp, xa, xa2, ep, rp,
    xe, xe2, ee, re,
    x2, x22, e2, r2,
    x1, x12, e1, r1,
    pre_two, slope_two, slope_one, w_one, w_two,
    part, parts_in,
    act_t, input_t, act_mate, input_mate, da2_mate, da1_mate,
    s1b, q1b, s2b, q2b, s3b, q3b, s1a, q1a, s2a, q2a, s3a, q3a,
    grad_stage,
    load_sem, halo_send, halo_recv, lead_send, lead_recv, mate_send, mate_recv,
    p1_send, p1_recv, p2_send, p2_recv, p3_send, p3_recv,
):
    here = Place()
    n_lead, planes, n_lon, seats = here.n_lead, here.planes, here.n_lon, here.seats
    half = planes // 2
    heads, batch_all, rows, cols, head_width = heads_hbm.shape
    samples = input_hbm.shape[0]
    cells = samples * rows * cols

    barrier = pltpu.get_barrier_semaphore()

    def greet(device):
        pl.semaphore_signal(barrier, inc=1, device_id=device, device_id_type=MESH)

    for has, step in ((here.has_low, -1), (here.has_high, 1)):

        def greet_rows(step=step):
            for col in (-1, 0, 1):
                greet(here.near(step, col))

        pl.when(has)(greet_rows)

    for col in (-1, 1):
        greet(here.near(0, col))
    for j in range(1, n_lead):
        greet(here.lead_device((here.lead + j) % n_lead))

    @pl.loop(1, seats)
    def _(j):
        greet(here.seat_device((here.seat + j) % seats))

    gathers = here.z // half == here.core
    first_source = (here.z + here.far) % 2
    first_target = here.core * half + first_source

    @pl.when(gathers)
    def _():
        @pl.loop(0, half)
        def _(j):
            z = 2 * j + first_source

            @pl.when(z != here.z)
            def _():
                greet(here.plane_device(z))

    own_share = jnp.logical_and(gathers, here.far == 0)
    greetings = (
        2 + (n_lead - 1) + (seats - 1) + half // 2
        + jnp.where(here.has_low, 3, 0)
        + jnp.where(here.has_high, 3, 0)
        - jnp.where(own_share, 1, 0)
    )

    names = ("heads", "first", "input", "head_w", "second", "w_two", "w_one", "out")
    body = pl.ds(1, rows)
    whole = {
        "heads": xh.at[body], "first": xp.at[body], "input": xe.at[body], "head_w": head_w,
        "second": pre_two, "w_two": w_two, "w_one": w_one, "out": grad_stage,
    }

    def load(key, source, target):
        pltpu.make_async_copy(source, target, load_sem.at[names.index(key)]).start()

    for row in range(rows):
        for h in range(heads):
            lanes = pl.ds(h * head_width, head_width)
            load("heads", heads_hbm.at[h, :, row], xh.at[1 + row, :, :, lanes])
    for row in range(rows):
        load("first", first_hbm.at[:, row], xp.at[1 + row])
        load("input", input_hbm.at[:, row], xe.at[1 + row])
    for h in range(heads):
        load("head_w", head_w_hbm.at[h], head_w.at[:, :, pl.ds(h * head_width, head_width)])
    for row in range(rows):
        load("second", second_hbm.at[:, row], pre_two.at[row])
    load("w_two", w_second_hbm, w_two)
    load("w_one", w_first_hbm, w_one)

    def ready(key):
        pltpu.make_async_copy(whole[key], whole[key], load_sem.at[names.index(key)]).wait()

    lane = [pl.ds(h * head_width, head_width) for h in range(heads)]
    halo_h = Halo(
        here,
        [[heads_hbm.at[h, :, rows - 1] for h in range(heads)], [heads_hbm.at[h, :, 0] for h in range(heads)]],
        [[xh.at[0, :, :, lane[h]] for h in range(heads)], [xh.at[rows + 1, :, :, lane[h]] for h in range(heads)]],
        xh, eh, rh, halo_send.at[0], halo_recv.at[0],
    )
    halo_p = Halo(
        here,
        [[first_hbm.at[:, rows - 1]], [first_hbm.at[:, 0]]],
        [[xp.at[0]], [xp.at[rows + 1]]],
        xp, ep, rp, halo_send.at[1], halo_recv.at[1],
    )
    halo_e = Halo(
        here,
        [[input_hbm.at[:, rows - 1]], [input_hbm.at[:, 0]]],
        [[xe.at[0]], [xe.at[rows + 1]]],
        xe, ee, re, halo_send.at[2], halo_recv.at[2],
    )
    halo_2 = Halo(
        here, [[x2.at[rows]], [x2.at[1]]], [[x2.at[0]], [x2.at[rows + 1]]],
        x2, e2, r2, halo_send.at[3], halo_recv.at[3],
    )
    halo_1 = Halo(
        here, [[x1.at[rows]], [x1.at[1]]], [[x1.at[0]], [x1.at[rows + 1]]],
        x1, e1, r1, halo_send.at[4], halo_recv.at[4],
    )

    halo_h.clear()
    halo_p.clear()
    halo_e.clear()
    halo_2.clear()
    halo_1.clear()
    pl.semaphore_wait(barrier, greetings)
    halo_h.start_rows()
    ready("heads")
    halo_h.take_edges()
    halo_h.start_columns()
    ready("first")
    halo_p.take_edges()
    halo_p.start_rows()
    halo_p.start_columns()
    ready("input")
    halo_e.take_edges()
    halo_e.start_rows()
    halo_e.start_columns()
    ready("head_w")

    pieces = (pl.ds(1, rows - 2), pl.ds(0, 1), pl.ds(rows - 1, 1))

    others = pl.ds(0, n_lead - 1)
    lead_group = pltpu.make_async_remote_copy(
        src_ref=part.at[others],
        dst_ref=parts_in.at[others],
        send_sem=lead_send.at[0],
        recv_sem=lead_recv.at[0],
        device_id=here.near(0, 1),
        device_id_type=MESH,
    )

    def lead_copy(source, owner, piece):
        return pltpu.make_async_remote_copy(
            src_ref=part.at[owner, pieces[piece]],
            dst_ref=parts_in.at[source, pieces[piece]],
            send_sem=lead_send.at[0],
            recv_sem=lead_recv.at[0],
            device_id=here.lead_device(owner),
            device_id_type=MESH,
        )

    def convolve(first, count, batch):
        total = None
        for k, (u, v) in enumerate(OFFSETS):
            term = matmul(window(xh, xh2, -u, -v, count, batch, first), head_w[k], NT)
            total = term if total is None else total + term
        return total.astype(BF)

    halo_h.wait_columns()
    halo_h.spread(xh, xh2, range(1, rows + 1))
    @pl.loop(0, 2)
    def _(j):
        far = (here.far + 1 + j) % 2
        block = convolve(1, rows - 2, pl.ds(far * 2 * samples, 2 * samples))
        block = block.reshape((rows - 2, 2 * samples) + part.shape[3:])
        for core in (0, 1):
            owner = 2 * far + core
            part[owner, pieces[0]] = block[:, core * samples : (core + 1) * samples]
            copy = lead_copy(here.lead, owner, 0)
            pl.when(owner != here.lead)(copy.start)

    for high in (0, 1):
        halo_h.wait_side(high)
        halo_h.spread(xh, xh2, [(rows + 1) * high])
        block = convolve((rows - 1) * high, 1, pl.ds(0, batch_all)).reshape((batch_all,) + part.shape[3:])
        for owner in range(n_lead):
            part[owner, (rows - 1) * high] = block[owner * samples : (owner + 1) * samples]
        for j in (2, 3, 1):
            lead_copy(here.lead, (here.lead + j) % n_lead, 1 + high).start()

    ready("second")
    for row in range(rows):
        slope_two[row] = gelu_slope(pre_two[row].astype(F32))
        slope_one[row] = gelu_slope(xp[1 + row].astype(F32))
    halo_p.wait_recv()
    for row in range(rows + 2):
        xa[row] = gelu_value(xp[row].astype(F32)).astype(BF)
    for side in (0, 1):
        for unit in range(rp.shape[1]):
            rp[side, unit] = gelu_value(rp[side, unit])
    halo_p.spread(xa, xa2)
    halo_e.wait_recv()
    halo_e.spread(xe, xe2)
    for k, (u, v) in enumerate(OFFSETS):
        block = window(xa, xa2, u, v, rows)
        act_t[pl.ds(k * block.shape[1], block.shape[1])] = block.T
        block = window(xe, xe2, u, v, rows)
        input_t[pl.ds(k * block.shape[1], block.shape[1])] = block.T

    mate = here.lead + 1 - 2 * here.core

    def mate_copy(number, source, target):
        return pltpu.make_async_remote_copy(
            src_ref=source,
            dst_ref=target,
            send_sem=mate_send.at[number],
            recv_sem=mate_recv.at[number],
            device_id=here.lead_device(mate),
            device_id_type=MESH,
        )

    def turned_rows(turned, side, core):
        block = turned.shape[0] // 4
        return pl.ds(pl.multiple_of((2 * side + core) * block, block), block)

    for stage, turned, taken in ((1, act_t, act_mate), (0, input_t, input_mate)):
        for side in (0, 1):
            rows_there = turned_rows(turned, side, 1 - here.core)
            mate_copy(stage, turned.at[rows_there], taken.at[side]).start()
    mates = [
        mate_copy(0, input_mate, input_mate),
        mate_copy(1, act_mate, act_mate),
        mate_copy(2, x1.at[body], da1_mate),
        mate_copy(3, x2.at[body], da2_mate),
    ]

    lead_group.wait_recv()
    parts_in[here.lead] = part[here.lead]
    for row in range(rows):
        total = parts_in[0, row].astype(F32)
        for a in range(1, n_lead):
            total += parts_in[a, row].astype(F32)
        x2[1 + row] = (total * slope_two[row]).astype(BF)
    halo_2.start_rows()
    halo_2.take_edges()
    halo_2.start_columns()
    mates[3].start()

    def share_copy(stage, sent, taken, send_seat, recv_seat, device=None):
        return pltpu.make_async_remote_copy(
            src_ref=sent.at[send_seat],
            dst_ref=taken.at[recv_seat],
            send_sem=p1_send.at[stage],
            recv_sem=p1_recv.at[stage],
            device_id=here.seat_device(send_seat) if device is None else device,
            device_id_type=MESH,
        )

    def share_group(stage, sent, taken):
        every = pl.ds(0, seats - 1)
        return share_copy(stage, sent, taken, every, every, here.near(0, 1))

    def weight_grad(stage, turned, turned_mate, da, da_mate, sent, taken):
        share = sent.shape[1] * 2 // half

        @pl.loop(0, 2)
        def _(j):
            side = (here.side + 1 + j) % 2
            product = matmul(turned[turned_rows(turned, side, here.core)], da, NN)

            @pl.when(j == 0)
            def _():
                mates[stage].wait_recv()
                mates[2 + stage].wait_recv()

            product += matmul(turned_mate[side], da_mate[...].reshape(da.shape), NN)
            for lon in range(n_lon):
                for odd in (0, 1):
                    far = (odd + here.z) % 2
                    seat = here.seat_of(side, lon, far)
                    for t in range(half // 2):
                        begin = ((2 * t + odd) * n_lon + lon) * share
                        piece = product[begin : begin + share].astype(BF)
                        sent[seat, t * share : (t + 1) * share] = piece

            @pl.loop(0, 2 * n_lon)
            def _(i):
                seat = 2 * n_lon * side + (here.seat + 2 + i) % (2 * n_lon)

                @pl.when(seat != here.seat)
                def _():
                    share_copy(stage, sent, taken, seat, here.seat).start()

    def plane_sum(stage, sent, taken):
        taken[here.seat] = sent[here.seat]

        share_group(stage, sent, taken).wait_recv()
        total = taken[0].astype(F32)
        for seat in range(1, seats):
            total += taken[seat].astype(F32)
        return total

    def plane_copy(stage, sent, taken, t, slot, z):
        return pltpu.make_async_remote_copy(
            src_ref=sent.at[t],
            dst_ref=taken.at[slot],
            send_sem=p2_send.at[stage],
            recv_sem=p2_recv.at[stage],
            device_id=here.plane_device(z),
            device_id_type=MESH,
        )

    def send_planes(stage, total, sent, taken):
        share = sent.shape[1]
        for t in range(half // 2):
            sent[t] = total[t * share : (t + 1) * share].astype(BF)
        for t in range(half // 2):
            z = first_target + 2 * t
            copy = plane_copy(stage, sent, taken, t, here.z // 2, z)
            pl.when(z != here.z)(copy.start)

        @pl.when(own_share)
        def _():
            taken[here.z // 2] = sent[here.z % half // 2]

    def plane_group(stage, sent, taken, own, act):
        count = half // 2 if act == "wait_send" else half
        for less in (0, 1):
            every = pl.ds(0, count - less)
            ref = sent.at[every] if act == "wait_send" else taken.at[every]
            group = pltpu.make_async_remote_copy(
                src_ref=ref,
                dst_ref=ref,
                send_sem=p2_send.at[stage],
                recv_sem=p2_recv.at[stage],
                device_id=here.near(0, 1),
                device_id_type=MESH,
            )
            pl.when(own if less else jnp.logical_not(own))(getattr(group, act))

    def last_copy(stage, sent, taken, lead, slot):
        return pltpu.make_async_remote_copy(
            src_ref=sent,
            dst_ref=taken.at[slot],
            send_sem=p3_send.at[stage],
            recv_sem=p3_recv.at[stage],
            device_id=here.lead_device(lead),
            device_id_type=MESH,
        )

    def send_last(stage, sent, taken, last, last_taken):
        @pl.when(gathers)
        def _():
            plane_group(stage, sent, taken, here.far == 0, "wait_recv")
            total = taken[0].astype(F32)
            for j in range(1, half):
                total += taken[j].astype(F32)
            last[...] = total
            for j in range(1, n_lead):
                last_copy(stage, last, last_taken, (here.lead + j) % n_lead, here.far).start()
            last_taken[here.far] = total

    def last_group(stage, last_taken, count):
        every = last_taken.at[pl.ds(0, count)]
        return pltpu.make_async_remote_copy(
            src_ref=every,
            dst_ref=every,
            send_sem=p3_send.at[stage],
            recv_sem=p3_recv.at[stage],
            device_id=here.near(0, 1),
            device_id_type=MESH,
        )

    def out_copy(stage, last_taken, out):
        return pltpu.make_async_copy(last_taken.at[2], out, load_sem.at[8 + stage])

    def final_sum(stage, last_taken, out):
        pl.when(gathers)(last_group(stage, last_taken, 1).wait_recv)
        pl.when(jnp.logical_not(gathers))(last_group(stage, last_taken, 2).wait_recv)
        last_taken[2] = (last_taken[0] + last_taken[1]) * norm
        out_copy(stage, last_taken, out).start()

    def tile(field):
        return field[pl.ds(1, rows)].reshape(cells, field.shape[-1])

    weight_grad(1, act_t, act_mate, tile(x2), da2_mate, s1b, q1b)

    ready("w_two")
    halo_2.wait_recv()
    halo_2.spread(x2, x22)
    total = jnp.zeros((cells, w_two.shape[1]), F32)
    for k, (u, v) in enumerate(OFFSETS):
        total += matmul(window(x2, x22, -u, -v, rows), w_two[k], NT)
    da_first = total.reshape(slope_one.shape) * slope_one[...]
    x1[pl.ds(1, rows)] = da_first.astype(BF)
    halo_1.start_rows()
    halo_1.take_edges()
    halo_1.start_columns()
    mates[2].start()
    weight_grad(0, input_t, input_mate, tile(x1), da1_mate, s1a, q1a)

    send_planes(1, plane_sum(1, s1b, q1b), s2b, q2b)

    ready("w_one")
    halo_1.wait_recv()
    halo_1.spread(x1, x12)
    total = jnp.zeros((cells, w_one.shape[1]), F32)
    for k, (u, v) in enumerate(OFFSETS):
        total += matmul(window(x1, x12, -u, -v, rows), w_one[k], NT)
    grad_stage[...] = total.astype(BF).reshape(grad_stage.shape)
    for row in range(rows):
        load("out", grad_stage.at[row], grad_out.at[:, row])

    send_planes(0, plane_sum(0, s1a, q1a), s2a, q2a)
    send_last(1, s2b, q2b, s3b, q3b)
    send_last(0, s2a, q2a, s3a, q3a)
    ready("out")
    for halo in (halo_h, halo_p, halo_e, halo_2, halo_1):
        halo.wait_send()
    for copy in mates:
        copy.wait_send()
    lead_group.wait_send()
    share_group(1, s1b, q1b).wait_send()
    share_group(0, s1a, q1a).wait_send()
    plane_group(1, s2b, q2b, own_share, "wait_send")
    plane_group(0, s2a, q2a, own_share, "wait_send")
    final_sum(1, q3b, second_out)
    final_sum(0, q3a, first_out)
    @pl.when(gathers)
    def _():
        last_group(1, q3b, n_lead - 1).wait_send()
        last_group(0, q3a, n_lead - 1).wait_send()

    out_copy(1, q3b, second_out).wait()
    out_copy(0, q3a, first_out).wait()


def per_device(head_grads, head_weights, encoder_input, pre_first, pre_second, w_first, w_second):
    heads, batch_all, rows, cols, head_width = head_grads.shape
    samples, _, _, in_width = encoder_input.shape
    width = head_weights.shape[2]
    taps = len(OFFSETS)
    n_lead, n_lat, n_lon = lax.axis_size("lead"), lax.axis_size("lat"), lax.axis_size("lon")
    half = n_lat // 4
    seats = 4 * n_lon
    lanes = heads * head_width
    cells = samples * rows * cols
    cells_total = cells * n_lead * n_lat * n_lon
    rows_two, rows_one = taps * width, taps * in_width
    last_two, last_one = rows_two // (n_lat * n_lon), rows_one // (n_lat * n_lon)

    def field(batch, lane):
        full = (rows + 2, batch, cols, lane)
        units = rows * batch // UNIT
        return (
            pltpu.VMEM(full, BF),
            pltpu.VMEM((2,) + full, BF),
            pltpu.VMEM((2, units, UNIT, lane), F32),
            pltpu.VMEM((2, units + 2, UNIT, lane), F32),
        )

    def reduce_buffers(share):
        return (
            pltpu.VMEM((seats, share * half // 2, width), BF),
            pltpu.VMEM((seats, share * half // 2, width), BF),
            pltpu.VMEM((half // 2, share, width), BF),
            pltpu.VMEM((half, share, width), BF),
            pltpu.VMEM((share, width), F32),
            pltpu.VMEM((3, share, width), F32),
        )

    own = (rows, samples, cols, width)
    act_field = field(samples, width)
    scratch = [
        *field(batch_all, lanes),
        pltpu.VMEM((taps, width, lanes), BF),
        act_field[0], *act_field,
        *field(samples, in_width),
        *field(samples, width),
        *field(samples, width),
        pltpu.VMEM(own, BF),
        pltpu.VMEM(own, F32),
        pltpu.VMEM(own, F32),
        pltpu.VMEM(w_first.shape, BF),
        pltpu.VMEM(w_second.shape, BF),
        pltpu.VMEM((n_lead,) + own, BF),
        pltpu.VMEM((n_lead,) + own, BF),
        pltpu.VMEM((rows_two, cells), BF),
        pltpu.VMEM((rows_one, cells), BF),
        pltpu.VMEM((2, rows_two // 4, cells), BF),
        pltpu.VMEM((2, rows_one // 4, cells), BF),
        pltpu.VMEM(own, BF),
        pltpu.VMEM(own, BF),
        *reduce_buffers(last_two),
        *reduce_buffers(last_one),
        pltpu.VMEM((rows, samples, cols, in_width), BF),
        pltpu.SemaphoreType.DMA((10,)),
        pltpu.SemaphoreType.DMA((5, 5)),
        pltpu.SemaphoreType.DMA((5, 5)),
        pltpu.SemaphoreType.DMA((1,)),
        pltpu.SemaphoreType.DMA((1,)),
        pltpu.SemaphoreType.DMA((4,)),
        pltpu.SemaphoreType.DMA((4,)),
        *[pltpu.SemaphoreType.DMA((2,)) for _ in range(6)],
    ]
    anywhere = pl.BlockSpec(memory_space=pl.ANY)
    input_grad, grad_first, grad_second = pl.pallas_call(
        functools.partial(kernel, 1.0 / math.sqrt(cells_total)),
        out_shape=(
            jax.ShapeDtypeStruct(encoder_input.shape, BF),
            jax.ShapeDtypeStruct((last_one, width), F32),
            jax.ShapeDtypeStruct((last_two, width), F32),
        ),
        in_specs=[anywhere] * 7,
        out_specs=[anywhere] * 3,
        scratch_shapes=scratch,
        compiler_params=pltpu.CompilerParams(
            collective_id=0, has_side_effects=True, vmem_limit_bytes=56 * 2**20
        ),
    )(head_grads, head_weights, encoder_input, pre_first, pre_second, w_first, w_second)
    return input_grad, grad_first.reshape(-1), grad_second.reshape(-1)


def solution(mesh):
    tile = P("lead", "lat", "lon", None)
    in_specs = (P("lead", None, "lat", "lon", None), P("lead", None, None, None), tile, tile, tile, P(), P())
    out_specs = (tile, P(("lat", "lon")), P(("lat", "lon")))
    return jax.shard_map(
        per_device, mesh=mesh, in_specs=in_specs, out_specs=out_specs, check_vma=False
    )
```

```python
import functools
import math

import jax
import jax.numpy as jnp
from jax import lax
from jax.experimental import pallas as pl
from jax.experimental.pallas import tpu as pltpu
from jax.sharding import PartitionSpec as P

OFFSETS = [(-1, -1), (-1, 0), (-1, 1), (0, -1), (0, 0), (0, 1), (1, -1), (1, 0), (1, 1)]
MESH = pl.DeviceIdType.MESH
BF = jnp.bfloat16
F32 = jnp.float32
NT = (((1,), (1,)), ((), ()))
NN = (((1,), (0,)), ((), ()))
UNIT = 8


def gelu_value(values):
    return 0.5 * values * (1.0 + lax.erf(values * 0.7071067811865476))


def gelu_slope(values):
    return (
        0.5 * (1.0 + lax.erf(values * 0.7071067811865476))
        + values * jnp.exp(-0.5 * values * values) * 0.3989422804014327
    )


def matmul(a, b, dims):
    return lax.dot_general(a, b, dims, preferred_element_type=F32)


class Place:
    def __init__(self):
        self.lead = lax.axis_index("lead")
        self.lat = lax.axis_index("lat")
        self.lon = lax.axis_index("lon")
        self.n_lead = lax.axis_size("lead")
        self.n_lat = lax.axis_size("lat")
        self.n_lon = lax.axis_size("lon")
        self.planes = self.n_lat // 2
        self.side = self.lat // self.planes
        self.z = self.lat % self.planes
        self.far = self.lead // 2
        self.core = self.lead % 2
        self.seats = 4 * self.n_lon
        self.seat = self.seat_of(self.side, self.lon, self.far)
        self.has_low = self.lat > 0
        self.has_high = self.lat < self.n_lat - 1

    def seat_of(self, side, lon, far):
        return (side * self.n_lon + lon) * 2 + far

    def seat_device(self, seat):
        far, lon, side = seat % 2, seat // 2 % self.n_lon, seat // (2 * self.n_lon)
        return (2 * far + self.core, side * self.planes + self.z, lon)

    def lead_device(self, lead):
        return (lead, self.lat, self.lon)

    def plane_device(self, z):
        return (self.lead, self.side * self.planes + z, self.lon)

    def near(self, rows, cols):
        return (self.lead, self.lat + rows, (self.lon + cols + self.n_lon) % self.n_lon)


class Halo:
    def __init__(self, here, rows_out, rows_in, field, edge, ring, send, recv):
        self.here, self.field, self.edge, self.ring = here, field, edge, ring
        self.units = edge.shape[1]
        self.rows = field.shape[0] - 2
        self.batch = field.shape[1]
        self.cols = field.shape[2]
        copies = []
        for high in (0, 1):
            step = 1 if high == 0 else -1
            sends = here.has_high if high == 0 else here.has_low
            for source, target in zip(rows_out[high], rows_in[high]):
                copies.append((sends, source, target, here.near(step, 0), 1 + high))
        self.row_count = len(copies)
        body = pl.ds(1, self.units)
        for right in (0, 1):
            step = 1 if right == 0 else -1
            copies.append((None, edge.at[1 - right], ring.at[right, body], here.near(0, step), 0))
        for high in (0, 1):
            for right in (0, 1):
                row_step = 1 if high == 0 else -1
                col_step = 1 if right == 0 else -1
                sends = here.has_high if high == 0 else here.has_low
                source = edge.at[1 - right, self.units - 1 if high == 0 else 0]
                target = ring.at[right, 0 if high == 0 else self.units + 1]
                copies.append((sends, source, target, here.near(row_step, col_step), 3 + high))

        def remote(source, target, device, number):
            return pltpu.make_async_remote_copy(
                src_ref=source,
                dst_ref=target,
                send_sem=send.at[number],
                recv_sem=recv.at[number],
                device_id=device,
                device_id_type=MESH,
            )

        self.copies = [
            (sends, remote(source, target, device, number))
            for sends, source, target, device, number in copies
        ]
        far_rows = (0, self.rows + 1)
        far_units = (0, self.units + 1)
        self.columns = remote(edge, ring.at[:, body], here.near(0, 1), 0)
        self.row_groups = [
            remote(field.at[far_rows[high]], field.at[far_rows[high]], here.near(0, 1), 1 + high)
            for high in (0, 1)
        ]
        self.corner_groups = [
            remote(edge.at[:, 0], ring.at[:, far_units[high]], here.near(0, 1), 3 + high)
            for high in (0, 1)
        ]

    def start(self, items):
        for sends, copy in items:
            if sends is None:
                copy.start()
            else:
                pl.when(sends)(copy.start)

    def start_rows(self):
        self.start(self.copies[: self.row_count])

    def start_columns(self):
        self.start(self.copies[self.row_count :])

    def wait_columns(self):
        self.columns.wait_recv()

    def wait_side(self, high):
        takes = self.here.has_high if high else self.here.has_low

        @pl.when(takes)
        def _():
            self.row_groups[high].wait_recv()
            self.corner_groups[high].wait_recv()

    def wait_recv(self):
        self.wait_columns()
        self.wait_side(0)
        self.wait_side(1)

    def wait_send(self):
        self.columns.wait_send()
        for high in (0, 1):
            sends = self.here.has_low if high else self.here.has_high

            @pl.when(sends)
            def _(high=high):
                self.row_groups[high].wait_send()
                self.corner_groups[high].wait_send()

    def clear(self):
        def low():
            self.field[0] = jnp.zeros(self.field.shape[1:], self.field.dtype)
            for side in (0, 1):
                self.ring[side, 0] = jnp.zeros(self.ring.shape[2:], F32)

        def high():
            self.field[self.rows + 1] = jnp.zeros(self.field.shape[1:], self.field.dtype)
            for side in (0, 1):
                self.ring[side, self.units + 1] = jnp.zeros(self.ring.shape[2:], F32)

        pl.when(jnp.logical_not(self.here.has_low))(low)
        pl.when(jnp.logical_not(self.here.has_high))(high)

    def place(self, row, b):
        flat = row * self.batch + b
        return flat // UNIT, flat % UNIT

    def take_edges(self):
        for row in range(self.rows):
            for b in range(self.batch):
                unit, sub = self.place(row, b)
                block = self.field[1 + row, b].astype(F32)
                self.edge[0, unit, sub : sub + 1] = block[0:1]
                self.edge[1, unit, sub : sub + 1] = block[self.cols - 1 : self.cols]

    def ring_row(self, side, ext, b):
        if ext == 0:
            unit, sub = self.place(self.rows - 1, b)
            unit = 0
        elif ext == self.rows + 1:
            unit, sub = self.place(0, b)
            unit = self.units + 1
        else:
            unit, sub = self.place(ext - 1, b)
            unit = unit + 1
        return self.ring[side, unit, sub : sub + 1]

    def spread(self, base, out, rows=None):
        for ext in range(self.rows + 2) if rows is None else rows:
            for b in range(self.batch):
                block = base[ext, b].astype(F32)
                column = lax.broadcasted_iota(jnp.int32, block.shape, 0)
                behind = jnp.where(
                    column == 0, self.ring_row(0, ext, b), pltpu.roll(block, 1, 0)
                )
                ahead = jnp.where(
                    column == self.cols - 1,
                    self.ring_row(1, ext, b),
                    pltpu.roll(block, self.cols - 1, 0),
                )
                out[0, ext, b] = behind.astype(BF)
                out[1, ext, b] = ahead.astype(BF)


def window(base, spread, step_row, step_col, rows, batch=None, first=0):
    row = pl.ds(1 + first + step_row, rows)
    if step_col == 0:
        view = base[row] if batch is None else base[row, batch]
    else:
        side = 0 if step_col < 0 else 1
        view = spread[side, row] if batch is None else spread[side, row, batch]
    return view.reshape(-1, view.shape[-1])


def kernel(
    norm,
    heads_hbm, head_w_hbm, input_hbm, first_hbm, second_hbm, w_first_hbm, w_second_hbm,
    grad_out, first_out, second_out,
    xh, xh2, eh, rh, head_w,
    xp, xa, xa2, ep, rp,
    xe, xe2, ee, re,
    x2, x22, e2, r2,
    x1, x12, e1, r1,
    pre_two, slope_two, slope_one, w_one, w_two,
    part, parts_in,
    act_t, input_t, act_mate, input_mate, da2_mate, da1_mate,
    s1b, q1b, s2b, q2b, s3b, q3b, s1a, q1a, s2a, q2a, s3a, q3a,
    grad_stage,
    load_sem, halo_send, halo_recv, lead_send, lead_recv, mate_send, mate_recv,
    p1_send, p1_recv, p2_send, p2_recv, p3_send, p3_recv,
):
    here = Place()
    n_lead, planes, n_lon, seats = here.n_lead, here.planes, here.n_lon, here.seats
    half = planes // 2
    heads, batch_all, rows, cols, head_width = heads_hbm.shape
    samples = input_hbm.shape[0]
    cells = samples * rows * cols

    barrier = pltpu.get_barrier_semaphore()

    def greet(device):
        pl.semaphore_signal(barrier, inc=1, device_id=device, device_id_type=MESH)

    for has, step in ((here.has_low, -1), (here.has_high, 1)):

        def greet_rows(step=step):
            for col in (-1, 0, 1):
                greet(here.near(step, col))

        pl.when(has)(greet_rows)

    for col in (-1, 1):
        greet(here.near(0, col))
    for j in range(1, n_lead):
        greet(here.lead_device((here.lead + j) % n_lead))

    @pl.loop(1, seats)
    def _(j):
        greet(here.seat_device((here.seat + j) % seats))

    gathers = here.z // half == here.core
    first_source = (here.z + here.far) % 2
    first_target = here.core * half + first_source

    @pl.when(gathers)
    def _():
        @pl.loop(0, half)
        def _(j):
            z = 2 * j + first_source

            @pl.when(z != here.z)
            def _():
                greet(here.plane_device(z))

    own_share = jnp.logical_and(gathers, here.far == 0)
    greetings = (
        2 + (n_lead - 1) + (seats - 1) + half // 2
        + jnp.where(here.has_low, 3, 0)
        + jnp.where(here.has_high, 3, 0)
        - jnp.where(own_share, 1, 0)
    )

    names = ("heads", "first", "input", "head_w", "second", "w_two", "w_one", "out")
    body = pl.ds(1, rows)
    whole = {
        "heads": xh.at[body], "first": xp.at[body], "input": xe.at[body], "head_w": head_w,
        "second": pre_two, "w_two": w_two, "w_one": w_one, "out": grad_stage,
    }

    def load(key, source, target):
        pltpu.make_async_copy(source, target, load_sem.at[names.index(key)]).start()

    for row in range(rows):
        for h in range(heads):
            lanes = pl.ds(h * head_width, head_width)
            load("heads", heads_hbm.at[h, :, row], xh.at[1 + row, :, :, lanes])
    for row in range(rows):
        load("first", first_hbm.at[:, row], xp.at[1 + row])
        load("input", input_hbm.at[:, row], xe.at[1 + row])
    for h in range(heads):
        load("head_w", head_w_hbm.at[h], head_w.at[:, :, pl.ds(h * head_width, head_width)])
    for row in range(rows):
        load("second", second_hbm.at[:, row], pre_two.at[row])
    load("w_two", w_second_hbm, w_two)
    load("w_one", w_first_hbm, w_one)

    def ready(key):
        pltpu.make_async_copy(whole[key], whole[key], load_sem.at[names.index(key)]).wait()

    lane = [pl.ds(h * head_width, head_width) for h in range(heads)]
    halo_h = Halo(
        here,
        [[heads_hbm.at[h, :, rows - 1] for h in range(heads)], [heads_hbm.at[h, :, 0] for h in range(heads)]],
        [[xh.at[0, :, :, lane[h]] for h in range(heads)], [xh.at[rows + 1, :, :, lane[h]] for h in range(heads)]],
        xh, eh, rh, halo_send.at[0], halo_recv.at[0],
    )
    halo_p = Halo(
        here,
        [[first_hbm.at[:, rows - 1]], [first_hbm.at[:, 0]]],
        [[xp.at[0]], [xp.at[rows + 1]]],
        xp, ep, rp, halo_send.at[1], halo_recv.at[1],
    )
    halo_e = Halo(
        here,
        [[input_hbm.at[:, rows - 1]], [input_hbm.at[:, 0]]],
        [[xe.at[0]], [xe.at[rows + 1]]],
        xe, ee, re, halo_send.at[2], halo_recv.at[2],
    )
    halo_2 = Halo(
        here, [[x2.at[rows]], [x2.at[1]]], [[x2.at[0]], [x2.at[rows + 1]]],
        x2, e2, r2, halo_send.at[3], halo_recv.at[3],
    )
    halo_1 = Halo(
        here, [[x1.at[rows]], [x1.at[1]]], [[x1.at[0]], [x1.at[rows + 1]]],
        x1, e1, r1, halo_send.at[4], halo_recv.at[4],
    )

    halo_h.clear()
    halo_p.clear()
    halo_e.clear()
    halo_2.clear()
    halo_1.clear()
    pl.semaphore_wait(barrier, greetings)
    halo_h.start_rows()
    ready("heads")
    halo_h.take_edges()
    halo_h.start_columns()
    ready("first")
    halo_p.take_edges()
    halo_p.start_rows()
    halo_p.start_columns()
    ready("input")
    halo_e.take_edges()
    halo_e.start_rows()
    halo_e.start_columns()
    ready("head_w")

    pieces = (pl.ds(1, rows - 2), pl.ds(0, 1), pl.ds(rows - 1, 1))

    others = pl.ds(0, n_lead - 1)
    lead_group = pltpu.make_async_remote_copy(
        src_ref=part.at[others],
        dst_ref=parts_in.at[others],
        send_sem=lead_send.at[0],
        recv_sem=lead_recv.at[0],
        device_id=here.near(0, 1),
        device_id_type=MESH,
    )

    def lead_copy(source, owner, piece):
        return pltpu.make_async_remote_copy(
            src_ref=part.at[owner, pieces[piece]],
            dst_ref=parts_in.at[source, pieces[piece]],
            send_sem=lead_send.at[0],
            recv_sem=lead_recv.at[0],
            device_id=here.lead_device(owner),
            device_id_type=MESH,
        )

    def convolve(first, count, batch):
        total = None
        for k, (u, v) in enumerate(OFFSETS):
            term = matmul(window(xh, xh2, -u, -v, count, batch, first), head_w[k], NT)
            total = term if total is None else total + term
        return total.astype(BF)

    halo_h.wait_columns()
    halo_h.spread(xh, xh2, range(1, rows + 1))
    @pl.loop(0, 2)
    def _(j):
        far = (here.far + 1 + j) % 2
        block = convolve(1, rows - 2, pl.ds(far * 2 * samples, 2 * samples))
        block = block.reshape((rows - 2, 2 * samples) + part.shape[3:])
        for core in (0, 1):
            owner = 2 * far + core
            part[owner, pieces[0]] = block[:, core * samples : (core + 1) * samples]
            copy = lead_copy(here.lead, owner, 0)
            pl.when(owner != here.lead)(copy.start)

    for high in (0, 1):
        halo_h.wait_side(high)
        halo_h.spread(xh, xh2, [(rows + 1) * high])
        block = convolve((rows - 1) * high, 1, pl.ds(0, batch_all)).reshape((batch_all,) + part.shape[3:])
        for owner in range(n_lead):
            part[owner, (rows - 1) * high] = block[owner * samples : (owner + 1) * samples]
        for j in (2, 3, 1):
            lead_copy(here.lead, (here.lead + j) % n_lead, 1 + high).start()

    ready("second")
    for row in range(rows):
        slope_two[row] = gelu_slope(pre_two[row].astype(F32))
        slope_one[row] = gelu_slope(xp[1 + row].astype(F32))
    halo_p.wait_recv()
    for row in range(rows + 2):
        xa[row] = gelu_value(xp[row].astype(F32)).astype(BF)
    for side in (0, 1):
        for unit in range(rp.shape[1]):
            rp[side, unit] = gelu_value(rp[side, unit])
    halo_p.spread(xa, xa2)
    halo_e.wait_recv()
    halo_e.spread(xe, xe2)
    for k, (u, v) in enumerate(OFFSETS):
        block = window(xa, xa2, u, v, rows)
        act_t[pl.ds(k * block.shape[1], block.shape[1])] = block.T
        block = window(xe, xe2, u, v, rows)
        input_t[pl.ds(k * block.shape[1], block.shape[1])] = block.T

    mate = here.lead + 1 - 2 * here.core

    def mate_copy(number, source, target):
        return pltpu.make_async_remote_copy(
            src_ref=source,
            dst_ref=target,
            send_sem=mate_send.at[number],
            recv_sem=mate_recv.at[number],
            device_id=here.lead_device(mate),
            device_id_type=MESH,
        )

    def turned_rows(turned, side, core):
        block = turned.shape[0] // 4
        return pl.ds(pl.multiple_of((2 * side + core) * block, block), block)

    for stage, turned, taken in ((1, act_t, act_mate), (0, input_t, input_mate)):
        for side in (0, 1):
            rows_there = turned_rows(turned, side, 1 - here.core)
            mate_copy(stage, turned.at[rows_there], taken.at[side]).start()
    mates = [
        mate_copy(0, input_mate, input_mate),
        mate_copy(1, act_mate, act_mate),
        mate_copy(2, x1.at[body], da1_mate),
        mate_copy(3, x2.at[body], da2_mate),
    ]

    lead_group.wait_recv()
    parts_in[here.lead] = part[here.lead]
    for row in range(rows):
        total = parts_in[0, row].astype(F32)
        for a in range(1, n_lead):
            total += parts_in[a, row].astype(F32)
        x2[1 + row] = (total * slope_two[row]).astype(BF)
    halo_2.start_rows()
    halo_2.take_edges()
    halo_2.start_columns()
    mates[3].start()

    def share_copy(stage, sent, taken, send_seat, recv_seat, device=None):
        return pltpu.make_async_remote_copy(
            src_ref=sent.at[send_seat],
            dst_ref=taken.at[recv_seat],
            send_sem=p1_send.at[stage],
            recv_sem=p1_recv.at[stage],
            device_id=here.seat_device(send_seat) if device is None else device,
            device_id_type=MESH,
        )

    def share_group(stage, sent, taken):
        every = pl.ds(0, seats - 1)
        return share_copy(stage, sent, taken, every, every, here.near(0, 1))

    def weight_grad(stage, turned, turned_mate, da, da_mate, sent, taken):
        share = sent.shape[1] * 2 // half

        @pl.loop(0, 2)
        def _(j):
            side = (here.side + 1 + j) % 2
            product = matmul(turned[turned_rows(turned, side, here.core)], da, NN)

            @pl.when(j == 0)
            def _():
                mates[stage].wait_recv()
                mates[2 + stage].wait_recv()

            product += matmul(turned_mate[side], da_mate[...].reshape(da.shape), NN)
            for lon in range(n_lon):
                for odd in (0, 1):
                    far = (odd + here.z) % 2
                    seat = here.seat_of(side, lon, far)
                    for t in range(half // 2):
                        begin = ((2 * t + odd) * n_lon + lon) * share
                        piece = product[begin : begin + share].astype(BF)
                        sent[seat, t * share : (t + 1) * share] = piece

            @pl.loop(0, 2 * n_lon)
            def _(i):
                seat = 2 * n_lon * side + (here.seat + 2 + i) % (2 * n_lon)

                @pl.when(seat != here.seat)
                def _():
                    share_copy(stage, sent, taken, seat, here.seat).start()

    def plane_sum(stage, sent, taken):
        taken[here.seat] = sent[here.seat]

        share_group(stage, sent, taken).wait_recv()
        total = taken[0].astype(F32)
        for seat in range(1, seats):
            total += taken[seat].astype(F32)
        return total

    def plane_copy(stage, sent, taken, t, slot, z):
        return pltpu.make_async_remote_copy(
            src_ref=sent.at[t],
            dst_ref=taken.at[slot],
            send_sem=p2_send.at[stage],
            recv_sem=p2_recv.at[stage],
            device_id=here.plane_device(z),
            device_id_type=MESH,
        )

    def send_planes(stage, total, sent, taken):
        share = sent.shape[1]
        for t in range(half // 2):
            sent[t] = total[t * share : (t + 1) * share].astype(BF)
        for t in range(half // 2):
            z = first_target + 2 * t
            copy = plane_copy(stage, sent, taken, t, here.z // 2, z)
            pl.when(z != here.z)(copy.start)

        @pl.when(own_share)
        def _():
            taken[here.z // 2] = sent[here.z % half // 2]

    def plane_group(stage, sent, taken, own, act):
        count = half // 2 if act == "wait_send" else half
        for less in (0, 1):
            every = pl.ds(0, count - less)
            ref = sent.at[every] if act == "wait_send" else taken.at[every]
            group = pltpu.make_async_remote_copy(
                src_ref=ref,
                dst_ref=ref,
                send_sem=p2_send.at[stage],
                recv_sem=p2_recv.at[stage],
                device_id=here.near(0, 1),
                device_id_type=MESH,
            )
            pl.when(own if less else jnp.logical_not(own))(getattr(group, act))

    def last_copy(stage, sent, taken, lead, slot):
        return pltpu.make_async_remote_copy(
            src_ref=sent,
            dst_ref=taken.at[slot],
            send_sem=p3_send.at[stage],
            recv_sem=p3_recv.at[stage],
            device_id=here.lead_device(lead),
            device_id_type=MESH,
        )

    def send_last(stage, sent, taken, last, last_taken):
        @pl.when(gathers)
        def _():
            plane_group(stage, sent, taken, here.far == 0, "wait_recv")
            total = taken[0].astype(F32)
            for j in range(1, half):
                total += taken[j].astype(F32)
            last[...] = total
            for j in range(1, n_lead):
                last_copy(stage, last, last_taken, (here.lead + j) % n_lead, here.far).start()
            last_taken[here.far] = total

    def last_group(stage, last_taken, count):
        every = last_taken.at[pl.ds(0, count)]
        return pltpu.make_async_remote_copy(
            src_ref=every,
            dst_ref=every,
            send_sem=p3_send.at[stage],
            recv_sem=p3_recv.at[stage],
            device_id=here.near(0, 1),
            device_id_type=MESH,
        )

    def final_sum(stage, last_taken, out):
        pl.when(gathers)(last_group(stage, last_taken, 1).wait_recv)
        pl.when(jnp.logical_not(gathers))(last_group(stage, last_taken, 2).wait_recv)
        out[...] = (last_taken[0] + last_taken[1]) * norm

    def tile(field):
        return field[pl.ds(1, rows)].reshape(cells, field.shape[-1])

    weight_grad(1, act_t, act_mate, tile(x2), da2_mate, s1b, q1b)

    ready("w_two")
    halo_2.wait_recv()
    halo_2.spread(x2, x22)
    total = jnp.zeros((cells, w_two.shape[1]), F32)
    for k, (u, v) in enumerate(OFFSETS):
        total += matmul(window(x2, x22, -u, -v, rows), w_two[k], NT)
    da_first = total.reshape(slope_one.shape) * slope_one[...]
    x1[pl.ds(1, rows)] = da_first.astype(BF)
    halo_1.start_rows()
    halo_1.take_edges()
    halo_1.start_columns()
    mates[2].start()
    weight_grad(0, input_t, input_mate, tile(x1), da1_mate, s1a, q1a)

    send_planes(1, plane_sum(1, s1b, q1b), s2b, q2b)

    ready("w_one")
    halo_1.wait_recv()
    halo_1.spread(x1, x12)
    total = jnp.zeros((cells, w_one.shape[1]), F32)
    for k, (u, v) in enumerate(OFFSETS):
        total += matmul(window(x1, x12, -u, -v, rows), w_one[k], NT)
    grad_stage[...] = total.astype(BF).reshape(grad_stage.shape)
    for row in range(rows):
        load("out", grad_stage.at[row], grad_out.at[:, row])

    send_planes(0, plane_sum(0, s1a, q1a), s2a, q2a)
    send_last(1, s2b, q2b, s3b, q3b)
    send_last(0, s2a, q2a, s3a, q3a)
    ready("out")
    for halo in (halo_h, halo_p, halo_e, halo_2, halo_1):
        halo.wait_send()
    for copy in mates:
        copy.wait_send()
    lead_group.wait_send()
    share_group(1, s1b, q1b).wait_send()
    share_group(0, s1a, q1a).wait_send()
    plane_group(1, s2b, q2b, own_share, "wait_send")
    plane_group(0, s2a, q2a, own_share, "wait_send")
    final_sum(1, q3b, second_out)
    final_sum(0, q3a, first_out)
    @pl.when(gathers)
    def _():
        last_group(1, q3b, n_lead - 1).wait_send()
        last_group(0, q3a, n_lead - 1).wait_send()


def per_device(head_grads, head_weights, encoder_input, pre_first, pre_second, w_first, w_second):
    heads, batch_all, rows, cols, head_width = head_grads.shape
    samples, _, _, in_width = encoder_input.shape
    width = head_weights.shape[2]
    taps = len(OFFSETS)
    n_lead, n_lat, n_lon = lax.axis_size("lead"), lax.axis_size("lat"), lax.axis_size("lon")
    half = n_lat // 4
    seats = 4 * n_lon
    lanes = heads * head_width
    cells = samples * rows * cols
    cells_total = cells * n_lead * n_lat * n_lon
    rows_two, rows_one = taps * width, taps * in_width
    last_two, last_one = rows_two // (n_lat * n_lon), rows_one // (n_lat * n_lon)

    def field(batch, lane):
        full = (rows + 2, batch, cols, lane)
        units = rows * batch // UNIT
        return (
            pltpu.VMEM(full, BF),
            pltpu.VMEM((2,) + full, BF),
            pltpu.VMEM((2, units, UNIT, lane), F32),
            pltpu.VMEM((2, units + 2, UNIT, lane), F32),
        )

    def reduce_buffers(share):
        return (
            pltpu.VMEM((seats, share * half // 2, width), BF),
            pltpu.VMEM((seats, share * half // 2, width), BF),
            pltpu.VMEM((half // 2, share, width), BF),
            pltpu.VMEM((half, share, width), BF),
            pltpu.VMEM((share, width), F32),
            pltpu.VMEM((3, share, width), F32),
        )

    own = (rows, samples, cols, width)
    act_field = field(samples, width)
    scratch = [
        *field(batch_all, lanes),
        pltpu.VMEM((taps, width, lanes), BF),
        act_field[0], *act_field,
        *field(samples, in_width),
        *field(samples, width),
        *field(samples, width),
        pltpu.VMEM(own, BF),
        pltpu.VMEM(own, F32),
        pltpu.VMEM(own, F32),
        pltpu.VMEM(w_first.shape, BF),
        pltpu.VMEM(w_second.shape, BF),
        pltpu.VMEM((n_lead,) + own, BF),
        pltpu.VMEM((n_lead,) + own, BF),
        pltpu.VMEM((rows_two, cells), BF),
        pltpu.VMEM((rows_one, cells), BF),
        pltpu.VMEM((2, rows_two // 4, cells), BF),
        pltpu.VMEM((2, rows_one // 4, cells), BF),
        pltpu.VMEM(own, BF),
        pltpu.VMEM(own, BF),
        *reduce_buffers(last_two),
        *reduce_buffers(last_one),
        pltpu.VMEM((rows, samples, cols, in_width), BF),
        pltpu.SemaphoreType.DMA((8,)),
        pltpu.SemaphoreType.DMA((5, 5)),
        pltpu.SemaphoreType.DMA((5, 5)),
        pltpu.SemaphoreType.DMA((1,)),
        pltpu.SemaphoreType.DMA((1,)),
        pltpu.SemaphoreType.DMA((4,)),
        pltpu.SemaphoreType.DMA((4,)),
        *[pltpu.SemaphoreType.DMA((2,)) for _ in range(6)],
    ]
    anywhere = pl.BlockSpec(memory_space=pl.ANY)
    input_grad, grad_first, grad_second = pl.pallas_call(
        functools.partial(kernel, 1.0 / math.sqrt(cells_total)),
        out_shape=(
            jax.ShapeDtypeStruct(encoder_input.shape, BF),
            jax.ShapeDtypeStruct((last_one, width), F32),
            jax.ShapeDtypeStruct((last_two, width), F32),
        ),
        in_specs=[anywhere] * 7,
        out_specs=[anywhere] + [pl.BlockSpec(memory_space=pltpu.VMEM)] * 2,
        scratch_shapes=scratch,
        compiler_params=pltpu.CompilerParams(
            collective_id=0, has_side_effects=True, vmem_limit_bytes=55091 * 1024
        ),
    )(head_grads, head_weights, encoder_input, pre_first, pre_second, w_first, w_second)
    return input_grad, grad_first.reshape(-1), grad_second.reshape(-1)


def solution(mesh):
    tile = P("lead", "lat", "lon", None)
    in_specs = (P("lead", None, "lat", "lon", None), P("lead", None, None, None), tile, tile, tile, P(), P())
    out_specs = (tile, P(("lat", "lon")), P(("lat", "lon")))
    return jax.shard_map(
        per_device, mesh=mesh, in_specs=in_specs, out_specs=out_specs, check_vma=False
    )
```

```python
import functools
import math

import jax
import jax.numpy as jnp
from jax import lax
from jax.experimental import pallas as pl
from jax.experimental.pallas import tpu as pltpu
from jax.sharding import PartitionSpec as P

OFFSETS = [(-1, -1), (-1, 0), (-1, 1), (0, -1), (0, 0), (0, 1), (1, -1), (1, 0), (1, 1)]
MESH = pl.DeviceIdType.MESH
BF = jnp.bfloat16
F32 = jnp.float32
NT = (((1,), (1,)), ((), ()))
NN = (((1,), (0,)), ((), ()))
UNIT = 8


def gelu_value(values):
    return 0.5 * values * (1.0 + lax.erf(values * 0.7071067811865476))


def gelu_slope(values):
    return (
        0.5 * (1.0 + lax.erf(values * 0.7071067811865476))
        + values * jnp.exp(-0.5 * values * values) * 0.3989422804014327
    )


def matmul(a, b, dims):
    return lax.dot_general(a, b, dims, preferred_element_type=F32)


class Place:
    def __init__(self):
        self.lead = lax.axis_index("lead")
        self.lat = lax.axis_index("lat")
        self.lon = lax.axis_index("lon")
        self.n_lead = lax.axis_size("lead")
        self.n_lat = lax.axis_size("lat")
        self.n_lon = lax.axis_size("lon")
        self.planes = self.n_lat // 2
        self.side = self.lat // self.planes
        self.z = self.lat % self.planes
        self.far = self.lead // 2
        self.core = self.lead % 2
        self.seats = 4 * self.n_lon
        self.seat = self.seat_of(self.side, self.lon, self.far)
        self.has_low = self.lat > 0
        self.has_high = self.lat < self.n_lat - 1

    def seat_of(self, side, lon, far):
        return (side * self.n_lon + lon) * 2 + far

    def seat_device(self, seat):
        far, lon, side = seat % 2, seat // 2 % self.n_lon, seat // (2 * self.n_lon)
        return (2 * far + self.core, side * self.planes + self.z, lon)

    def lead_device(self, lead):
        return (lead, self.lat, self.lon)

    def plane_device(self, z):
        return (self.lead, self.side * self.planes + z, self.lon)

    def near(self, rows, cols):
        return (self.lead, self.lat + rows, (self.lon + cols + self.n_lon) % self.n_lon)


class Halo:
    def __init__(self, here, rows_out, rows_in, field, edge, ring, send, recv):
        self.here, self.field, self.edge, self.ring = here, field, edge, ring
        self.units = edge.shape[1]
        self.rows = field.shape[0] - 2
        self.batch = field.shape[1]
        self.cols = field.shape[2]
        copies = []
        for high in (0, 1):
            step = 1 if high == 0 else -1
            sends = here.has_high if high == 0 else here.has_low
            for source, target in zip(rows_out[high], rows_in[high]):
                copies.append((sends, source, target, here.near(step, 0), 1 + high))
        self.row_count = len(copies)
        body = pl.ds(1, self.units)
        for right in (0, 1):
            step = 1 if right == 0 else -1
            copies.append((None, edge.at[1 - right], ring.at[right, body], here.near(0, step), 0))
        for high in (0, 1):
            for right in (0, 1):
                row_step = 1 if high == 0 else -1
                col_step = 1 if right == 0 else -1
                sends = here.has_high if high == 0 else here.has_low
                source = edge.at[1 - right, self.units - 1 if high == 0 else 0]
                target = ring.at[right, 0 if high == 0 else self.units + 1]
                copies.append((sends, source, target, here.near(row_step, col_step), 3 + high))

        def remote(source, target, device, number):
            return pltpu.make_async_remote_copy(
                src_ref=source,
                dst_ref=target,
                send_sem=send.at[number],
                recv_sem=recv.at[number],
                device_id=device,
                device_id_type=MESH,
            )

        self.copies = [
            (sends, remote(source, target, device, number))
            for sends, source, target, device, number in copies
        ]
        far_rows = (0, self.rows + 1)
        far_units = (0, self.units + 1)
        self.columns = remote(edge, ring.at[:, body], here.near(0, 1), 0)
        self.row_groups = [
            remote(field.at[far_rows[high]], field.at[far_rows[high]], here.near(0, 1), 1 + high)
            for high in (0, 1)
        ]
        self.corner_groups = [
            remote(edge.at[:, 0], ring.at[:, far_units[high]], here.near(0, 1), 3 + high)
            for high in (0, 1)
        ]

    def start(self, items):
        for sends, copy in items:
            if sends is None:
                copy.start()
            else:
                pl.when(sends)(copy.start)

    def start_rows(self):
        self.start(self.copies[: self.row_count])

    def start_columns(self):
        self.start(self.copies[self.row_count :])

    def wait_columns(self):
        self.columns.wait_recv()

    def wait_side(self, high):
        takes = self.here.has_high if high else self.here.has_low

        @pl.when(takes)
        def _():
            self.row_groups[high].wait_recv()
            self.corner_groups[high].wait_recv()

    def wait_recv(self):
        self.wait_columns()
        self.wait_side(0)
        self.wait_side(1)

    def wait_send(self):
        self.columns.wait_send()
        for high in (0, 1):
            sends = self.here.has_low if high else self.here.has_high

            @pl.when(sends)
            def _(high=high):
                self.row_groups[high].wait_send()
                self.corner_groups[high].wait_send()

    def clear(self):
        def low():
            self.field[0] = jnp.zeros(self.field.shape[1:], self.field.dtype)
            for side in (0, 1):
                self.ring[side, 0] = jnp.zeros(self.ring.shape[2:], F32)

        def high():
            self.field[self.rows + 1] = jnp.zeros(self.field.shape[1:], self.field.dtype)
            for side in (0, 1):
                self.ring[side, self.units + 1] = jnp.zeros(self.ring.shape[2:], F32)

        pl.when(jnp.logical_not(self.here.has_low))(low)
        pl.when(jnp.logical_not(self.here.has_high))(high)

    def place(self, row, b):
        flat = row * self.batch + b
        return flat // UNIT, flat % UNIT

    def take_edges(self):
        for row in range(self.rows):
            for b in range(self.batch):
                unit, sub = self.place(row, b)
                block = self.field[1 + row, b].astype(F32)
                self.edge[0, unit, sub : sub + 1] = block[0:1]
                self.edge[1, unit, sub : sub + 1] = block[self.cols - 1 : self.cols]

    def ring_row(self, side, ext, b):
        if ext == 0:
            unit, sub = self.place(self.rows - 1, b)
            unit = 0
        elif ext == self.rows + 1:
            unit, sub = self.place(0, b)
            unit = self.units + 1
        else:
            unit, sub = self.place(ext - 1, b)
            unit = unit + 1
        return self.ring[side, unit, sub : sub + 1]

    def spread(self, base, out, rows=None):
        for ext in range(self.rows + 2) if rows is None else rows:
            for b in range(self.batch):
                block = base[ext, b].astype(F32)
                column = lax.broadcasted_iota(jnp.int32, block.shape, 0)
                behind = jnp.where(
                    column == 0, self.ring_row(0, ext, b), pltpu.roll(block, 1, 0)
                )
                ahead = jnp.where(
                    column == self.cols - 1,
                    self.ring_row(1, ext, b),
                    pltpu.roll(block, self.cols - 1, 0),
                )
                out[0, ext, b] = behind.astype(BF)
                out[1, ext, b] = ahead.astype(BF)


def window(base, spread, step_row, step_col, rows, batch=None, first=0):
    row = pl.ds(1 + first + step_row, rows)
    if step_col == 0:
        view = base[row] if batch is None else base[row, batch]
    else:
        side = 0 if step_col < 0 else 1
        view = spread[side, row] if batch is None else spread[side, row, batch]
    return view.reshape(-1, view.shape[-1])


def kernel(
    norm,
    heads_hbm, head_w_hbm, input_hbm, first_hbm, second_hbm, w_first_hbm, w_second_hbm,
    grad_out, first_out, second_out,
    xh, xh2, eh, rh, head_w,
    xp, xa, xa2, ep, rp,
    xe, xe2, ee, re,
    x2, x22, e2, r2,
    x1, x12, e1, r1,
    pre_two, slope_two, slope_one, w_one, w_two,
    part, parts_in,
    act_t, input_t, act_mate, input_mate, da2_mate, da1_mate,
    along_y, from_y, along_x, from_x, then_x, last_x, then_y, last_y, s2b, q2b, s3b, q3b, s1a, q1a, s2a, q2a, s3a, q3a,
    grad_stage,
    load_sem, halo_send, halo_recv, lead_send, lead_recv, mate_send, mate_recv,
    line_send, line_recv, p1_send, p1_recv, p2_send, p2_recv, p3_send, p3_recv, token,
):
    here = Place()
    n_lead, planes, n_lon, seats = here.n_lead, here.planes, here.n_lon, here.seats
    half = planes // 2
    heads, batch_all, rows, cols, head_width = heads_hbm.shape
    samples = input_hbm.shape[0]
    cells = samples * rows * cols

    barrier = pltpu.get_barrier_semaphore()

    def greet(device):
        pl.semaphore_signal(barrier, inc=1, device_id=device, device_id_type=MESH)

    for has, step in ((here.has_low, -1), (here.has_high, 1)):

        def greet_rows(step=step):
            for col in (-1, 0, 1):
                greet(here.near(step, col))

        pl.when(has)(greet_rows)

    for col in (-1, 1, 2):
        greet(here.near(0, col))
    x_here = 2 * here.far + here.side

    def x_device(x):
        return (2 * (x // 2) + here.core, x % 2 * planes + here.z, here.lon)

    def z_device(step):
        return here.plane_device((here.z + step + planes) % planes)

    for step in (1, 3):
        greet(x_device((x_here + step) % 4))
    for step in (-1, 1):
        greet(z_device(step))
    for j in range(1, n_lead):
        greet(here.lead_device((here.lead + j) % n_lead))

    greetings = (
        3 + 2 + 2 + (n_lead - 1)
        + jnp.where(here.has_low, 3, 0)
        + jnp.where(here.has_high, 3, 0)
    )

    def send_token(number, device):
        pl.semaphore_signal(token.at[number], inc=1, device_id=device, device_id_type=MESH)

    def send_plane_tokens():
        for number, step in enumerate((-1, 1, 2)):
            send_token(number, here.near(0, step))

    def send_z_tokens(level):
        for number, step in enumerate((-1, 1)):
            send_token(3 + 2 * level + number, z_device(step * 2**level))

    def wait_tokens(*numbers):
        for number in numbers:
            pl.semaphore_wait(token.at[number], 1)

    gathers = here.z // half == here.core
    first_source = (here.z + here.far) % 2
    first_target = here.core * half + first_source
    own_share = jnp.logical_and(gathers, here.far == 0)

    names = ("heads", "first", "input", "head_w", "second", "w_two", "w_one", "out")
    body = pl.ds(1, rows)
    whole = {
        "heads": xh.at[body], "first": xp.at[body], "input": xe.at[body], "head_w": head_w,
        "second": pre_two, "w_two": w_two, "w_one": w_one, "out": grad_stage,
    }

    def load(key, source, target):
        pltpu.make_async_copy(source, target, load_sem.at[names.index(key)]).start()

    for row in range(rows):
        for h in range(heads):
            lanes = pl.ds(h * head_width, head_width)
            load("heads", heads_hbm.at[h, :, row], xh.at[1 + row, :, :, lanes])
    for row in range(rows):
        load("first", first_hbm.at[:, row], xp.at[1 + row])
        load("input", input_hbm.at[:, row], xe.at[1 + row])
    for h in range(heads):
        load("head_w", head_w_hbm.at[h], head_w.at[:, :, pl.ds(h * head_width, head_width)])
    for row in range(rows):
        load("second", second_hbm.at[:, row], pre_two.at[row])
    load("w_two", w_second_hbm, w_two)
    load("w_one", w_first_hbm, w_one)

    def ready(key):
        pltpu.make_async_copy(whole[key], whole[key], load_sem.at[names.index(key)]).wait()

    lane = [pl.ds(h * head_width, head_width) for h in range(heads)]
    halo_h = Halo(
        here,
        [[heads_hbm.at[h, :, rows - 1] for h in range(heads)], [heads_hbm.at[h, :, 0] for h in range(heads)]],
        [[xh.at[0, :, :, lane[h]] for h in range(heads)], [xh.at[rows + 1, :, :, lane[h]] for h in range(heads)]],
        xh, eh, rh, halo_send.at[0], halo_recv.at[0],
    )
    halo_p = Halo(
        here,
        [[first_hbm.at[:, rows - 1]], [first_hbm.at[:, 0]]],
        [[xp.at[0]], [xp.at[rows + 1]]],
        xp, ep, rp, halo_send.at[1], halo_recv.at[1],
    )
    halo_e = Halo(
        here,
        [[input_hbm.at[:, rows - 1]], [input_hbm.at[:, 0]]],
        [[xe.at[0]], [xe.at[rows + 1]]],
        xe, ee, re, halo_send.at[2], halo_recv.at[2],
    )
    halo_2 = Halo(
        here, [[x2.at[rows]], [x2.at[1]]], [[x2.at[0]], [x2.at[rows + 1]]],
        x2, e2, r2, halo_send.at[3], halo_recv.at[3],
    )
    halo_1 = Halo(
        here, [[x1.at[rows]], [x1.at[1]]], [[x1.at[0]], [x1.at[rows + 1]]],
        x1, e1, r1, halo_send.at[4], halo_recv.at[4],
    )

    halo_h.clear()
    halo_p.clear()
    halo_e.clear()
    halo_2.clear()
    halo_1.clear()
    pl.semaphore_wait(barrier, greetings)
    halo_h.start_rows()
    send_plane_tokens()
    send_z_tokens(0)
    ready("heads")
    halo_h.take_edges()
    halo_h.start_columns()
    ready("first")
    halo_p.take_edges()
    halo_p.start_rows()
    halo_p.start_columns()
    ready("input")
    halo_e.take_edges()
    halo_e.start_rows()
    halo_e.start_columns()
    ready("head_w")

    pieces = (pl.ds(1, rows - 2), pl.ds(0, 1), pl.ds(rows - 1, 1))

    others = pl.ds(0, n_lead - 1)
    lead_group = pltpu.make_async_remote_copy(
        src_ref=part.at[others],
        dst_ref=parts_in.at[others],
        send_sem=lead_send.at[0],
        recv_sem=lead_recv.at[0],
        device_id=here.near(0, 1),
        device_id_type=MESH,
    )

    def lead_copy(source, owner, piece):
        return pltpu.make_async_remote_copy(
            src_ref=part.at[owner, pieces[piece]],
            dst_ref=parts_in.at[source, pieces[piece]],
            send_sem=lead_send.at[0],
            recv_sem=lead_recv.at[0],
            device_id=here.lead_device(owner),
            device_id_type=MESH,
        )

    def convolve(first, count, batch):
        total = None
        for k, (u, v) in enumerate(OFFSETS):
            term = matmul(window(xh, xh2, -u, -v, count, batch, first), head_w[k], NT)
            total = term if total is None else total + term
        return total.astype(BF)

    halo_h.wait_columns()
    halo_h.spread(xh, xh2, range(1, rows + 1))
    @pl.loop(0, 2)
    def _(j):
        far = (here.far + 1 + j) % 2
        block = convolve(1, rows - 2, pl.ds(far * 2 * samples, 2 * samples))
        block = block.reshape((rows - 2, 2 * samples) + part.shape[3:])
        for core in (0, 1):
            owner = 2 * far + core
            part[owner, pieces[0]] = block[:, core * samples : (core + 1) * samples]
            copy = lead_copy(here.lead, owner, 0)
            pl.when(owner != here.lead)(copy.start)

    for high in (0, 1):
        halo_h.wait_side(high)
        halo_h.spread(xh, xh2, [(rows + 1) * high])
        block = convolve((rows - 1) * high, 1, pl.ds(0, batch_all)).reshape((batch_all,) + part.shape[3:])
        for owner in range(n_lead):
            part[owner, (rows - 1) * high] = block[owner * samples : (owner + 1) * samples]
        for j in (2, 3, 1):
            lead_copy(here.lead, (here.lead + j) % n_lead, 1 + high).start()

    wait_tokens(3, 4)
    send_z_tokens(1)

    ready("second")
    for row in range(rows):
        slope_two[row] = gelu_slope(pre_two[row].astype(F32))
        slope_one[row] = gelu_slope(xp[1 + row].astype(F32))
    halo_p.wait_recv()
    for row in range(rows + 2):
        xa[row] = gelu_value(xp[row].astype(F32)).astype(BF)
    for side in (0, 1):
        for unit in range(rp.shape[1]):
            rp[side, unit] = gelu_value(rp[side, unit])
    halo_p.spread(xa, xa2)
    halo_e.wait_recv()
    halo_e.spread(xe, xe2)
    for k, (u, v) in enumerate(OFFSETS):
        block = window(xa, xa2, u, v, rows)
        act_t[pl.ds(k * block.shape[1], block.shape[1])] = block.T
        block = window(xe, xe2, u, v, rows)
        input_t[pl.ds(k * block.shape[1], block.shape[1])] = block.T

    mate = here.lead + 1 - 2 * here.core

    def mate_copy(number, source, target):
        return pltpu.make_async_remote_copy(
            src_ref=source,
            dst_ref=target,
            send_sem=mate_send.at[number],
            recv_sem=mate_recv.at[number],
            device_id=here.lead_device(mate),
            device_id_type=MESH,
        )

    def turned_rows(turned, side, core):
        block = turned.shape[0] // 4
        return pl.ds(pl.multiple_of((2 * side + core) * block, block), block)

    for stage, turned, taken in ((1, act_t, act_mate), (0, input_t, input_mate)):
        for side in (0, 1):
            rows_there = turned_rows(turned, side, 1 - here.core)
            mate_copy(stage, turned.at[rows_there], taken.at[side]).start()
    mates = [
        mate_copy(0, input_mate, input_mate),
        mate_copy(1, act_mate, act_mate),
        mate_copy(2, x1.at[body], da1_mate),
        mate_copy(3, x2.at[body], da2_mate),
    ]

    lead_group.wait_recv()
    parts_in[here.lead] = part[here.lead]
    for row in range(rows):
        total = parts_in[0, row].astype(F32)
        for a in range(1, n_lead):
            total += parts_in[a, row].astype(F32)
        x2[1 + row] = (total * slope_two[row]).astype(BF)
    halo_2.start_rows()
    halo_2.take_edges()
    halo_2.start_columns()
    mates[3].start()
    wait_tokens(5, 6)
    send_z_tokens(2)
    wait_tokens(0, 1, 2)

    def weight_grad(stage, turned, turned_mate, da, da_mate, share, put, send):
        @pl.loop(0, 2)
        def _(j):
            side = (here.side + 1 + j) % 2
            product = matmul(turned[turned_rows(turned, side, here.core)], da, NN)

            @pl.when(j == 0)
            def _():
                mates[stage].wait_recv()
                mates[2 + stage].wait_recv()

            product += matmul(turned_mate[side], da_mate[...].reshape(da.shape), NN)
            for lon in range(n_lon):
                for odd in (0, 1):
                    far = (odd + here.z) % 2
                    for t in range(half // 2):
                        begin = ((2 * t + odd) * n_lon + lon) * share
                        put(side, lon, far, t, product[begin : begin + share].astype(BF))
            send(side)

    quarter = half // 4

    def lon_device(lon):
        return (here.lead, here.lat, lon)

    def line_copy(number, source, target, device):
        return pltpu.make_async_remote_copy(
            src_ref=source,
            dst_ref=target,
            send_sem=line_send.at[number],
            recv_sem=line_recv.at[number],
            device_id=device,
            device_id_type=MESH,
        )

    lines = (
        (along_y, from_y, here.lon, n_lon, lon_device),
        (along_x, from_x, x_here, 4, x_device),
        (then_x, last_x, x_here, 4, x_device),
        (then_y, last_y, here.lon, n_lon, lon_device),
    )

    def line_send_to(number, there):
        sent, taken, own, _, device = lines[number]
        line_copy(number, sent.at[there], taken.at[own], device(there)).start()

    def line_send_all(number):
        _, _, own, count, _ = lines[number]
        for j in range(1, count):
            line_send_to(number, (own + j) % count)

    def line_group(number):
        sent, taken, _, count, _ = lines[number]
        others = pl.ds(0, count - 1)
        return line_copy(number, sent.at[others], taken.at[others], here.near(0, 1))

    def line_take(number):
        sent, taken, own, _, _ = lines[number]
        line_group(number).wait_recv()
        taken[own] = sent[own]

    def put_second(side, lon, far, t, piece):
        x = 2 * far + side
        begin = t % quarter * piece.shape[0]
        rows_there = slice(begin, begin + piece.shape[0])
        if t < quarter:
            along_y[lon, x, rows_there] = piece
        else:
            along_x[x, lon, rows_there] = piece

    def send_second(side):
        for far in (0, 1):
            x = 2 * far + side
            pl.when(x != x_here)(functools.partial(line_send_to, 1, x))

    def pass_second():
        for number in (0, 1):
            line_take(number)
            _, taken, _, count, _ = lines[number]
            sent = lines[2 + number][0]
            for there in range(sent.shape[0]):
                total = taken[0, there].astype(F32)
                for source in range(1, count):
                    total += taken[source, there].astype(F32)
                sent[there] = total.astype(BF)
            line_send_all(2 + number)

    def second_sums(share):
        pieces = []
        for number in (2, 3):
            line_take(number)
            _, taken, _, count, _ = lines[number]
            total = taken[0].astype(F32)
            for source in range(1, count):
                total += taken[source].astype(F32)
            pieces += [total[t * share : (t + 1) * share] for t in range(quarter)]
        return pieces

    def share_copy(stage, sent, taken, send_seat, recv_seat, device=None):
        return pltpu.make_async_remote_copy(
            src_ref=sent.at[send_seat],
            dst_ref=taken.at[recv_seat],
            send_sem=p1_send.at[stage],
            recv_sem=p1_recv.at[stage],
            device_id=here.seat_device(send_seat) if device is None else device,
            device_id_type=MESH,
        )

    def share_group(stage, sent, taken):
        every = pl.ds(0, seats - 1)
        return share_copy(stage, sent, taken, every, every, here.near(0, 1))

    def put_first(side, lon, far, t, piece):
        begin = t * piece.shape[0]
        s1a[here.seat_of(side, lon, far), begin : begin + piece.shape[0]] = piece

    def send_first(side):
        @pl.loop(0, 2 * n_lon)
        def _(i):
            seat = 2 * n_lon * side + (here.seat + 2 + i) % (2 * n_lon)

            @pl.when(seat != here.seat)
            def _():
                share_copy(0, s1a, q1a, seat, here.seat).start()

    def plane_sum(stage, sent, taken, share):
        taken[here.seat] = sent[here.seat]

        share_group(stage, sent, taken).wait_recv()
        total = taken[0].astype(F32)
        for seat in range(1, seats):
            total += taken[seat].astype(F32)
        return [total[t * share : (t + 1) * share] for t in range(half // 2)]

    def plane_copy(stage, sent, taken, t, slot, z):
        return pltpu.make_async_remote_copy(
            src_ref=sent.at[t],
            dst_ref=taken.at[slot],
            send_sem=p2_send.at[stage],
            recv_sem=p2_recv.at[stage],
            device_id=here.plane_device(z),
            device_id_type=MESH,
        )

    def send_planes(stage, pieces, sent, taken):
        for t in range(half // 2):
            sent[t] = pieces[t].astype(BF)
        for t in range(half // 2):
            z = first_target + 2 * t
            copy = plane_copy(stage, sent, taken, t, here.z // 2, z)
            pl.when(z != here.z)(copy.start)

        @pl.when(own_share)
        def _():
            taken[here.z // 2] = sent[here.z % half // 2]

    def plane_group(stage, sent, taken, own, act):
        count = half // 2 if act == "wait_send" else half
        for less in (0, 1):
            every = pl.ds(0, count - less)
            ref = sent.at[every] if act == "wait_send" else taken.at[every]
            group = pltpu.make_async_remote_copy(
                src_ref=ref,
                dst_ref=ref,
                send_sem=p2_send.at[stage],
                recv_sem=p2_recv.at[stage],
                device_id=here.near(0, 1),
                device_id_type=MESH,
            )
            pl.when(own if less else jnp.logical_not(own))(getattr(group, act))

    def last_copy(stage, sent, taken, lead, slot):
        return pltpu.make_async_remote_copy(
            src_ref=sent,
            dst_ref=taken.at[slot],
            send_sem=p3_send.at[stage],
            recv_sem=p3_recv.at[stage],
            device_id=here.lead_device(lead),
            device_id_type=MESH,
        )

    def send_last(stage, sent, taken, last, last_taken):
        @pl.when(gathers)
        def _():
            plane_group(stage, sent, taken, here.far == 0, "wait_recv")
            total = taken[0].astype(F32)
            for j in range(1, half):
                total += taken[j].astype(F32)
            last[...] = total
            for j in range(1, n_lead):
                last_copy(stage, last, last_taken, (here.lead + j) % n_lead, here.far).start()
            last_taken[here.far] = total

    def last_group(stage, last_taken, count):
        every = last_taken.at[pl.ds(0, count)]
        return pltpu.make_async_remote_copy(
            src_ref=every,
            dst_ref=every,
            send_sem=p3_send.at[stage],
            recv_sem=p3_recv.at[stage],
            device_id=here.near(0, 1),
            device_id_type=MESH,
        )

    def final_sum(stage, last_taken, out):
        pl.when(gathers)(last_group(stage, last_taken, 1).wait_recv)
        pl.when(jnp.logical_not(gathers))(last_group(stage, last_taken, 2).wait_recv)
        out[...] = (last_taken[0] + last_taken[1]) * norm

    def tile(field):
        return field[pl.ds(1, rows)].reshape(cells, field.shape[-1])

    weight_grad(1, act_t, act_mate, tile(x2), da2_mate, s3b.shape[0], put_second, send_second)
    line_send_all(0)

    ready("w_two")
    halo_2.wait_recv()
    halo_2.spread(x2, x22)
    total = jnp.zeros((cells, w_two.shape[1]), F32)
    for k, (u, v) in enumerate(OFFSETS):
        total += matmul(window(x2, x22, -u, -v, rows), w_two[k], NT)
    da_first = total.reshape(slope_one.shape) * slope_one[...]
    x1[pl.ds(1, rows)] = da_first.astype(BF)
    halo_1.start_rows()
    halo_1.take_edges()
    halo_1.start_columns()
    mates[2].start()
    weight_grad(0, input_t, input_mate, tile(x1), da1_mate, s3a.shape[0], put_first, send_first)
    pass_second()

    ready("w_one")
    halo_1.wait_recv()
    halo_1.spread(x1, x12)
    total = jnp.zeros((cells, w_one.shape[1]), F32)
    for k, (u, v) in enumerate(OFFSETS):
        total += matmul(window(x1, x12, -u, -v, rows), w_one[k], NT)
    grad_stage[...] = total.astype(BF).reshape(grad_stage.shape)
    for row in range(rows):
        load("out", grad_stage.at[row], grad_out.at[:, row])

    wait_tokens(7, 8)
    send_planes(1, second_sums(s3b.shape[0]), s2b, q2b)
    send_planes(0, plane_sum(0, s1a, q1a, s3a.shape[0]), s2a, q2a)
    send_last(1, s2b, q2b, s3b, q3b)
    send_last(0, s2a, q2a, s3a, q3a)
    ready("out")
    for halo in (halo_h, halo_p, halo_e, halo_2, halo_1):
        halo.wait_send()
    for copy in mates:
        copy.wait_send()
    lead_group.wait_send()
    for number in range(4):
        line_group(number).wait_send()
    share_group(0, s1a, q1a).wait_send()
    plane_group(1, s2b, q2b, own_share, "wait_send")
    plane_group(0, s2a, q2a, own_share, "wait_send")
    final_sum(1, q3b, second_out)
    final_sum(0, q3a, first_out)
    @pl.when(gathers)
    def _():
        last_group(1, q3b, n_lead - 1).wait_send()
        last_group(0, q3a, n_lead - 1).wait_send()


def per_device(head_grads, head_weights, encoder_input, pre_first, pre_second, w_first, w_second):
    heads, batch_all, rows, cols, head_width = head_grads.shape
    samples, _, _, in_width = encoder_input.shape
    width = head_weights.shape[2]
    taps = len(OFFSETS)
    n_lead, n_lat, n_lon = lax.axis_size("lead"), lax.axis_size("lat"), lax.axis_size("lon")
    half = n_lat // 4
    seats = 4 * n_lon
    lanes = heads * head_width
    cells = samples * rows * cols
    cells_total = cells * n_lead * n_lat * n_lon
    rows_two, rows_one = taps * width, taps * in_width
    last_two, last_one = rows_two // (n_lat * n_lon), rows_one // (n_lat * n_lon)

    def field(batch, lane):
        full = (rows + 2, batch, cols, lane)
        units = rows * batch // UNIT
        return (
            pltpu.VMEM(full, BF),
            pltpu.VMEM((2,) + full, BF),
            pltpu.VMEM((2, units, UNIT, lane), F32),
            pltpu.VMEM((2, units + 2, UNIT, lane), F32),
        )

    def reduce_buffers(share):
        return (
            pltpu.VMEM((half // 2, share, width), BF),
            pltpu.VMEM((half, share, width), BF),
            pltpu.VMEM((share, width), F32),
            pltpu.VMEM((3, share, width), F32),
        )

    def line_buffers(first, then):
        return [pltpu.VMEM((first, then, last_two * half // 4, width), BF)] * 2

    own = (rows, samples, cols, width)
    act_field = field(samples, width)
    scratch = [
        *field(batch_all, lanes),
        pltpu.VMEM((taps, width, lanes), BF),
        act_field[0], *act_field,
        *field(samples, in_width),
        *field(samples, width),
        *field(samples, width),
        pltpu.VMEM(own, BF),
        pltpu.VMEM(own, F32),
        pltpu.VMEM(own, F32),
        pltpu.VMEM(w_first.shape, BF),
        pltpu.VMEM(w_second.shape, BF),
        pltpu.VMEM((n_lead,) + own, BF),
        pltpu.VMEM((n_lead,) + own, BF),
        pltpu.VMEM((rows_two, cells), BF),
        pltpu.VMEM((rows_one, cells), BF),
        pltpu.VMEM((2, rows_two // 4, cells), BF),
        pltpu.VMEM((2, rows_one // 4, cells), BF),
        pltpu.VMEM(own, BF),
        pltpu.VMEM(own, BF),
        *line_buffers(n_lon, 4),
        *line_buffers(4, n_lon),
        *[pltpu.VMEM((4, last_two * half // 4, width), BF)] * 2,
        *[pltpu.VMEM((n_lon, last_two * half // 4, width), BF)] * 2,
        *reduce_buffers(last_two),
        *[pltpu.VMEM((seats, last_one * half // 2, width), BF)] * 2,
        *reduce_buffers(last_one),
        pltpu.VMEM((rows, samples, cols, in_width), BF),
        pltpu.SemaphoreType.DMA((8,)),
        pltpu.SemaphoreType.DMA((5, 5)),
        pltpu.SemaphoreType.DMA((5, 5)),
        pltpu.SemaphoreType.DMA((1,)),
        pltpu.SemaphoreType.DMA((1,)),
        pltpu.SemaphoreType.DMA((4,)),
        pltpu.SemaphoreType.DMA((4,)),
        pltpu.SemaphoreType.DMA((4,)),
        pltpu.SemaphoreType.DMA((4,)),
        *[pltpu.SemaphoreType.DMA((2,)) for _ in range(6)],
        pltpu.SemaphoreType.REGULAR((9,)),
    ]
    anywhere = pl.BlockSpec(memory_space=pl.ANY)
    input_grad, grad_first, grad_second = pl.pallas_call(
        functools.partial(kernel, 1.0 / math.sqrt(cells_total)),
        out_shape=(
            jax.ShapeDtypeStruct(encoder_input.shape, BF),
            jax.ShapeDtypeStruct((last_one, width), F32),
            jax.ShapeDtypeStruct((last_two, width), F32),
        ),
        in_specs=[anywhere] * 7,
        out_specs=[anywhere] + [pl.BlockSpec(memory_space=pltpu.VMEM)] * 2,
        scratch_shapes=scratch,
        compiler_params=pltpu.CompilerParams(
            collective_id=0, has_side_effects=True, vmem_limit_bytes=55091 * 1024
        ),
    )(head_grads, head_weights, encoder_input, pre_first, pre_second, w_first, w_second)
    return input_grad, grad_first.reshape(-1), grad_second.reshape(-1)


def solution(mesh):
    tile = P("lead", "lat", "lon", None)
    in_specs = (P("lead", None, "lat", "lon", None), P("lead", None, None, None), tile, tile, tile, P(), P())
    out_specs = (tile, P(("lat", "lon")), P(("lat", "lon")))
    return jax.shard_map(
        per_device, mesh=mesh, in_specs=in_specs, out_specs=out_specs, check_vma=False
    )
```

```python
import functools
import math

import jax
import jax.numpy as jnp
from jax import lax
from jax.experimental import pallas as pl
from jax.experimental.pallas import tpu as pltpu
from jax.sharding import PartitionSpec as P

OFFSETS = [(-1, -1), (-1, 0), (-1, 1), (0, -1), (0, 0), (0, 1), (1, -1), (1, 0), (1, 1)]
MESH = pl.DeviceIdType.MESH
BF = jnp.bfloat16
F32 = jnp.float32
NT = (((1,), (1,)), ((), ()))
NN = (((1,), (0,)), ((), ()))
UNIT = 8


def gelu_value(values):
    return 0.5 * values * (1.0 + lax.erf(values * 0.7071067811865476))


def gelu_slope(values):
    return (
        0.5 * (1.0 + lax.erf(values * 0.7071067811865476))
        + values * jnp.exp(-0.5 * values * values) * 0.3989422804014327
    )


def matmul(a, b, dims):
    return lax.dot_general(a, b, dims, preferred_element_type=F32)


class Place:
    def __init__(self):
        self.lead = lax.axis_index("lead")
        self.lat = lax.axis_index("lat")
        self.lon = lax.axis_index("lon")
        self.n_lead = lax.axis_size("lead")
        self.n_lat = lax.axis_size("lat")
        self.n_lon = lax.axis_size("lon")
        self.planes = self.n_lat // 2
        self.side = self.lat // self.planes
        self.z = self.lat % self.planes
        self.far = self.lead // 2
        self.core = self.lead % 2
        self.seats = 4 * self.n_lon
        self.seat = self.seat_of(self.side, self.lon, self.far)
        self.has_low = self.lat > 0
        self.has_high = self.lat < self.n_lat - 1

    def seat_of(self, side, lon, far):
        return (side * self.n_lon + lon) * 2 + far

    def seat_device(self, seat):
        far, lon, side = seat % 2, seat // 2 % self.n_lon, seat // (2 * self.n_lon)
        return (2 * far + self.core, side * self.planes + self.z, lon)

    def lead_device(self, lead):
        return (lead, self.lat, self.lon)

    def plane_device(self, z):
        return (self.lead, self.side * self.planes + z, self.lon)

    def near(self, rows, cols):
        return (self.lead, self.lat + rows, (self.lon + cols + self.n_lon) % self.n_lon)


class Halo:
    def __init__(self, here, rows_out, rows_in, field, edge, ring, send, recv):
        self.here, self.field, self.edge, self.ring = here, field, edge, ring
        self.units = edge.shape[1]
        self.rows = field.shape[0] - 2
        self.batch = field.shape[1]
        self.cols = field.shape[2]
        copies = []
        for high in (0, 1):
            step = 1 if high == 0 else -1
            sends = here.has_high if high == 0 else here.has_low
            for source, target in zip(rows_out[high], rows_in[high]):
                copies.append((sends, source, target, here.near(step, 0), 1 + high))
        self.row_count = len(copies)
        body = pl.ds(1, self.units)
        for right in (0, 1):
            step = 1 if right == 0 else -1
            copies.append((None, edge.at[1 - right], ring.at[right, body], here.near(0, step), 0))
        for high in (0, 1):
            for right in (0, 1):
                row_step = 1 if high == 0 else -1
                col_step = 1 if right == 0 else -1
                sends = here.has_high if high == 0 else here.has_low
                source = edge.at[1 - right, self.units - 1 if high == 0 else 0]
                target = ring.at[right, 0 if high == 0 else self.units + 1]
                copies.append((sends, source, target, here.near(row_step, col_step), 3 + high))

        def remote(source, target, device, number):
            return pltpu.make_async_remote_copy(
                src_ref=source,
                dst_ref=target,
                send_sem=send.at[number],
                recv_sem=recv.at[number],
                device_id=device,
                device_id_type=MESH,
            )

        self.copies = [
            (sends, remote(source, target, device, number))
            for sends, source, target, device, number in copies
        ]
        far_rows = (0, self.rows + 1)
        far_units = (0, self.units + 1)
        self.columns = remote(edge, ring.at[:, body], here.near(0, 1), 0)
        self.row_groups = [
            remote(field.at[far_rows[high]], field.at[far_rows[high]], here.near(0, 1), 1 + high)
            for high in (0, 1)
        ]
        self.corner_groups = [
            remote(edge.at[:, 0], ring.at[:, far_units[high]], here.near(0, 1), 3 + high)
            for high in (0, 1)
        ]

    def start(self, items):
        for sends, copy in items:
            if sends is None:
                copy.start()
            else:
                pl.when(sends)(copy.start)

    def start_rows(self):
        self.start(self.copies[: self.row_count])

    def start_columns(self):
        self.start(self.copies[self.row_count :])

    def wait_columns(self):
        self.columns.wait_recv()

    def wait_side(self, high):
        takes = self.here.has_high if high else self.here.has_low

        @pl.when(takes)
        def _():
            self.row_groups[high].wait_recv()
            self.corner_groups[high].wait_recv()

    def wait_recv(self):
        self.wait_columns()
        self.wait_side(0)
        self.wait_side(1)

    def wait_send(self):
        self.columns.wait_send()
        for high in (0, 1):
            sends = self.here.has_low if high else self.here.has_high

            @pl.when(sends)
            def _(high=high):
                self.row_groups[high].wait_send()
                self.corner_groups[high].wait_send()

    def clear(self):
        def low():
            self.field[0] = jnp.zeros(self.field.shape[1:], self.field.dtype)
            for side in (0, 1):
                self.ring[side, 0] = jnp.zeros(self.ring.shape[2:], F32)

        def high():
            self.field[self.rows + 1] = jnp.zeros(self.field.shape[1:], self.field.dtype)
            for side in (0, 1):
                self.ring[side, self.units + 1] = jnp.zeros(self.ring.shape[2:], F32)

        pl.when(jnp.logical_not(self.here.has_low))(low)
        pl.when(jnp.logical_not(self.here.has_high))(high)

    def place(self, row, b):
        flat = row * self.batch + b
        return flat // UNIT, flat % UNIT

    def take_edges(self):
        for row in range(self.rows):
            for b in range(self.batch):
                unit, sub = self.place(row, b)
                block = self.field[1 + row, b].astype(F32)
                self.edge[0, unit, sub : sub + 1] = block[0:1]
                self.edge[1, unit, sub : sub + 1] = block[self.cols - 1 : self.cols]

    def ring_row(self, side, ext, b):
        if ext == 0:
            unit, sub = self.place(self.rows - 1, b)
            unit = 0
        elif ext == self.rows + 1:
            unit, sub = self.place(0, b)
            unit = self.units + 1
        else:
            unit, sub = self.place(ext - 1, b)
            unit = unit + 1
        return self.ring[side, unit, sub : sub + 1]

    def spread(self, base, out, rows=None):
        for ext in range(self.rows + 2) if rows is None else rows:
            for b in range(self.batch):
                block = base[ext, b].astype(F32)
                column = lax.broadcasted_iota(jnp.int32, block.shape, 0)
                behind = jnp.where(
                    column == 0, self.ring_row(0, ext, b), pltpu.roll(block, 1, 0)
                )
                ahead = jnp.where(
                    column == self.cols - 1,
                    self.ring_row(1, ext, b),
                    pltpu.roll(block, self.cols - 1, 0),
                )
                out[0, ext, b] = behind.astype(BF)
                out[1, ext, b] = ahead.astype(BF)


def window(base, spread, step_row, step_col, rows, batch=None, first=0):
    row = pl.ds(1 + first + step_row, rows)
    if step_col == 0:
        view = base[row] if batch is None else base[row, batch]
    else:
        side = 0 if step_col < 0 else 1
        view = spread[side, row] if batch is None else spread[side, row, batch]
    return view.reshape(-1, view.shape[-1])


def kernel(
    norm,
    heads_hbm, head_w_hbm, input_hbm, first_hbm, second_hbm, w_first_hbm, w_second_hbm,
    grad_out, first_out, second_out,
    xh, xh2, eh, rh, head_w,
    xp, xa, xa2, ep, rp,
    xe, xe2, ee, re,
    x2, x22, e2, r2,
    x1, x12, e1, r1,
    pre_two, slope_two, slope_one, w_one, w_two,
    part, parts_in,
    act_t, input_t, act_mate, input_mate, da2_mate, da1_mate,
    along_y, from_y, along_x, from_x, then_x, last_x, then_y, last_y, s2b, q2b, s3b, q3b, s1a, q1a, s2a, q2a, s3a, q3a,
    grad_stage,
    load_sem, halo_send, halo_recv, lead_send, lead_recv, mate_send, mate_recv,
    line_send, line_recv, p1_send, p1_recv, p2_send, p2_recv, p3_send, p3_recv, token,
):
    here = Place()
    n_lead, planes, n_lon, seats = here.n_lead, here.planes, here.n_lon, here.seats
    half = planes // 2
    heads, batch_all, rows, cols, head_width = heads_hbm.shape
    samples = input_hbm.shape[0]
    cells = samples * rows * cols

    barrier = pltpu.get_barrier_semaphore()

    def greet(device):
        pl.semaphore_signal(barrier, inc=1, device_id=device, device_id_type=MESH)

    for has, step in ((here.has_low, -1), (here.has_high, 1)):

        def greet_rows(step=step):
            for col in (-1, 0, 1):
                greet(here.near(step, col))

        pl.when(has)(greet_rows)

    for col in (-1, 1, 2):
        greet(here.near(0, col))
    x_here = 2 * here.far + here.side

    def x_device(x):
        return (2 * (x // 2) + here.core, x % 2 * planes + here.z, here.lon)

    def z_device(step):
        return here.plane_device((here.z + step + planes) % planes)

    for step in (1, 3):
        greet(x_device((x_here + step) % 4))
    for step in (-1, 1):
        greet(z_device(step))
    for j in range(1, n_lead):
        greet(here.lead_device((here.lead + j) % n_lead))

    greetings = (
        3 + 2 + 2 + (n_lead - 1)
        + jnp.where(here.has_low, 3, 0)
        + jnp.where(here.has_high, 3, 0)
    )

    def send_token(number, device):
        pl.semaphore_signal(token.at[number], inc=1, device_id=device, device_id_type=MESH)

    def send_plane_tokens():
        for number, step in enumerate((-1, 1, 2)):
            send_token(number, here.near(0, step))

    def send_z_tokens(level):
        for number, step in enumerate((-1, 1)):
            send_token(3 + 2 * level + number, z_device(step * 2**level))

    def wait_tokens(*numbers):
        for number in numbers:
            pl.semaphore_wait(token.at[number], 1)

    gathers = here.z // half == here.core
    first_source = (here.z + here.far) % 2
    first_target = here.core * half + first_source
    own_share = jnp.logical_and(gathers, here.far == 0)

    names = ("heads", "first", "input", "head_w", "second", "w_two", "w_one", "out")
    body = pl.ds(1, rows)
    whole = {
        "heads": xh.at[body], "first": xp.at[body], "input": xe.at[body], "head_w": head_w,
        "second": pre_two, "w_two": w_two, "w_one": w_one, "out": grad_stage,
    }

    def load(key, source, target):
        pltpu.make_async_copy(source, target, load_sem.at[names.index(key)]).start()

    for row in range(rows):
        for h in range(heads):
            lanes = pl.ds(h * head_width, head_width)
            load("heads", heads_hbm.at[h, :, row], xh.at[1 + row, :, :, lanes])
    for row in range(rows):
        load("first", first_hbm.at[:, row], xp.at[1 + row])
        load("input", input_hbm.at[:, row], xe.at[1 + row])
    for h in range(heads):
        load("head_w", head_w_hbm.at[h], head_w.at[:, :, pl.ds(h * head_width, head_width)])
    for row in range(rows):
        load("second", second_hbm.at[:, row], pre_two.at[row])
    load("w_two", w_second_hbm, w_two)
    load("w_one", w_first_hbm, w_one)

    def ready(key):
        pltpu.make_async_copy(whole[key], whole[key], load_sem.at[names.index(key)]).wait()

    lane = [pl.ds(h * head_width, head_width) for h in range(heads)]
    halo_h = Halo(
        here,
        [[heads_hbm.at[h, :, rows - 1] for h in range(heads)], [heads_hbm.at[h, :, 0] for h in range(heads)]],
        [[xh.at[0, :, :, lane[h]] for h in range(heads)], [xh.at[rows + 1, :, :, lane[h]] for h in range(heads)]],
        xh, eh, rh, halo_send.at[0], halo_recv.at[0],
    )
    halo_p = Halo(
        here,
        [[first_hbm.at[:, rows - 1]], [first_hbm.at[:, 0]]],
        [[xp.at[0]], [xp.at[rows + 1]]],
        xp, ep, rp, halo_send.at[1], halo_recv.at[1],
    )
    halo_e = Halo(
        here,
        [[input_hbm.at[:, rows - 1]], [input_hbm.at[:, 0]]],
        [[xe.at[0]], [xe.at[rows + 1]]],
        xe, ee, re, halo_send.at[2], halo_recv.at[2],
    )
    halo_2 = Halo(
        here, [[x2.at[rows]], [x2.at[1]]], [[x2.at[0]], [x2.at[rows + 1]]],
        x2, e2, r2, halo_send.at[3], halo_recv.at[3],
    )
    halo_1 = Halo(
        here, [[x1.at[rows]], [x1.at[1]]], [[x1.at[0]], [x1.at[rows + 1]]],
        x1, e1, r1, halo_send.at[4], halo_recv.at[4],
    )

    halo_h.clear()
    halo_p.clear()
    halo_e.clear()
    halo_2.clear()
    halo_1.clear()
    pl.semaphore_wait(barrier, greetings)
    halo_h.start_rows()
    send_plane_tokens()
    send_z_tokens(0)
    ready("heads")
    halo_h.take_edges()
    halo_h.start_columns()
    ready("first")
    halo_p.take_edges()
    halo_p.start_rows()
    halo_p.start_columns()
    ready("input")
    halo_e.take_edges()
    halo_e.start_rows()
    halo_e.start_columns()
    ready("head_w")

    pieces = (pl.ds(1, rows - 2), pl.ds(0, 1), pl.ds(rows - 1, 1))

    others = pl.ds(0, n_lead - 1)
    lead_group = pltpu.make_async_remote_copy(
        src_ref=part.at[others],
        dst_ref=parts_in.at[others],
        send_sem=lead_send.at[0],
        recv_sem=lead_recv.at[0],
        device_id=here.near(0, 1),
        device_id_type=MESH,
    )

    def lead_copy(source, owner, piece):
        return pltpu.make_async_remote_copy(
            src_ref=part.at[owner, pieces[piece]],
            dst_ref=parts_in.at[source, pieces[piece]],
            send_sem=lead_send.at[0],
            recv_sem=lead_recv.at[0],
            device_id=here.lead_device(owner),
            device_id_type=MESH,
        )

    def convolve(first, count, batch):
        total = None
        for k, (u, v) in enumerate(OFFSETS):
            term = matmul(window(xh, xh2, -u, -v, count, batch, first), head_w[k], NT)
            total = term if total is None else total + term
        return total.astype(BF)

    halo_h.wait_columns()
    halo_h.spread(xh, xh2, range(1, rows + 1))
    @pl.loop(0, 2)
    def _(j):
        far = (here.far + 1 + j) % 2
        block = convolve(1, rows - 2, pl.ds(far * 2 * samples, 2 * samples))
        block = block.reshape((rows - 2, 2 * samples) + part.shape[3:])
        for core in (0, 1):
            owner = 2 * far + core
            part[owner, pieces[0]] = block[:, core * samples : (core + 1) * samples]
            copy = lead_copy(here.lead, owner, 0)
            pl.when(owner != here.lead)(copy.start)

    for high in (0, 1):
        halo_h.wait_side(high)
        halo_h.spread(xh, xh2, [(rows + 1) * high])
        block = convolve((rows - 1) * high, 1, pl.ds(0, batch_all)).reshape((batch_all,) + part.shape[3:])
        for owner in range(n_lead):
            part[owner, (rows - 1) * high] = block[owner * samples : (owner + 1) * samples]
        for j in (2, 3, 1):
            lead_copy(here.lead, (here.lead + j) % n_lead, 1 + high).start()

    wait_tokens(3, 4)
    send_z_tokens(1)

    ready("second")
    for row in range(rows):
        slope_two[row] = gelu_slope(pre_two[row].astype(F32))
        slope_one[row] = gelu_slope(xp[1 + row].astype(F32))
    halo_p.wait_recv()
    for row in range(rows + 2):
        xa[row] = gelu_value(xp[row].astype(F32)).astype(BF)
    for side in (0, 1):
        for unit in range(rp.shape[1]):
            rp[side, unit] = gelu_value(rp[side, unit])
    halo_p.spread(xa, xa2)
    halo_e.wait_recv()
    halo_e.spread(xe, xe2)
    for k, (u, v) in enumerate(OFFSETS):
        block = window(xa, xa2, u, v, rows)
        act_t[pl.ds(k * block.shape[1], block.shape[1])] = block.T
        block = window(xe, xe2, u, v, rows)
        input_t[pl.ds(k * block.shape[1], block.shape[1])] = block.T

    mate = here.lead + 1 - 2 * here.core
    far_same, far_mate = (here.lead + 2) % n_lead, (mate + 2) % n_lead

    def mate_copy(number, source, target):
        return pltpu.make_async_remote_copy(
            src_ref=source,
            dst_ref=target,
            send_sem=mate_send.at[number],
            recv_sem=mate_recv.at[number],
            device_id=here.lead_device(mate),
            device_id_type=MESH,
        )

    def turned_rows(turned, side, core):
        block = turned.shape[0] // 4
        return pl.ds(pl.multiple_of((2 * side + core) * block, block), block)

    for stage, turned, taken in ((1, act_t, act_mate), (0, input_t, input_mate)):
        for side in (0, 1):
            rows_there = turned_rows(turned, side, 1 - here.core)
            mate_copy(stage, turned.at[rows_there], taken.at[side]).start()
    mates = [
        mate_copy(0, input_mate, input_mate),
        mate_copy(1, act_mate, act_mate),
        mate_copy(2, x1.at[body], da1_mate),
        mate_copy(3, x2.at[body], da2_mate),
    ]

    lead_group.wait_recv()
    parts_in[here.lead] = part[here.lead]
    for row in range(rows):
        total = parts_in[0, row].astype(F32)
        for a in range(1, n_lead):
            total += parts_in[a, row].astype(F32)
        x2[1 + row] = (total * slope_two[row]).astype(BF)
    halo_2.start_rows()
    halo_2.take_edges()
    halo_2.start_columns()
    mates[3].start()
    wait_tokens(5, 6)
    send_z_tokens(2)
    wait_tokens(0, 1, 2)

    def weight_grad(stage, turned, turned_mate, da, da_mate, share, put, send):
        @pl.loop(0, 2)
        def _(j):
            side = (here.side + 1 + j) % 2
            product = matmul(turned[turned_rows(turned, side, here.core)], da, NN)

            @pl.when(j == 0)
            def _():
                mates[stage].wait_recv()
                mates[2 + stage].wait_recv()

            product += matmul(turned_mate[side], da_mate[...].reshape(da.shape), NN)
            for lon in range(n_lon):
                for odd in (0, 1):
                    far = (odd + here.z) % 2
                    for t in range(half // 2):
                        begin = ((2 * t + odd) * n_lon + lon) * share
                        put(side, lon, far, t, product[begin : begin + share].astype(BF))
            send(side)

    quarter = half // 4

    def lon_device(lon):
        return (here.lead, here.lat, lon)

    def line_copy(number, source, target, device):
        return pltpu.make_async_remote_copy(
            src_ref=source,
            dst_ref=target,
            send_sem=line_send.at[number],
            recv_sem=line_recv.at[number],
            device_id=device,
            device_id_type=MESH,
        )

    lines = (
        (along_y, from_y, here.lon, n_lon, lon_device),
        (along_x, from_x, x_here, 4, x_device),
        (then_x, last_x, x_here, 4, x_device),
        (then_y, last_y, here.lon, n_lon, lon_device),
    )

    def line_send_to(number, there):
        sent, taken, own, _, device = lines[number]
        line_copy(number, sent.at[there], taken.at[own], device(there)).start()

    def line_send_all(number):
        _, _, own, count, _ = lines[number]
        for j in range(1, count):
            line_send_to(number, (own + j) % count)

    def line_group(number):
        sent, taken, _, count, _ = lines[number]
        others = pl.ds(0, count - 1)
        return line_copy(number, sent.at[others], taken.at[others], here.near(0, 1))

    def line_take(number):
        sent, taken, own, _, _ = lines[number]
        line_group(number).wait_recv()
        taken[own] = sent[own]

    def put_second(side, lon, far, t, piece):
        x = 2 * far + side
        begin = t % quarter * piece.shape[0]
        rows_there = slice(begin, begin + piece.shape[0])
        if t < quarter:
            along_y[lon, x, rows_there] = piece
        else:
            along_x[x, lon, rows_there] = piece

    def send_second(side):
        for far in (0, 1):
            x = 2 * far + side
            pl.when(x != x_here)(functools.partial(line_send_to, 1, x))

    def pass_second():
        for number in (0, 1):
            line_take(number)
            _, taken, _, count, _ = lines[number]
            sent = lines[2 + number][0]
            for there in range(sent.shape[0]):
                total = taken[0, there].astype(F32)
                for source in range(1, count):
                    total += taken[source, there].astype(F32)
                sent[there] = total.astype(BF)
            line_send_all(2 + number)

    def second_sums(share):
        pieces = []
        for number in (2, 3):
            line_take(number)
            _, taken, _, count, _ = lines[number]
            total = taken[0].astype(F32)
            for source in range(1, count):
                total += taken[source].astype(F32)
            pieces += [total[t * share : (t + 1) * share] for t in range(quarter)]
        return pieces

    def share_copy(stage, sent, taken, send_seat, recv_seat, device=None):
        return pltpu.make_async_remote_copy(
            src_ref=sent.at[send_seat],
            dst_ref=taken.at[recv_seat],
            send_sem=p1_send.at[stage],
            recv_sem=p1_recv.at[stage],
            device_id=here.seat_device(send_seat) if device is None else device,
            device_id_type=MESH,
        )

    def share_group(stage, sent, taken):
        every = pl.ds(0, seats - 1)
        return share_copy(stage, sent, taken, every, every, here.near(0, 1))

    def put_first(side, lon, far, t, piece):
        begin = t * piece.shape[0]
        s1a[here.seat_of(side, lon, far), begin : begin + piece.shape[0]] = piece

    def send_first(side):
        @pl.loop(0, 2 * n_lon)
        def _(i):
            seat = 2 * n_lon * side + (here.seat + 2 + i) % (2 * n_lon)

            @pl.when(seat != here.seat)
            def _():
                share_copy(0, s1a, q1a, seat, here.seat).start()

    def plane_sum(stage, sent, taken, share):
        taken[here.seat] = sent[here.seat]

        share_group(stage, sent, taken).wait_recv()
        total = taken[0].astype(F32)
        for seat in range(1, seats):
            total += taken[seat].astype(F32)
        return [total[t * share : (t + 1) * share] for t in range(half // 2)]

    def plane_copy(stage, sent, taken, t, slot, z):
        return pltpu.make_async_remote_copy(
            src_ref=sent.at[t],
            dst_ref=taken.at[slot],
            send_sem=p2_send.at[stage],
            recv_sem=p2_recv.at[stage],
            device_id=here.plane_device(z),
            device_id_type=MESH,
        )

    def send_planes(stage, pieces, sent, taken):
        for t in range(half // 2):
            sent[t] = pieces[t].astype(BF)
        for t in range(half // 2):
            z = first_target + 2 * t
            copy = plane_copy(stage, sent, taken, t, here.z // 2, z)
            pl.when(z != here.z)(copy.start)

        @pl.when(own_share)
        def _():
            taken[here.z // 2] = sent[here.z % half // 2]

    def plane_group(stage, sent, taken, own, act):
        count = half // 2 if act == "wait_send" else half
        for less in (0, 1):
            every = pl.ds(0, count - less)
            ref = sent.at[every] if act == "wait_send" else taken.at[every]
            group = pltpu.make_async_remote_copy(
                src_ref=ref,
                dst_ref=ref,
                send_sem=p2_send.at[stage],
                recv_sem=p2_recv.at[stage],
                device_id=here.near(0, 1),
                device_id_type=MESH,
            )
            pl.when(own if less else jnp.logical_not(own))(getattr(group, act))

    def last_copy(stage, sent, taken, lead, slot):
        return pltpu.make_async_remote_copy(
            src_ref=sent,
            dst_ref=taken.at[slot],
            send_sem=p3_send.at[stage],
            recv_sem=p3_recv.at[stage],
            device_id=here.lead_device(lead),
            device_id_type=MESH,
        )

    def send_last(stage, sent, taken, last, last_taken):
        @pl.when(gathers)
        def _():
            plane_group(stage, sent, taken, here.far == 0, "wait_recv")
            total = taken[0].astype(F32)
            for j in range(1, half):
                total += taken[j].astype(F32)
            last[...] = total.astype(BF)
            for lead in (far_same, far_mate, mate):
                last_copy(stage, last, last_taken, lead, here.far).start()
            last_taken[here.far] = total.astype(BF)

    def last_group(stage, last_taken, count):
        every = last_taken.at[pl.ds(0, count)]
        return pltpu.make_async_remote_copy(
            src_ref=every,
            dst_ref=every,
            send_sem=p3_send.at[stage],
            recv_sem=p3_recv.at[stage],
            device_id=here.near(0, 1),
            device_id_type=MESH,
        )

    def final_sum(stage, last_taken, out):
        pl.when(gathers)(last_group(stage, last_taken, 1).wait_recv)
        pl.when(jnp.logical_not(gathers))(last_group(stage, last_taken, 2).wait_recv)
        out[...] = (last_taken[0].astype(F32) + last_taken[1].astype(F32)) * norm

    def tile(field):
        return field[pl.ds(1, rows)].reshape(cells, field.shape[-1])

    weight_grad(1, act_t, act_mate, tile(x2), da2_mate, s3b.shape[0], put_second, send_second)
    line_send_all(0)

    ready("w_two")
    halo_2.wait_recv()
    halo_2.spread(x2, x22)
    total = jnp.zeros((cells, w_two.shape[1]), F32)
    for k, (u, v) in enumerate(OFFSETS):
        total += matmul(window(x2, x22, -u, -v, rows), w_two[k], NT)
    da_first = total.reshape(slope_one.shape) * slope_one[...]
    x1[pl.ds(1, rows)] = da_first.astype(BF)
    halo_1.start_rows()
    halo_1.take_edges()
    halo_1.start_columns()
    mates[2].start()
    weight_grad(0, input_t, input_mate, tile(x1), da1_mate, s3a.shape[0], put_first, send_first)
    pass_second()

    ready("w_one")
    halo_1.wait_recv()
    halo_1.spread(x1, x12)
    total = jnp.zeros((cells, w_one.shape[1]), F32)
    for k, (u, v) in enumerate(OFFSETS):
        total += matmul(window(x1, x12, -u, -v, rows), w_one[k], NT)
    grad_stage[...] = total.astype(BF).reshape(grad_stage.shape)
    for row in range(rows):
        load("out", grad_stage.at[row], grad_out.at[:, row])

    wait_tokens(7, 8)
    send_planes(0, plane_sum(0, s1a, q1a, s3a.shape[0]), s2a, q2a)
    send_planes(1, second_sums(s3b.shape[0]), s2b, q2b)
    send_last(0, s2a, q2a, s3a, q3a)
    send_last(1, s2b, q2b, s3b, q3b)
    ready("out")
    for halo in (halo_h, halo_p, halo_e, halo_2, halo_1):
        halo.wait_send()
    for copy in mates:
        copy.wait_send()
    lead_group.wait_send()
    for number in range(4):
        line_group(number).wait_send()
    share_group(0, s1a, q1a).wait_send()
    plane_group(1, s2b, q2b, own_share, "wait_send")
    plane_group(0, s2a, q2a, own_share, "wait_send")
    final_sum(0, q3a, first_out)
    final_sum(1, q3b, second_out)
    @pl.when(gathers)
    def _():
        last_group(1, q3b, n_lead - 1).wait_send()
        last_group(0, q3a, n_lead - 1).wait_send()


def write_out(input_grad, grad_first, grad_second, grad_out, first_out, second_out, first, second, sem):
    copies = [pltpu.make_async_copy(input_grad, grad_out, sem.at[0])]
    copies[0].start()
    for number, (grad, line, out) in enumerate(((grad_first, first, first_out), (grad_second, second, second_out))):
        width = grad.shape[1]
        for row in range(grad.shape[0]):
            line[pl.ds(row * width, width)] = grad[row]
        copies.append(pltpu.make_async_copy(line, out, sem.at[1 + number]))
        copies[-1].start()
    for copy in copies:
        copy.wait()


def per_device(head_grads, head_weights, encoder_input, pre_first, pre_second, w_first, w_second):
    heads, batch_all, rows, cols, head_width = head_grads.shape
    samples, _, _, in_width = encoder_input.shape
    width = head_weights.shape[2]
    taps = len(OFFSETS)
    n_lead, n_lat, n_lon = lax.axis_size("lead"), lax.axis_size("lat"), lax.axis_size("lon")
    half = n_lat // 4
    seats = 4 * n_lon
    lanes = heads * head_width
    cells = samples * rows * cols
    cells_total = cells * n_lead * n_lat * n_lon
    rows_two, rows_one = taps * width, taps * in_width
    last_two, last_one = rows_two // (n_lat * n_lon), rows_one // (n_lat * n_lon)

    def field(batch, lane):
        full = (rows + 2, batch, cols, lane)
        units = rows * batch // UNIT
        return (
            pltpu.VMEM(full, BF),
            pltpu.VMEM((2,) + full, BF),
            pltpu.VMEM((2, units, UNIT, lane), F32),
            pltpu.VMEM((2, units + 2, UNIT, lane), F32),
        )

    def reduce_buffers(share):
        return (
            pltpu.VMEM((half // 2, share, width), BF),
            pltpu.VMEM((half, share, width), BF),
            pltpu.VMEM((share, width), BF),
            pltpu.VMEM((3, share, width), BF),
        )

    def line_buffers(first, then):
        return [pltpu.VMEM((first, then, last_two * half // 4, width), BF)] * 2

    own = (rows, samples, cols, width)
    act_field = field(samples, width)
    scratch = [
        *field(batch_all, lanes),
        pltpu.VMEM((taps, width, lanes), BF),
        act_field[0], *act_field,
        *field(samples, in_width),
        *field(samples, width),
        *field(samples, width),
        pltpu.VMEM(own, BF),
        pltpu.VMEM(own, F32),
        pltpu.VMEM(own, F32),
        pltpu.VMEM(w_first.shape, BF),
        pltpu.VMEM(w_second.shape, BF),
        pltpu.VMEM((n_lead,) + own, BF),
        pltpu.VMEM((n_lead,) + own, BF),
        pltpu.VMEM((rows_two, cells), BF),
        pltpu.VMEM((rows_one, cells), BF),
        pltpu.VMEM((2, rows_two // 4, cells), BF),
        pltpu.VMEM((2, rows_one // 4, cells), BF),
        pltpu.VMEM(own, BF),
        pltpu.VMEM(own, BF),
        *line_buffers(n_lon, 4),
        *line_buffers(4, n_lon),
        *[pltpu.VMEM((4, last_two * half // 4, width), BF)] * 2,
        *[pltpu.VMEM((n_lon, last_two * half // 4, width), BF)] * 2,
        *reduce_buffers(last_two),
        *[pltpu.VMEM((seats, last_one * half // 2, width), BF)] * 2,
        *reduce_buffers(last_one),
        pltpu.VMEM((rows, samples, cols, in_width), BF),
        pltpu.SemaphoreType.DMA((8,)),
        pltpu.SemaphoreType.DMA((5, 5)),
        pltpu.SemaphoreType.DMA((5, 5)),
        pltpu.SemaphoreType.DMA((1,)),
        pltpu.SemaphoreType.DMA((1,)),
        pltpu.SemaphoreType.DMA((4,)),
        pltpu.SemaphoreType.DMA((4,)),
        pltpu.SemaphoreType.DMA((4,)),
        pltpu.SemaphoreType.DMA((4,)),
        *[pltpu.SemaphoreType.DMA((2,)) for _ in range(6)],
        pltpu.SemaphoreType.REGULAR((9,)),
    ]
    anywhere = pl.BlockSpec(memory_space=pl.ANY)
    input_grad, grad_first, grad_second = pl.pallas_call(
        functools.partial(kernel, 1.0 / math.sqrt(cells_total)),
        out_shape=(
            jax.ShapeDtypeStruct(encoder_input.shape, BF),
            jax.ShapeDtypeStruct((last_one, width), F32),
            jax.ShapeDtypeStruct((last_two, width), F32),
        ),
        in_specs=[anywhere] * 7,
        out_specs=[anywhere] + [pl.BlockSpec(memory_space=pltpu.VMEM)] * 2,
        scratch_shapes=scratch,
        compiler_params=pltpu.CompilerParams(
            collective_id=0, has_side_effects=True, vmem_limit_bytes=55091 * 1024
        ),
    )(head_grads, head_weights, encoder_input, pre_first, pre_second, w_first, w_second)
    flat = [jax.ShapeDtypeStruct((grad.size,), F32) for grad in (grad_first, grad_second)]
    return pl.pallas_call(
        write_out,
        out_shape=(jax.ShapeDtypeStruct(input_grad.shape, BF), *flat),
        in_specs=[anywhere] + [pl.BlockSpec(memory_space=pltpu.VMEM)] * 2,
        out_specs=(anywhere, anywhere, anywhere),
        scratch_shapes=[
            pltpu.VMEM(flat[0].shape, F32),
            pltpu.VMEM(flat[1].shape, F32),
            pltpu.SemaphoreType.DMA((3,)),
        ],
        compiler_params=pltpu.CompilerParams(vmem_limit_bytes=2**20),
    )(input_grad, grad_first, grad_second)


def solution(mesh):
    tile = P("lead", "lat", "lon", None)
    in_specs = (P("lead", None, "lat", "lon", None), P("lead", None, None, None), tile, tile, tile, P(), P())
    out_specs = (tile, P(("lat", "lon")), P(("lat", "lon")))
    return jax.shard_map(
        per_device, mesh=mesh, in_specs=in_specs, out_specs=out_specs, check_vma=False
    )
```

```python
import functools
import math

import jax
import jax.numpy as jnp
from jax import lax
from jax.experimental import pallas as pl
from jax.experimental.pallas import tpu as pltpu
from jax.sharding import PartitionSpec as P

OFFSETS = [(-1, -1), (-1, 0), (-1, 1), (0, -1), (0, 0), (0, 1), (1, -1), (1, 0), (1, 1)]
MESH = pl.DeviceIdType.MESH
BF = jnp.bfloat16
F32 = jnp.float32
NT = (((1,), (1,)), ((), ()))
NN = (((1,), (0,)), ((), ()))
UNIT = 8


def gelu_value(values):
    return 0.5 * values * (1.0 + lax.erf(values * 0.7071067811865476))


def gelu_slope(values):
    return (
        0.5 * (1.0 + lax.erf(values * 0.7071067811865476))
        + values * jnp.exp(-0.5 * values * values) * 0.3989422804014327
    )


def matmul(a, b, dims):
    return lax.dot_general(a, b, dims, preferred_element_type=F32)


class Place:
    def __init__(self):
        self.lead = lax.axis_index("lead")
        self.lat = lax.axis_index("lat")
        self.lon = lax.axis_index("lon")
        self.n_lead = lax.axis_size("lead")
        self.n_lat = lax.axis_size("lat")
        self.n_lon = lax.axis_size("lon")
        self.planes = self.n_lat // 2
        self.side = self.lat // self.planes
        self.z = self.lat % self.planes
        self.far = self.lead // 2
        self.core = self.lead % 2
        self.seats = 4 * self.n_lon
        self.seat = self.seat_of(self.side, self.lon, self.far)
        self.has_low = self.lat > 0
        self.has_high = self.lat < self.n_lat - 1

    def seat_of(self, side, lon, far):
        return (side * self.n_lon + lon) * 2 + far

    def seat_device(self, seat):
        far, lon, side = seat % 2, seat // 2 % self.n_lon, seat // (2 * self.n_lon)
        return (2 * far + self.core, side * self.planes + self.z, lon)

    def lead_device(self, lead):
        return (lead, self.lat, self.lon)

    def plane_device(self, z):
        return (self.lead, self.side * self.planes + z, self.lon)

    def near(self, rows, cols):
        return (self.lead, self.lat + rows, (self.lon + cols + self.n_lon) % self.n_lon)


class Halo:
    def __init__(self, here, rows_out, rows_in, field, edge, ring, send, recv):
        self.here, self.field, self.edge, self.ring = here, field, edge, ring
        self.units = edge.shape[1]
        self.rows = field.shape[0] - 2
        self.batch = field.shape[1]
        self.cols = field.shape[2]
        copies = []
        for high in (0, 1):
            step = 1 if high == 0 else -1
            sends = here.has_high if high == 0 else here.has_low
            for source, target in zip(rows_out[high], rows_in[high]):
                copies.append((sends, source, target, here.near(step, 0), 1 + high))
        self.row_count = len(copies)
        body = pl.ds(1, self.units)
        for right in (0, 1):
            step = 1 if right == 0 else -1
            copies.append((None, edge.at[1 - right], ring.at[right, body], here.near(0, step), 0))
        for high in (0, 1):
            for right in (0, 1):
                row_step = 1 if high == 0 else -1
                col_step = 1 if right == 0 else -1
                sends = here.has_high if high == 0 else here.has_low
                source = edge.at[1 - right, self.units - 1 if high == 0 else 0]
                target = ring.at[right, 0 if high == 0 else self.units + 1]
                copies.append((sends, source, target, here.near(row_step, col_step), 3 + high))

        def remote(source, target, device, number):
            return pltpu.make_async_remote_copy(
                src_ref=source,
                dst_ref=target,
                send_sem=send.at[number],
                recv_sem=recv.at[number],
                device_id=device,
                device_id_type=MESH,
            )

        self.copies = [
            (sends, remote(source, target, device, number))
            for sends, source, target, device, number in copies
        ]
        far_rows = (0, self.rows + 1)
        far_units = (0, self.units + 1)
        self.columns = remote(edge, ring.at[:, body], here.near(0, 1), 0)
        self.row_groups = [
            remote(field.at[far_rows[high]], field.at[far_rows[high]], here.near(0, 1), 1 + high)
            for high in (0, 1)
        ]
        self.corner_groups = [
            remote(edge.at[:, 0], ring.at[:, far_units[high]], here.near(0, 1), 3 + high)
            for high in (0, 1)
        ]

    def start(self, items):
        for sends, copy in items:
            if sends is None:
                copy.start()
            else:
                pl.when(sends)(copy.start)

    def start_rows(self):
        self.start(self.copies[: self.row_count])

    def start_columns(self):
        self.start(self.copies[self.row_count : self.row_count + 2])

    def start_corners(self):
        self.start(self.copies[self.row_count + 2 :])

    def wait_columns(self):
        self.columns.wait_recv()

    def wait_side(self, high):
        takes = self.here.has_high if high else self.here.has_low

        @pl.when(takes)
        def _():
            self.row_groups[high].wait_recv()
            self.corner_groups[high].wait_recv()

    def wait_recv(self):
        self.wait_columns()
        self.wait_side(0)
        self.wait_side(1)

    def wait_send(self):
        self.columns.wait_send()
        for high in (0, 1):
            sends = self.here.has_low if high else self.here.has_high

            @pl.when(sends)
            def _(high=high):
                self.row_groups[high].wait_send()
                self.corner_groups[high].wait_send()

    def clear(self):
        def low():
            self.field[0] = jnp.zeros(self.field.shape[1:], self.field.dtype)
            for side in (0, 1):
                self.ring[side, 0] = jnp.zeros(self.ring.shape[2:], F32)

        def high():
            self.field[self.rows + 1] = jnp.zeros(self.field.shape[1:], self.field.dtype)
            for side in (0, 1):
                self.ring[side, self.units + 1] = jnp.zeros(self.ring.shape[2:], F32)

        pl.when(jnp.logical_not(self.here.has_low))(low)
        pl.when(jnp.logical_not(self.here.has_high))(high)

    def place(self, row, b):
        flat = row * self.batch + b
        return flat // UNIT, flat % UNIT

    def take_edges(self):
        for row in range(self.rows):
            for b in range(self.batch):
                unit, sub = self.place(row, b)
                block = self.field[1 + row, b].astype(F32)
                self.edge[0, unit, sub : sub + 1] = block[0:1]
                self.edge[1, unit, sub : sub + 1] = block[self.cols - 1 : self.cols]

    def ring_row(self, side, ext, b):
        if ext == 0:
            unit, sub = self.place(self.rows - 1, b)
            unit = 0
        elif ext == self.rows + 1:
            unit, sub = self.place(0, b)
            unit = self.units + 1
        else:
            unit, sub = self.place(ext - 1, b)
            unit = unit + 1
        return self.ring[side, unit, sub : sub + 1]

    def spread(self, base, out, rows=None):
        for ext in range(self.rows + 2) if rows is None else rows:
            for b in range(self.batch):
                block = base[ext, b].astype(F32)
                column = lax.broadcasted_iota(jnp.int32, block.shape, 0)
                behind = jnp.where(
                    column == 0, self.ring_row(0, ext, b), pltpu.roll(block, 1, 0)
                )
                ahead = jnp.where(
                    column == self.cols - 1,
                    self.ring_row(1, ext, b),
                    pltpu.roll(block, self.cols - 1, 0),
                )
                out[0, ext, b] = behind.astype(BF)
                out[1, ext, b] = ahead.astype(BF)


def window(base, spread, step_row, step_col, rows, batch=None, first=0):
    row = pl.ds(1 + first + step_row, rows)
    if step_col == 0:
        view = base[row] if batch is None else base[row, batch]
    else:
        side = 0 if step_col < 0 else 1
        view = spread[side, row] if batch is None else spread[side, row, batch]
    return view.reshape(-1, view.shape[-1])


def kernel(
    norm,
    heads_hbm, head_w_hbm, input_hbm, first_hbm, second_hbm, w_first_hbm, w_second_hbm,
    grad_out, first_out, second_out,
    xh, xh2, eh, rh, head_w,
    xp, xa, xa2, ep, rp,
    xe, xe2, ee, re,
    x2, x22, e2, r2,
    x1, x12, e1, r1,
    pre_two, slope_two, slope_one, w_one, w_two,
    part, parts_in, edge_sum,
    act_t, input_t, act_mate, input_mate, da2_mate, da1_mate,
    along_y, from_y, along_x, from_x, then_x, last_x, then_y, last_y, s2b, q2b, s3b, q3b, s1a, q1a, s2a, q2a, s3a, q3a,
    grad_stage,
    load_sem, halo_send, halo_recv, lead_send, lead_recv, mate_send, mate_recv,
    line_send, line_recv, p1_send, p1_recv, p2_send, p2_recv, p3_send, p3_recv, token,
):
    here = Place()
    n_lead, planes, n_lon, seats = here.n_lead, here.planes, here.n_lon, here.seats
    half = planes // 2
    heads, batch_all, rows, cols, head_width = heads_hbm.shape
    samples = input_hbm.shape[0]
    cells = samples * rows * cols

    barrier = pltpu.get_barrier_semaphore()

    def greet(device):
        pl.semaphore_signal(barrier, inc=1, device_id=device, device_id_type=MESH)

    for has, step in ((here.has_low, -1), (here.has_high, 1)):

        def greet_rows(step=step):
            greet(here.near(step, 0))

        pl.when(has)(greet_rows)

    for col in (-1, 1):
        greet(here.near(0, col))
    x_here = 2 * here.far + here.side

    def x_device(x):
        return (2 * (x // 2) + here.core, x % 2 * planes + here.z, here.lon)

    def z_device(step):
        return here.plane_device((here.z + step + planes) % planes)

    for step in (1, 3):
        greet(x_device((x_here + step) % 4))
    for step in (-1, 1):
        greet(z_device(step))
    mate = here.lead + 1 - 2 * here.core
    far_same, far_mate = (here.lead + 2) % n_lead, (mate + 2) % n_lead
    greet(here.lead_device(mate))

    greetings = (
        2 + 2 + 2 + 1
        + jnp.where(here.has_low, 1, 0)
        + jnp.where(here.has_high, 1, 0)
    )

    def send_token(number, device):
        pl.semaphore_signal(token.at[number], inc=1, device_id=device, device_id_type=MESH)

    def send_first_tokens():
        for number, step in ((9, -1), (10, 1)):
            send_token(number, here.near(0, step))
        for number, step in ((11, 1), (12, 3)):
            send_token(number, x_device((x_here + step) % 4))
        send_z_tokens(0)

    def send_plane_tokens():
        send_token(13, here.lead_device(mate))
        for number, step in enumerate((-1, 1, 2)):
            send_token(number, here.near(0, step))

    def send_z_tokens(level):
        for number, step in enumerate((-1, 1)):
            send_token(3 + 2 * level + number, z_device(step * 2**level))

    def wait_tokens(*numbers):
        for number in numbers:
            pl.semaphore_wait(token.at[number], 1)

    gathers = here.z // half == here.core
    first_source = (here.z + here.far) % 2
    first_target = here.core * half + first_source
    own_share = jnp.logical_and(gathers, here.far == 0)

    names = ("heads", "first", "input", "head_w", "second", "w_two", "w_one", "out")
    body = pl.ds(1, rows)
    whole = {
        "heads": xh.at[body], "first": xp.at[body], "input": xe.at[body], "head_w": head_w,
        "second": pre_two, "w_two": w_two, "w_one": w_one, "out": grad_stage,
    }

    def load(key, source, target):
        pltpu.make_async_copy(source, target, load_sem.at[names.index(key)]).start()

    for row in range(rows):
        for h in range(heads):
            lanes = pl.ds(h * head_width, head_width)
            load("heads", heads_hbm.at[h, :, row], xh.at[1 + row, :, :, lanes])
    for row in range(rows):
        load("first", first_hbm.at[:, row], xp.at[1 + row])
        load("input", input_hbm.at[:, row], xe.at[1 + row])
    for h in range(heads):
        load("head_w", head_w_hbm.at[h], head_w.at[:, :, pl.ds(h * head_width, head_width)])
    for row in range(rows):
        load("second", second_hbm.at[:, row], pre_two.at[row])
    load("w_two", w_second_hbm, w_two)
    load("w_one", w_first_hbm, w_one)

    def ready(key):
        pltpu.make_async_copy(whole[key], whole[key], load_sem.at[names.index(key)]).wait()

    lane = [pl.ds(h * head_width, head_width) for h in range(heads)]
    halo_h = Halo(
        here,
        [[heads_hbm.at[h, :, rows - 1] for h in range(heads)], [heads_hbm.at[h, :, 0] for h in range(heads)]],
        [[xh.at[0, :, :, lane[h]] for h in range(heads)], [xh.at[rows + 1, :, :, lane[h]] for h in range(heads)]],
        xh, eh, rh, halo_send.at[0], halo_recv.at[0],
    )
    halo_p = Halo(
        here,
        [[first_hbm.at[:, rows - 1]], [first_hbm.at[:, 0]]],
        [[xp.at[0]], [xp.at[rows + 1]]],
        xp, ep, rp, halo_send.at[1], halo_recv.at[1],
    )
    halo_e = Halo(
        here,
        [[input_hbm.at[:, rows - 1]], [input_hbm.at[:, 0]]],
        [[xe.at[0]], [xe.at[rows + 1]]],
        xe, ee, re, halo_send.at[2], halo_recv.at[2],
    )
    halo_2 = Halo(
        here, [[x2.at[rows]], [x2.at[1]]], [[x2.at[0]], [x2.at[rows + 1]]],
        x2, e2, r2, halo_send.at[3], halo_recv.at[3],
    )
    halo_1 = Halo(
        here, [[x1.at[rows]], [x1.at[1]]], [[x1.at[0]], [x1.at[rows + 1]]],
        x1, e1, r1, halo_send.at[4], halo_recv.at[4],
    )

    halo_h.clear()
    halo_p.clear()
    halo_e.clear()
    halo_2.clear()
    halo_1.clear()
    pl.semaphore_wait(barrier, greetings)
    halo_h.start_rows()
    send_first_tokens()
    ready("heads")
    halo_h.take_edges()
    halo_h.start_columns()
    wait_tokens(9, 10, 11, 12, 3, 4)
    halo_h.start_corners()
    send_plane_tokens()
    send_z_tokens(1)
    ready("first")
    halo_p.take_edges()
    halo_p.start_rows()
    halo_p.start_columns()
    halo_p.start_corners()
    ready("input")
    halo_e.take_edges()
    halo_e.start_rows()
    halo_e.start_columns()
    halo_e.start_corners()
    ready("head_w")

    pieces = (pl.ds(1, rows - 2), pl.ds(0, 1), pl.ds(rows - 1, 1))

    others = pl.ds(0, n_lead - 1)
    lead_group = pltpu.make_async_remote_copy(
        src_ref=part.at[others],
        dst_ref=parts_in.at[others],
        send_sem=lead_send.at[0],
        recv_sem=lead_recv.at[0],
        device_id=here.near(0, 1),
        device_id_type=MESH,
    )

    def lead_copy(source, owner, piece):
        return pltpu.make_async_remote_copy(
            src_ref=part.at[owner, pieces[piece]],
            dst_ref=parts_in.at[source, pieces[piece]],
            send_sem=lead_send.at[0],
            recv_sem=lead_recv.at[0],
            device_id=here.lead_device(owner),
            device_id_type=MESH,
        )

    def convolve(first, count, batch, steps=(-1, 0, 1)):
        total = None
        for k, (u, v) in enumerate(OFFSETS):
            if u in steps:
                term = matmul(window(xh, xh2, -u, -v, count, batch, first), head_w[k], NT)
                total = term if total is None else total + term
        return total

    everyone = pl.ds(0, batch_all)

    halo_h.wait_columns()
    halo_h.spread(xh, xh2, range(1, rows + 1))
    wait_tokens(13)

    @pl.loop(0, 2)
    def _(j):
        far = (here.far + 1 + j) % 2
        block = convolve(1, rows - 2, pl.ds(far * 2 * samples, 2 * samples))
        block = block.astype(BF).reshape((rows - 2, 2 * samples) + part.shape[3:])
        for core in (0, 1):
            owner = 2 * far + core
            part[owner, pieces[0]] = block[:, core * samples : (core + 1) * samples]
            copy = lead_copy(here.lead, owner, 0)
            pl.when(owner != here.lead)(copy.start)

    edge_sum[0] = convolve(0, 1, everyone, (-1, 0))
    edge_sum[1] = convolve(rows - 1, 1, everyone, (0, 1))
    for high in (0, 1):
        halo_h.wait_side(high)
        halo_h.spread(xh, xh2, [(rows + 1) * high])
        block = edge_sum[high] + convolve((rows - 1) * high, 1, everyone, (-1 if high else 1,))
        block = block.astype(BF).reshape((batch_all,) + part.shape[3:])
        for owner in range(n_lead):
            part[owner, (rows - 1) * high] = block[owner * samples : (owner + 1) * samples]
        for j in (2, 3, 1):
            lead_copy(here.lead, (here.lead + j) % n_lead, 1 + high).start()

    ready("second")
    for row in range(rows):
        slope_two[row] = gelu_slope(pre_two[row].astype(F32))
        slope_one[row] = gelu_slope(xp[1 + row].astype(F32))
    halo_p.wait_recv()
    for row in range(rows + 2):
        xa[row] = gelu_value(xp[row].astype(F32)).astype(BF)
    for side in (0, 1):
        for unit in range(rp.shape[1]):
            rp[side, unit] = gelu_value(rp[side, unit])
    halo_p.spread(xa, xa2)
    halo_e.wait_recv()
    halo_e.spread(xe, xe2)
    for k, (u, v) in enumerate(OFFSETS):
        block = window(xa, xa2, u, v, rows)
        act_t[pl.ds(k * block.shape[1], block.shape[1])] = block.T
        block = window(xe, xe2, u, v, rows)
        input_t[pl.ds(k * block.shape[1], block.shape[1])] = block.T

    def mate_copy(number, source, target):
        return pltpu.make_async_remote_copy(
            src_ref=source,
            dst_ref=target,
            send_sem=mate_send.at[number],
            recv_sem=mate_recv.at[number],
            device_id=here.lead_device(mate),
            device_id_type=MESH,
        )

    def turned_rows(turned, side, core):
        block = turned.shape[0] // 4
        return pl.ds(pl.multiple_of((2 * side + core) * block, block), block)

    for stage, turned, taken in ((1, act_t, act_mate), (0, input_t, input_mate)):
        for side in (0, 1):
            rows_there = turned_rows(turned, side, 1 - here.core)
            mate_copy(stage, turned.at[rows_there], taken.at[side]).start()
    mates = [
        mate_copy(0, input_mate, input_mate),
        mate_copy(1, act_mate, act_mate),
        mate_copy(2, x1.at[body], da1_mate),
        mate_copy(3, x2.at[body], da2_mate),
    ]

    lead_group.wait_recv()
    parts_in[here.lead] = part[here.lead]
    for row in range(rows):
        total = parts_in[0, row].astype(F32)
        for a in range(1, n_lead):
            total += parts_in[a, row].astype(F32)
        x2[1 + row] = (total * slope_two[row]).astype(BF)
    halo_2.start_rows()
    halo_2.take_edges()
    halo_2.start_columns()
    halo_2.start_corners()
    mates[3].start()
    wait_tokens(5, 6)
    send_z_tokens(2)
    wait_tokens(0, 1, 2)

    def weight_grad(stage, turned, turned_mate, da, da_mate, share, put, send):
        @pl.loop(0, 2)
        def _(j):
            side = (here.side + 1 + j) % 2
            product = matmul(turned[turned_rows(turned, side, here.core)], da, NN)

            @pl.when(j == 0)
            def _():
                mates[stage].wait_recv()
                mates[2 + stage].wait_recv()

            product += matmul(turned_mate[side], da_mate[...].reshape(da.shape), NN)
            for lon in range(n_lon):
                for odd in (0, 1):
                    far = (odd + here.z) % 2
                    for t in range(half // 2):
                        begin = ((2 * t + odd) * n_lon + lon) * share
                        put(side, lon, far, t, product[begin : begin + share].astype(BF))
            send(side)

    quarter = half // 4

    def lon_device(lon):
        return (here.lead, here.lat, lon)

    def line_copy(number, source, target, device):
        return pltpu.make_async_remote_copy(
            src_ref=source,
            dst_ref=target,
            send_sem=line_send.at[number],
            recv_sem=line_recv.at[number],
            device_id=device,
            device_id_type=MESH,
        )

    lines = (
        (along_y, from_y, here.lon, n_lon, lon_device),
        (along_x, from_x, x_here, 4, x_device),
        (then_x, last_x, x_here, 4, x_device),
        (then_y, last_y, here.lon, n_lon, lon_device),
    )

    def line_send_to(number, there):
        sent, taken, own, _, device = lines[number]
        line_copy(number, sent.at[there], taken.at[own], device(there)).start()

    def line_send_all(number):
        _, _, own, count, _ = lines[number]
        for j in range(1, count):
            line_send_to(number, (own + j) % count)

    def line_group(number):
        sent, taken, _, count, _ = lines[number]
        others = pl.ds(0, count - 1)
        return line_copy(number, sent.at[others], taken.at[others], here.near(0, 1))

    def line_take(number):
        sent, taken, own, _, _ = lines[number]
        line_group(number).wait_recv()
        taken[own] = sent[own]

    def put_second(side, lon, far, t, piece):
        x = 2 * far + side
        begin = t % quarter * piece.shape[0]
        rows_there = slice(begin, begin + piece.shape[0])
        if t < quarter:
            along_y[lon, x, rows_there] = piece
        else:
            along_x[x, lon, rows_there] = piece

    def send_second(side):
        for far in (0, 1):
            x = 2 * far + side
            pl.when(x != x_here)(functools.partial(line_send_to, 1, x))

    def pass_second():
        for number in (0, 1):
            line_take(number)
            _, taken, _, count, _ = lines[number]
            sent = lines[2 + number][0]
            for there in range(sent.shape[0]):
                total = taken[0, there].astype(F32)
                for source in range(1, count):
                    total += taken[source, there].astype(F32)
                sent[there] = total.astype(BF)
            line_send_all(2 + number)

    def second_sums(share):
        pieces = []
        for number in (2, 3):
            line_take(number)
            _, taken, _, count, _ = lines[number]
            total = taken[0].astype(F32)
            for source in range(1, count):
                total += taken[source].astype(F32)
            pieces += [total[t * share : (t + 1) * share] for t in range(quarter)]
        return pieces

    def share_copy(stage, sent, taken, send_seat, recv_seat, device=None):
        return pltpu.make_async_remote_copy(
            src_ref=sent.at[send_seat],
            dst_ref=taken.at[recv_seat],
            send_sem=p1_send.at[stage],
            recv_sem=p1_recv.at[stage],
            device_id=here.seat_device(send_seat) if device is None else device,
            device_id_type=MESH,
        )

    def share_group(stage, sent, taken):
        every = pl.ds(0, seats - 1)
        return share_copy(stage, sent, taken, every, every, here.near(0, 1))

    def put_first(side, lon, far, t, piece):
        begin = t * piece.shape[0]
        s1a[here.seat_of(side, lon, far), begin : begin + piece.shape[0]] = piece

    def send_first(side):
        @pl.loop(0, 2 * n_lon)
        def _(i):
            seat = 2 * n_lon * side + (here.seat + 2 + i) % (2 * n_lon)

            @pl.when(seat != here.seat)
            def _():
                share_copy(0, s1a, q1a, seat, here.seat).start()

    def plane_sum(stage, sent, taken, share):
        taken[here.seat] = sent[here.seat]

        share_group(stage, sent, taken).wait_recv()
        total = taken[0].astype(F32)
        for seat in range(1, seats):
            total += taken[seat].astype(F32)
        return [total[t * share : (t + 1) * share] for t in range(half // 2)]

    def plane_copy(stage, sent, taken, t, slot, z):
        return pltpu.make_async_remote_copy(
            src_ref=sent.at[t],
            dst_ref=taken.at[slot],
            send_sem=p2_send.at[stage],
            recv_sem=p2_recv.at[stage],
            device_id=here.plane_device(z),
            device_id_type=MESH,
        )

    def send_planes(stage, pieces, sent, taken):
        for t in range(half // 2):
            sent[t] = pieces[t].astype(BF)
        for t in range(half // 2):
            z = first_target + 2 * t
            copy = plane_copy(stage, sent, taken, t, here.z // 2, z)
            pl.when(z != here.z)(copy.start)

        @pl.when(own_share)
        def _():
            taken[here.z // 2] = sent[here.z % half // 2]

    def plane_group(stage, sent, taken, own, act):
        count = half // 2 if act == "wait_send" else half
        for less in (0, 1):
            every = pl.ds(0, count - less)
            ref = sent.at[every] if act == "wait_send" else taken.at[every]
            group = pltpu.make_async_remote_copy(
                src_ref=ref,
                dst_ref=ref,
                send_sem=p2_send.at[stage],
                recv_sem=p2_recv.at[stage],
                device_id=here.near(0, 1),
                device_id_type=MESH,
            )
            pl.when(own if less else jnp.logical_not(own))(getattr(group, act))

    def last_copy(stage, sent, taken, lead, slot):
        return pltpu.make_async_remote_copy(
            src_ref=sent,
            dst_ref=taken.at[slot],
            send_sem=p3_send.at[stage],
            recv_sem=p3_recv.at[stage],
            device_id=here.lead_device(lead),
            device_id_type=MESH,
        )

    def send_last(stage, sent, taken, last, last_taken):
        @pl.when(gathers)
        def _():
            plane_group(stage, sent, taken, here.far == 0, "wait_recv")
            total = taken[0].astype(F32)
            for j in range(1, half):
                total += taken[j].astype(F32)
            last[...] = total.astype(BF)
            for lead in (far_same, far_mate, mate):
                last_copy(stage, last, last_taken, lead, here.far).start()
            last_taken[here.far] = total.astype(BF)

    def last_group(stage, last_taken, count):
        every = last_taken.at[pl.ds(0, count)]
        return pltpu.make_async_remote_copy(
            src_ref=every,
            dst_ref=every,
            send_sem=p3_send.at[stage],
            recv_sem=p3_recv.at[stage],
            device_id=here.near(0, 1),
            device_id_type=MESH,
        )

    def final_sum(stage, last_taken, out):
        pl.when(gathers)(last_group(stage, last_taken, 1).wait_recv)
        pl.when(jnp.logical_not(gathers))(last_group(stage, last_taken, 2).wait_recv)
        out[...] = (last_taken[0].astype(F32) + last_taken[1].astype(F32)) * norm

    def tile(field):
        return field[pl.ds(1, rows)].reshape(cells, field.shape[-1])

    weight_grad(1, act_t, act_mate, tile(x2), da2_mate, s3b.shape[0], put_second, send_second)
    line_send_all(0)

    ready("w_two")
    halo_2.wait_recv()
    halo_2.spread(x2, x22)
    total = jnp.zeros((cells, w_two.shape[1]), F32)
    for k, (u, v) in enumerate(OFFSETS):
        total += matmul(window(x2, x22, -u, -v, rows), w_two[k], NT)
    da_first = total.reshape(slope_one.shape) * slope_one[...]
    x1[pl.ds(1, rows)] = da_first.astype(BF)
    halo_1.start_rows()
    halo_1.take_edges()
    halo_1.start_columns()
    halo_1.start_corners()
    mates[2].start()
    weight_grad(0, input_t, input_mate, tile(x1), da1_mate, s3a.shape[0], put_first, send_first)
    pass_second()

    ready("w_one")
    halo_1.wait_recv()
    halo_1.spread(x1, x12)
    total = jnp.zeros((cells, w_one.shape[1]), F32)
    for k, (u, v) in enumerate(OFFSETS):
        total += matmul(window(x1, x12, -u, -v, rows), w_one[k], NT)
    grad_stage[...] = total.astype(BF).reshape(grad_stage.shape)
    for row in range(rows):
        load("out", grad_stage.at[row], grad_out.at[:, row])

    wait_tokens(7, 8)
    send_planes(0, plane_sum(0, s1a, q1a, s3a.shape[0]), s2a, q2a)
    send_planes(1, second_sums(s3b.shape[0]), s2b, q2b)
    send_last(0, s2a, q2a, s3a, q3a)
    send_last(1, s2b, q2b, s3b, q3b)
    ready("out")
    for halo in (halo_h, halo_p, halo_e, halo_2, halo_1):
        halo.wait_send()
    for copy in mates:
        copy.wait_send()
    lead_group.wait_send()
    for number in range(4):
        line_group(number).wait_send()
    share_group(0, s1a, q1a).wait_send()
    plane_group(1, s2b, q2b, own_share, "wait_send")
    plane_group(0, s2a, q2a, own_share, "wait_send")
    final_sum(0, q3a, first_out)
    final_sum(1, q3b, second_out)
    @pl.when(gathers)
    def _():
        last_group(1, q3b, n_lead - 1).wait_send()
        last_group(0, q3a, n_lead - 1).wait_send()


def write_out(input_grad, grad_first, grad_second, grad_out, first_out, second_out, first, second, sem):
    copies = [pltpu.make_async_copy(input_grad, grad_out, sem.at[0])]
    copies[0].start()
    for number, (grad, line, out) in enumerate(((grad_first, first, first_out), (grad_second, second, second_out))):
        width = grad.shape[1]
        for row in range(grad.shape[0]):
            line[pl.ds(row * width, width)] = grad[row]
        copies.append(pltpu.make_async_copy(line, out, sem.at[1 + number]))
        copies[-1].start()
    for copy in copies:
        copy.wait()


def per_device(head_grads, head_weights, encoder_input, pre_first, pre_second, w_first, w_second):
    heads, batch_all, rows, cols, head_width = head_grads.shape
    samples, _, _, in_width = encoder_input.shape
    width = head_weights.shape[2]
    taps = len(OFFSETS)
    n_lead, n_lat, n_lon = lax.axis_size("lead"), lax.axis_size("lat"), lax.axis_size("lon")
    half = n_lat // 4
    seats = 4 * n_lon
    lanes = heads * head_width
    cells = samples * rows * cols
    cells_total = cells * n_lead * n_lat * n_lon
    rows_two, rows_one = taps * width, taps * in_width
    last_two, last_one = rows_two // (n_lat * n_lon), rows_one // (n_lat * n_lon)

    def field(batch, lane):
        full = (rows + 2, batch, cols, lane)
        units = rows * batch // UNIT
        return (
            pltpu.VMEM(full, BF),
            pltpu.VMEM((2,) + full, BF),
            pltpu.VMEM((2, units, UNIT, lane), F32),
            pltpu.VMEM((2, units + 2, UNIT, lane), F32),
        )

    def reduce_buffers(share):
        return (
            pltpu.VMEM((half // 2, share, width), BF),
            pltpu.VMEM((half, share, width), BF),
            pltpu.VMEM((share, width), BF),
            pltpu.VMEM((3, share, width), BF),
        )

    def line_buffers(first, then):
        return [pltpu.VMEM((first, then, last_two * half // 4, width), BF)] * 2

    own = (rows, samples, cols, width)
    act_field = field(samples, width)
    scratch = [
        *field(batch_all, lanes),
        pltpu.VMEM((taps, width, lanes), BF),
        act_field[0], *act_field,
        *field(samples, in_width),
        *field(samples, width),
        *field(samples, width),
        pltpu.VMEM(own, BF),
        pltpu.VMEM(own, F32),
        pltpu.VMEM(own, F32),
        pltpu.VMEM(w_first.shape, BF),
        pltpu.VMEM(w_second.shape, BF),
        pltpu.VMEM((n_lead,) + own, BF),
        pltpu.VMEM((n_lead,) + own, BF),
        pltpu.VMEM((2, batch_all * cols, width), F32),
        pltpu.VMEM((rows_two, cells), BF),
        pltpu.VMEM((rows_one, cells), BF),
        pltpu.VMEM((2, rows_two // 4, cells), BF),
        pltpu.VMEM((2, rows_one // 4, cells), BF),
        pltpu.VMEM(own, BF),
        pltpu.VMEM(own, BF),
        *line_buffers(n_lon, 4),
        *line_buffers(4, n_lon),
        *[pltpu.VMEM((4, last_two * half // 4, width), BF)] * 2,
        *[pltpu.VMEM((n_lon, last_two * half // 4, width), BF)] * 2,
        *reduce_buffers(last_two),
        *[pltpu.VMEM((seats, last_one * half // 2, width), BF)] * 2,
        *reduce_buffers(last_one),
        pltpu.VMEM((rows, samples, cols, in_width), BF),
        pltpu.SemaphoreType.DMA((8,)),
        pltpu.SemaphoreType.DMA((5, 5)),
        pltpu.SemaphoreType.DMA((5, 5)),
        pltpu.SemaphoreType.DMA((1,)),
        pltpu.SemaphoreType.DMA((1,)),
        pltpu.SemaphoreType.DMA((4,)),
        pltpu.SemaphoreType.DMA((4,)),
        pltpu.SemaphoreType.DMA((4,)),
        pltpu.SemaphoreType.DMA((4,)),
        *[pltpu.SemaphoreType.DMA((2,)) for _ in range(6)],
        pltpu.SemaphoreType.REGULAR((14,)),
    ]
    anywhere = pl.BlockSpec(memory_space=pl.ANY)
    input_grad, grad_first, grad_second = pl.pallas_call(
        functools.partial(kernel, 1.0 / math.sqrt(cells_total)),
        out_shape=(
            jax.ShapeDtypeStruct(encoder_input.shape, BF),
            jax.ShapeDtypeStruct((last_one, width), F32),
            jax.ShapeDtypeStruct((last_two, width), F32),
        ),
        in_specs=[anywhere] * 7,
        out_specs=[anywhere] + [pl.BlockSpec(memory_space=pltpu.VMEM)] * 2,
        scratch_shapes=scratch,
        compiler_params=pltpu.CompilerParams(
            collective_id=0, has_side_effects=True, vmem_limit_bytes=55091 * 1024
        ),
    )(head_grads, head_weights, encoder_input, pre_first, pre_second, w_first, w_second)
    flat = [jax.ShapeDtypeStruct((grad.size,), F32) for grad in (grad_first, grad_second)]
    return pl.pallas_call(
        write_out,
        out_shape=(jax.ShapeDtypeStruct(input_grad.shape, BF), *flat),
        in_specs=[anywhere] + [pl.BlockSpec(memory_space=pltpu.VMEM)] * 2,
        out_specs=(anywhere, anywhere, anywhere),
        scratch_shapes=[
            pltpu.VMEM(flat[0].shape, F32),
            pltpu.VMEM(flat[1].shape, F32),
            pltpu.SemaphoreType.DMA((3,)),
        ],
        compiler_params=pltpu.CompilerParams(vmem_limit_bytes=2**20),
    )(input_grad, grad_first, grad_second)


def solution(mesh):
    tile = P("lead", "lat", "lon", None)
    in_specs = (P("lead", None, "lat", "lon", None), P("lead", None, None, None), tile, tile, tile, P(), P())
    out_specs = (tile, P(("lat", "lon")), P(("lat", "lon")))
    return jax.shard_map(
        per_device, mesh=mesh, in_specs=in_specs, out_specs=out_specs, check_vma=False
    )
```

```python
import functools
import math

import jax
import jax.numpy as jnp
from jax import lax
from jax.experimental import pallas as pl
from jax.experimental.pallas import tpu as pltpu
from jax.sharding import PartitionSpec as P

OFFSETS = [(-1, -1), (-1, 0), (-1, 1), (0, -1), (0, 0), (0, 1), (1, -1), (1, 0), (1, 1)]
MESH = pl.DeviceIdType.MESH
BF = jnp.bfloat16
F32 = jnp.float32
NT = (((1,), (1,)), ((), ()))
NN = (((1,), (0,)), ((), ()))
UNIT = 8


def gelu_value(values):
    return 0.5 * values * (1.0 + lax.erf(values * 0.7071067811865476))


def gelu_slope(values):
    return (
        0.5 * (1.0 + lax.erf(values * 0.7071067811865476))
        + values * jnp.exp(-0.5 * values * values) * 0.3989422804014327
    )


def matmul(a, b, dims):
    return lax.dot_general(a, b, dims, preferred_element_type=F32)


class Place:
    def __init__(self):
        self.lead = lax.axis_index("lead")
        self.lat = lax.axis_index("lat")
        self.lon = lax.axis_index("lon")
        self.n_lead = lax.axis_size("lead")
        self.n_lat = lax.axis_size("lat")
        self.n_lon = lax.axis_size("lon")
        self.planes = self.n_lat // 2
        self.side = self.lat // self.planes
        self.z = self.lat % self.planes
        self.far = self.lead // 2
        self.core = self.lead % 2
        self.seats = 4 * self.n_lon
        self.seat = self.seat_of(self.side, self.lon, self.far)
        self.has_low = self.lat > 0
        self.has_high = self.lat < self.n_lat - 1

    def seat_of(self, side, lon, far):
        return (side * self.n_lon + lon) * 2 + far

    def seat_device(self, seat):
        far, lon, side = seat % 2, seat // 2 % self.n_lon, seat // (2 * self.n_lon)
        return (2 * far + self.core, side * self.planes + self.z, lon)

    def lead_device(self, lead):
        return (lead, self.lat, self.lon)

    def plane_device(self, z):
        return (self.lead, self.side * self.planes + z, self.lon)

    def near(self, rows, cols):
        return (self.lead, self.lat + rows, (self.lon + cols + self.n_lon) % self.n_lon)


class Halo:
    def __init__(self, here, rows_out, rows_in, field, edge, ring, send, recv):
        self.here, self.field, self.edge, self.ring = here, field, edge, ring
        self.units = edge.shape[1]
        self.rows = field.shape[0] - 2
        self.batch = field.shape[1]
        self.cols = field.shape[2]
        copies = []
        for high in (0, 1):
            step = 1 if high == 0 else -1
            sends = here.has_high if high == 0 else here.has_low
            for source, target in zip(rows_out[high], rows_in[high]):
                copies.append((sends, source, target, here.near(step, 0), 1 + high))
        self.row_count = len(copies)
        body = pl.ds(1, self.units)
        for right in (0, 1):
            step = 1 if right == 0 else -1
            copies.append((None, edge.at[1 - right], ring.at[right, body], here.near(0, step), 0))
        for high in (0, 1):
            for right in (0, 1):
                row_step = 1 if high == 0 else -1
                col_step = 1 if right == 0 else -1
                sends = here.has_high if high == 0 else here.has_low
                source = edge.at[1 - right, self.units - 1 if high == 0 else 0]
                target = ring.at[right, 0 if high == 0 else self.units + 1]
                copies.append((sends, source, target, here.near(row_step, col_step), 3 + high))

        def remote(source, target, device, number):
            return pltpu.make_async_remote_copy(
                src_ref=source,
                dst_ref=target,
                send_sem=send.at[number],
                recv_sem=recv.at[number],
                device_id=device,
                device_id_type=MESH,
            )

        self.copies = [
            (sends, remote(source, target, device, number))
            for sends, source, target, device, number in copies
        ]
        far_rows = (0, self.rows + 1)
        far_units = (0, self.units + 1)
        self.columns = remote(edge, ring.at[:, body], here.near(0, 1), 0)
        self.row_groups = [
            remote(field.at[far_rows[high]], field.at[far_rows[high]], here.near(0, 1), 1 + high)
            for high in (0, 1)
        ]
        self.corner_groups = [
            remote(edge.at[:, 0], ring.at[:, far_units[high]], here.near(0, 1), 3 + high)
            for high in (0, 1)
        ]

    def start(self, items):
        for sends, copy in items:
            if sends is None:
                copy.start()
            else:
                pl.when(sends)(copy.start)

    def start_rows(self):
        self.start(self.copies[: self.row_count])

    def start_columns(self):
        self.start(self.copies[self.row_count : self.row_count + 2])

    def start_corners(self):
        self.start(self.copies[self.row_count + 2 :])

    def wait_columns(self):
        self.columns.wait_recv()

    def wait_side(self, high):
        takes = self.here.has_high if high else self.here.has_low

        @pl.when(takes)
        def _():
            self.row_groups[high].wait_recv()
            self.corner_groups[high].wait_recv()

    def wait_recv(self):
        self.wait_columns()
        self.wait_side(0)
        self.wait_side(1)

    def wait_send(self):
        self.columns.wait_send()
        for high in (0, 1):
            sends = self.here.has_low if high else self.here.has_high

            @pl.when(sends)
            def _(high=high):
                self.row_groups[high].wait_send()
                self.corner_groups[high].wait_send()

    def clear(self):
        def low():
            self.field[0] = jnp.zeros(self.field.shape[1:], self.field.dtype)
            for side in (0, 1):
                self.ring[side, 0] = jnp.zeros(self.ring.shape[2:], F32)

        def high():
            self.field[self.rows + 1] = jnp.zeros(self.field.shape[1:], self.field.dtype)
            for side in (0, 1):
                self.ring[side, self.units + 1] = jnp.zeros(self.ring.shape[2:], F32)

        pl.when(jnp.logical_not(self.here.has_low))(low)
        pl.when(jnp.logical_not(self.here.has_high))(high)

    def place(self, row, b):
        flat = row * self.batch + b
        return flat // UNIT, flat % UNIT

    def take_edges(self):
        for row in range(self.rows):
            for b in range(self.batch):
                unit, sub = self.place(row, b)
                block = self.field[1 + row, b].astype(F32)
                self.edge[0, unit, sub : sub + 1] = block[0:1]
                self.edge[1, unit, sub : sub + 1] = block[self.cols - 1 : self.cols]

    def ring_row(self, side, ext, b):
        if ext == 0:
            unit, sub = self.place(self.rows - 1, b)
            unit = 0
        elif ext == self.rows + 1:
            unit, sub = self.place(0, b)
            unit = self.units + 1
        else:
            unit, sub = self.place(ext - 1, b)
            unit = unit + 1
        return self.ring[side, unit, sub : sub + 1]

    def spread(self, base, out, rows=None):
        for ext in range(self.rows + 2) if rows is None else rows:
            for b in range(self.batch):
                block = base[ext, b].astype(F32)
                column = lax.broadcasted_iota(jnp.int32, block.shape, 0)
                behind = jnp.where(
                    column == 0, self.ring_row(0, ext, b), pltpu.roll(block, 1, 0)
                )
                ahead = jnp.where(
                    column == self.cols - 1,
                    self.ring_row(1, ext, b),
                    pltpu.roll(block, self.cols - 1, 0),
                )
                out[0, ext, b] = behind.astype(BF)
                out[1, ext, b] = ahead.astype(BF)


def window(base, spread, step_row, step_col, rows, batch=None, first=0):
    row = pl.ds(1 + first + step_row, rows)
    if step_col == 0:
        view = base[row] if batch is None else base[row, batch]
    else:
        side = 0 if step_col < 0 else 1
        view = spread[side, row] if batch is None else spread[side, row, batch]
    return view.reshape(-1, view.shape[-1])


def kernel(
    norm,
    heads_hbm, head_w_hbm, input_hbm, first_hbm, second_hbm, w_first_hbm, w_second_hbm,
    grad_out, first_out, second_out,
    xh, xh2, eh, rh, head_w,
    xp, xa, xa2, ep, rp,
    xe, xe2, ee, re,
    x2, x22, e2, r2,
    x1, x12, e1, r1,
    pre_two, slope_two, slope_one, w_one, w_two,
    part, parts_in, edge_sum, own_product,
    act_t, input_t, act_mate, input_mate, da2_mate, da1_mate,
    along_y, from_y, along_x, from_x, then_x, last_x, then_y, last_y, s2b, q2b, s3b, q3b, s1a, q1a, s2a, q2a, s3a, q3a,
    grad_stage,
    load_sem, halo_send, halo_recv, lead_send, lead_recv, mate_send, mate_recv,
    line_send, line_recv, p1_send, p1_recv, p2_send, p2_recv, p3_send, p3_recv, token,
):
    here = Place()
    n_lead, planes, n_lon, seats = here.n_lead, here.planes, here.n_lon, here.seats
    half = planes // 2
    heads, batch_all, rows, cols, head_width = heads_hbm.shape
    samples = input_hbm.shape[0]
    cells = samples * rows * cols

    barrier = pltpu.get_barrier_semaphore()

    def greet(device):
        pl.semaphore_signal(barrier, inc=1, device_id=device, device_id_type=MESH)

    for has, step in ((here.has_low, -1), (here.has_high, 1)):

        def greet_rows(step=step):
            greet(here.near(step, 0))

        pl.when(has)(greet_rows)

    for col in (-1, 1):
        greet(here.near(0, col))
    x_here = 2 * here.far + here.side

    def x_device(x):
        return (2 * (x // 2) + here.core, x % 2 * planes + here.z, here.lon)

    def z_device(step):
        return here.plane_device((here.z + step + planes) % planes)

    for step in (1, 3):
        greet(x_device((x_here + step) % 4))
    for step in (-1, 1):
        greet(z_device(step))
    mate = here.lead + 1 - 2 * here.core
    far_same, far_mate = (here.lead + 2) % n_lead, (mate + 2) % n_lead
    greet(here.lead_device(mate))

    greetings = (
        2 + 2 + 2 + 1
        + jnp.where(here.has_low, 1, 0)
        + jnp.where(here.has_high, 1, 0)
    )

    def send_token(number, device):
        pl.semaphore_signal(token.at[number], inc=1, device_id=device, device_id_type=MESH)

    def send_first_tokens():
        for number, step in ((9, -1), (10, 1)):
            send_token(number, here.near(0, step))
        for number, step in ((11, 1), (12, 3)):
            send_token(number, x_device((x_here + step) % 4))
        send_z_tokens(0)

    def send_plane_tokens():
        send_token(13, here.lead_device(mate))
        for number, step in enumerate((-1, 1, 2)):
            send_token(number, here.near(0, step))

    def send_z_tokens(level):
        for number, step in enumerate((-1, 1)):
            send_token(3 + 2 * level + number, z_device(step * 2**level))

    def wait_tokens(*numbers):
        for number in numbers:
            pl.semaphore_wait(token.at[number], 1)

    gathers = here.z // half == here.core
    first_source = (here.z + here.far) % 2
    first_target = here.core * half + first_source
    own_share = jnp.logical_and(gathers, here.far == 0)

    names = ("heads", "first", "input", "head_w", "second", "w_two", "w_one", "out")
    body = pl.ds(1, rows)
    whole = {
        "heads": xh.at[body], "first": xp.at[body], "input": xe.at[body], "head_w": head_w,
        "second": pre_two, "w_two": w_two, "w_one": w_one, "out": grad_stage,
    }

    def load(key, source, target):
        pltpu.make_async_copy(source, target, load_sem.at[names.index(key)]).start()

    for row in range(rows):
        for h in range(heads):
            lanes = pl.ds(h * head_width, head_width)
            load("heads", heads_hbm.at[h, :, row], xh.at[1 + row, :, :, lanes])
    for row in range(rows):
        load("first", first_hbm.at[:, row], xp.at[1 + row])
        load("input", input_hbm.at[:, row], xe.at[1 + row])
    for h in range(heads):
        load("head_w", head_w_hbm.at[h], head_w.at[:, :, pl.ds(h * head_width, head_width)])
    for row in range(rows):
        load("second", second_hbm.at[:, row], pre_two.at[row])
    load("w_two", w_second_hbm, w_two)
    load("w_one", w_first_hbm, w_one)

    def ready(key):
        pltpu.make_async_copy(whole[key], whole[key], load_sem.at[names.index(key)]).wait()

    lane = [pl.ds(h * head_width, head_width) for h in range(heads)]
    halo_h = Halo(
        here,
        [[heads_hbm.at[h, :, rows - 1] for h in range(heads)], [heads_hbm.at[h, :, 0] for h in range(heads)]],
        [[xh.at[0, :, :, lane[h]] for h in range(heads)], [xh.at[rows + 1, :, :, lane[h]] for h in range(heads)]],
        xh, eh, rh, halo_send.at[0], halo_recv.at[0],
    )
    halo_p = Halo(
        here,
        [[first_hbm.at[:, rows - 1]], [first_hbm.at[:, 0]]],
        [[xp.at[0]], [xp.at[rows + 1]]],
        xp, ep, rp, halo_send.at[1], halo_recv.at[1],
    )
    halo_e = Halo(
        here,
        [[input_hbm.at[:, rows - 1]], [input_hbm.at[:, 0]]],
        [[xe.at[0]], [xe.at[rows + 1]]],
        xe, ee, re, halo_send.at[2], halo_recv.at[2],
    )
    halo_2 = Halo(
        here, [[x2.at[rows]], [x2.at[1]]], [[x2.at[0]], [x2.at[rows + 1]]],
        x2, e2, r2, halo_send.at[3], halo_recv.at[3],
    )
    halo_1 = Halo(
        here, [[x1.at[rows]], [x1.at[1]]], [[x1.at[0]], [x1.at[rows + 1]]],
        x1, e1, r1, halo_send.at[4], halo_recv.at[4],
    )

    halo_h.clear()
    halo_p.clear()
    halo_e.clear()
    halo_2.clear()
    halo_1.clear()
    pl.semaphore_wait(barrier, greetings)
    halo_h.start_rows()
    send_first_tokens()
    ready("heads")
    halo_h.take_edges()
    halo_h.start_columns()
    wait_tokens(9, 10, 11, 12, 3, 4)
    halo_h.start_corners()
    send_plane_tokens()
    send_z_tokens(1)
    ready("first")
    halo_p.take_edges()
    halo_p.start_rows()
    halo_p.start_columns()
    halo_p.start_corners()
    ready("input")
    halo_e.take_edges()
    halo_e.start_rows()
    halo_e.start_columns()
    halo_e.start_corners()
    ready("head_w")

    pieces = (pl.ds(1, rows - 2), pl.ds(0, 1), pl.ds(rows - 1, 1))

    others = pl.ds(0, n_lead - 1)
    lead_group = pltpu.make_async_remote_copy(
        src_ref=part.at[others],
        dst_ref=parts_in.at[others],
        send_sem=lead_send.at[0],
        recv_sem=lead_recv.at[0],
        device_id=here.near(0, 1),
        device_id_type=MESH,
    )

    def lead_copy(source, owner, piece):
        return pltpu.make_async_remote_copy(
            src_ref=part.at[owner, pieces[piece]],
            dst_ref=parts_in.at[source, pieces[piece]],
            send_sem=lead_send.at[0],
            recv_sem=lead_recv.at[0],
            device_id=here.lead_device(owner),
            device_id_type=MESH,
        )

    def convolve(first, count, batch, steps=(-1, 0, 1)):
        total = None
        for k, (u, v) in enumerate(OFFSETS):
            if u in steps:
                term = matmul(window(xh, xh2, -u, -v, count, batch, first), head_w[k], NT)
                total = term if total is None else total + term
        return total

    everyone = pl.ds(0, batch_all)

    halo_h.wait_columns()
    halo_h.spread(xh, xh2, range(1, rows + 1))
    wait_tokens(13)

    @pl.loop(0, 2)
    def _(j):
        far = (here.far + 1 + j) % 2
        block = convolve(1, rows - 2, pl.ds(far * 2 * samples, 2 * samples))
        block = block.astype(BF).reshape((rows - 2, 2 * samples) + part.shape[3:])
        for core in (0, 1):
            owner = 2 * far + core
            part[owner, pieces[0]] = block[:, core * samples : (core + 1) * samples]
            copy = lead_copy(here.lead, owner, 0)
            pl.when(owner != here.lead)(copy.start)

    edge_sum[0] = convolve(0, 1, everyone, (-1, 0))
    edge_sum[1] = convolve(rows - 1, 1, everyone, (0, 1))
    for high in (0, 1):
        halo_h.wait_side(high)
        halo_h.spread(xh, xh2, [(rows + 1) * high])
        block = edge_sum[high] + convolve((rows - 1) * high, 1, everyone, (-1 if high else 1,))
        block = block.astype(BF).reshape((batch_all,) + part.shape[3:])
        for owner in range(n_lead):
            part[owner, (rows - 1) * high] = block[owner * samples : (owner + 1) * samples]
        for j in (2, 3, 1):
            lead_copy(here.lead, (here.lead + j) % n_lead, 1 + high).start()

    ready("second")
    for row in range(rows):
        slope_two[row] = gelu_slope(pre_two[row].astype(F32))
        slope_one[row] = gelu_slope(xp[1 + row].astype(F32))
    halo_p.wait_recv()
    for row in range(rows + 2):
        xa[row] = gelu_value(xp[row].astype(F32)).astype(BF)
    for side in (0, 1):
        for unit in range(rp.shape[1]):
            rp[side, unit] = gelu_value(rp[side, unit])
    halo_p.spread(xa, xa2)
    halo_e.wait_recv()
    halo_e.spread(xe, xe2)
    for k, (u, v) in enumerate(OFFSETS):
        block = window(xa, xa2, u, v, rows)
        act_t[pl.ds(k * block.shape[1], block.shape[1])] = block.T
        block = window(xe, xe2, u, v, rows)
        input_t[pl.ds(k * block.shape[1], block.shape[1])] = block.T

    def mate_copy(number, source, target):
        return pltpu.make_async_remote_copy(
            src_ref=source,
            dst_ref=target,
            send_sem=mate_send.at[number],
            recv_sem=mate_recv.at[number],
            device_id=here.lead_device(mate),
            device_id_type=MESH,
        )

    def turned_rows(turned, side, core):
        block = turned.shape[0] // 4
        return pl.ds(pl.multiple_of((2 * side + core) * block, block), block)

    for stage, turned, taken in ((1, act_t, act_mate), (0, input_t, input_mate)):
        for side in (0, 1):
            rows_there = turned_rows(turned, side, 1 - here.core)
            mate_copy(stage, turned.at[rows_there], taken.at[side]).start()
    mates = [
        mate_copy(0, input_mate, input_mate),
        mate_copy(1, act_mate, act_mate),
        mate_copy(2, x1.at[body], da1_mate),
        mate_copy(3, x2.at[body], da2_mate),
    ]

    lead_group.wait_recv()
    parts_in[here.lead] = part[here.lead]
    for row in range(rows):
        total = parts_in[0, row].astype(F32)
        for a in range(1, n_lead):
            total += parts_in[a, row].astype(F32)
        x2[1 + row] = (total * slope_two[row]).astype(BF)
    halo_2.start_rows()
    halo_2.take_edges()
    halo_2.start_columns()
    halo_2.start_corners()
    mates[3].start()
    wait_tokens(5, 6)
    send_z_tokens(2)
    wait_tokens(0, 1, 2)

    def weight_grad(stage, turned, turned_mate, da, da_mate, share, put, send):
        block = turned.shape[0] // 4
        for j in (0, 1):
            side = (here.side + 1 + j) % 2
            own_product[j, pl.ds(0, block)] = matmul(turned[turned_rows(turned, side, here.core)], da, NN)
        mates[stage].wait_recv()
        mates[2 + stage].wait_recv()

        @pl.loop(0, 2)
        def _(j):
            side = (here.side + 1 + j) % 2
            product = own_product[j, pl.ds(0, block)]
            product += matmul(turned_mate[side], da_mate[...].reshape(da.shape), NN)
            for lon in range(n_lon):
                for odd in (0, 1):
                    far = (odd + here.z) % 2
                    for t in range(half // 2):
                        begin = ((2 * t + odd) * n_lon + lon) * share
                        put(side, lon, far, t, product[begin : begin + share].astype(BF))
            send(side)

    quarter = half // 4

    def lon_device(lon):
        return (here.lead, here.lat, lon)

    def line_copy(number, source, target, device):
        return pltpu.make_async_remote_copy(
            src_ref=source,
            dst_ref=target,
            send_sem=line_send.at[number],
            recv_sem=line_recv.at[number],
            device_id=device,
            device_id_type=MESH,
        )

    lines = (
        (along_y, from_y, here.lon, n_lon, lon_device),
        (along_x, from_x, x_here, 4, x_device),
        (then_x, last_x, x_here, 4, x_device),
        (then_y, last_y, here.lon, n_lon, lon_device),
    )

    def line_send_to(number, there):
        sent, taken, own, _, device = lines[number]
        line_copy(number, sent.at[there], taken.at[own], device(there)).start()

    def line_send_all(number):
        _, _, own, count, _ = lines[number]
        for j in range(1, count):
            line_send_to(number, (own + j) % count)

    def line_group(number):
        sent, taken, _, count, _ = lines[number]
        others = pl.ds(0, count - 1)
        return line_copy(number, sent.at[others], taken.at[others], here.near(0, 1))

    def line_take(number):
        sent, taken, own, _, _ = lines[number]
        line_group(number).wait_recv()
        taken[own] = sent[own]

    def put_second(side, lon, far, t, piece):
        x = 2 * far + side
        begin = t % quarter * piece.shape[0]
        rows_there = slice(begin, begin + piece.shape[0])
        if t < quarter:
            along_y[lon, x, rows_there] = piece
        else:
            along_x[x, lon, rows_there] = piece

    def send_second(side):
        for far in (0, 1):
            x = 2 * far + side
            pl.when(x != x_here)(functools.partial(line_send_to, 1, x))

    def pass_second():
        for number in (0, 1):
            line_take(number)
            _, taken, _, count, _ = lines[number]
            sent = lines[2 + number][0]
            for there in range(sent.shape[0]):
                total = taken[0, there].astype(F32)
                for source in range(1, count):
                    total += taken[source, there].astype(F32)
                sent[there] = total.astype(BF)
            line_send_all(2 + number)

    def second_sums(share):
        pieces = []
        for number in (2, 3):
            line_take(number)
            _, taken, _, count, _ = lines[number]
            total = taken[0].astype(F32)
            for source in range(1, count):
                total += taken[source].astype(F32)
            pieces += [total[t * share : (t + 1) * share] for t in range(quarter)]
        return pieces

    def share_copy(stage, sent, taken, send_seat, recv_seat, device=None):
        return pltpu.make_async_remote_copy(
            src_ref=sent.at[send_seat],
            dst_ref=taken.at[recv_seat],
            send_sem=p1_send.at[stage],
            recv_sem=p1_recv.at[stage],
            device_id=here.seat_device(send_seat) if device is None else device,
            device_id_type=MESH,
        )

    def share_group(stage, sent, taken):
        every = pl.ds(0, seats - 1)
        return share_copy(stage, sent, taken, every, every, here.near(0, 1))

    def put_first(side, lon, far, t, piece):
        begin = t * piece.shape[0]
        s1a[here.seat_of(side, lon, far), begin : begin + piece.shape[0]] = piece

    def send_first(side):
        @pl.loop(0, 2 * n_lon)
        def _(i):
            seat = 2 * n_lon * side + (here.seat + 2 + i) % (2 * n_lon)

            @pl.when(seat != here.seat)
            def _():
                share_copy(0, s1a, q1a, seat, here.seat).start()

    def plane_sum(stage, sent, taken, share):
        taken[here.seat] = sent[here.seat]

        share_group(stage, sent, taken).wait_recv()
        total = taken[0].astype(F32)
        for seat in range(1, seats):
            total += taken[seat].astype(F32)
        return [total[t * share : (t + 1) * share] for t in range(half // 2)]

    def plane_copy(stage, sent, taken, t, slot, z):
        return pltpu.make_async_remote_copy(
            src_ref=sent.at[t],
            dst_ref=taken.at[slot],
            send_sem=p2_send.at[stage],
            recv_sem=p2_recv.at[stage],
            device_id=here.plane_device(z),
            device_id_type=MESH,
        )

    def send_planes(stage, pieces, sent, taken):
        for t in range(half // 2):
            sent[t] = pieces[t].astype(BF)
        for t in range(half // 2):
            z = first_target + 2 * t
            copy = plane_copy(stage, sent, taken, t, here.z // 2, z)
            pl.when(z != here.z)(copy.start)

        @pl.when(own_share)
        def _():
            taken[here.z // 2] = sent[here.z % half // 2]

    def plane_group(stage, sent, taken, own, act):
        count = half // 2 if act == "wait_send" else half
        for less in (0, 1):
            every = pl.ds(0, count - less)
            ref = sent.at[every] if act == "wait_send" else taken.at[every]
            group = pltpu.make_async_remote_copy(
                src_ref=ref,
                dst_ref=ref,
                send_sem=p2_send.at[stage],
                recv_sem=p2_recv.at[stage],
                device_id=here.near(0, 1),
                device_id_type=MESH,
            )
            pl.when(own if less else jnp.logical_not(own))(getattr(group, act))

    def last_copy(stage, sent, taken, lead, slot):
        return pltpu.make_async_remote_copy(
            src_ref=sent,
            dst_ref=taken.at[slot],
            send_sem=p3_send.at[stage],
            recv_sem=p3_recv.at[stage],
            device_id=here.lead_device(lead),
            device_id_type=MESH,
        )

    def send_last(stage, sent, taken, last, last_taken):
        @pl.when(gathers)
        def _():
            plane_group(stage, sent, taken, here.far == 0, "wait_recv")
            total = taken[0].astype(F32)
            for j in range(1, half):
                total += taken[j].astype(F32)
            last[...] = total.astype(BF)
            for lead in (far_same, far_mate, mate):
                last_copy(stage, last, last_taken, lead, here.far).start()
            last_taken[here.far] = total.astype(BF)

    def last_group(stage, last_taken, count):
        every = last_taken.at[pl.ds(0, count)]
        return pltpu.make_async_remote_copy(
            src_ref=every,
            dst_ref=every,
            send_sem=p3_send.at[stage],
            recv_sem=p3_recv.at[stage],
            device_id=here.near(0, 1),
            device_id_type=MESH,
        )

    def final_sum(stage, last_taken, out):
        pl.when(gathers)(last_group(stage, last_taken, 1).wait_recv)
        pl.when(jnp.logical_not(gathers))(last_group(stage, last_taken, 2).wait_recv)
        out[...] = (last_taken[0].astype(F32) + last_taken[1].astype(F32)) * norm

    def tile(field):
        return field[pl.ds(1, rows)].reshape(cells, field.shape[-1])

    weight_grad(1, act_t, act_mate, tile(x2), da2_mate, s3b.shape[0], put_second, send_second)
    line_send_all(0)

    def second_layer(first, count, steps=(-1, 0, 1)):
        total = None
        for k, (u, v) in enumerate(OFFSETS):
            if u in steps:
                term = matmul(window(x2, x22, -u, -v, count, None, first), w_two[k], NT)
                total = term if total is None else total + term
        return total

    def store_first(first, count, total):
        slope = slope_one[pl.ds(first, count)]
        x1[pl.ds(1 + first, count)] = (total.reshape(slope.shape) * slope).astype(BF)

    ready("w_two")
    halo_2.wait_columns()
    halo_2.spread(x2, x22, range(1, rows + 1))
    store_first(1, rows - 2, second_layer(1, rows - 2))
    early = (second_layer(0, 1, (-1, 0)), second_layer(rows - 1, 1, (0, 1)))
    halo_2.wait_side(0)
    halo_2.wait_side(1)
    halo_2.spread(x2, x22, (0, rows + 1))
    store_first(0, 1, early[0] + second_layer(0, 1, (1,)))
    store_first(rows - 1, 1, early[1] + second_layer(rows - 1, 1, (-1,)))
    halo_1.start_rows()
    halo_1.take_edges()
    halo_1.start_columns()
    halo_1.start_corners()
    mates[2].start()
    weight_grad(0, input_t, input_mate, tile(x1), da1_mate, s3a.shape[0], put_first, send_first)
    pass_second()

    ready("w_one")
    halo_1.wait_recv()
    halo_1.spread(x1, x12)
    total = jnp.zeros((cells, w_one.shape[1]), F32)
    for k, (u, v) in enumerate(OFFSETS):
        total += matmul(window(x1, x12, -u, -v, rows), w_one[k], NT)
    grad_stage[...] = total.astype(BF).reshape(grad_stage.shape)
    for row in range(rows):
        load("out", grad_stage.at[row], grad_out.at[:, row])

    wait_tokens(7, 8)
    send_planes(0, plane_sum(0, s1a, q1a, s3a.shape[0]), s2a, q2a)
    send_planes(1, second_sums(s3b.shape[0]), s2b, q2b)
    send_last(0, s2a, q2a, s3a, q3a)
    send_last(1, s2b, q2b, s3b, q3b)
    ready("out")
    for halo in (halo_h, halo_p, halo_e, halo_2, halo_1):
        halo.wait_send()
    for copy in mates:
        copy.wait_send()
    lead_group.wait_send()
    for number in range(4):
        line_group(number).wait_send()
    share_group(0, s1a, q1a).wait_send()
    plane_group(1, s2b, q2b, own_share, "wait_send")
    plane_group(0, s2a, q2a, own_share, "wait_send")
    final_sum(0, q3a, first_out)
    final_sum(1, q3b, second_out)
    @pl.when(gathers)
    def _():
        last_group(1, q3b, n_lead - 1).wait_send()
        last_group(0, q3a, n_lead - 1).wait_send()


def write_out(input_grad, grad_first, grad_second, grad_out, first_out, second_out, first, second, sem):
    copies = [pltpu.make_async_copy(input_grad, grad_out, sem.at[0])]
    copies[0].start()
    for number, (grad, line, out) in enumerate(((grad_first, first, first_out), (grad_second, second, second_out))):
        width = grad.shape[1]
        for row in range(grad.shape[0]):
            line[pl.ds(row * width, width)] = grad[row]
        copies.append(pltpu.make_async_copy(line, out, sem.at[1 + number]))
        copies[-1].start()
    for copy in copies:
        copy.wait()


def per_device(head_grads, head_weights, encoder_input, pre_first, pre_second, w_first, w_second):
    heads, batch_all, rows, cols, head_width = head_grads.shape
    samples, _, _, in_width = encoder_input.shape
    width = head_weights.shape[2]
    taps = len(OFFSETS)
    n_lead, n_lat, n_lon = lax.axis_size("lead"), lax.axis_size("lat"), lax.axis_size("lon")
    half = n_lat // 4
    seats = 4 * n_lon
    lanes = heads * head_width
    cells = samples * rows * cols
    cells_total = cells * n_lead * n_lat * n_lon
    rows_two, rows_one = taps * width, taps * in_width
    last_two, last_one = rows_two // (n_lat * n_lon), rows_one // (n_lat * n_lon)

    def field(batch, lane):
        full = (rows + 2, batch, cols, lane)
        units = rows * batch // UNIT
        return (
            pltpu.VMEM(full, BF),
            pltpu.VMEM((2,) + full, BF),
            pltpu.VMEM((2, units, UNIT, lane), F32),
            pltpu.VMEM((2, units + 2, UNIT, lane), F32),
        )

    def reduce_buffers(share):
        return (
            pltpu.VMEM((half // 2, share, width), BF),
            pltpu.VMEM((half, share, width), BF),
            pltpu.VMEM((share, width), BF),
            pltpu.VMEM((3, share, width), BF),
        )

    def line_buffers(first, then):
        return [pltpu.VMEM((first, then, last_two * half // 4, width), BF)] * 2

    own = (rows, samples, cols, width)
    act_field = field(samples, width)
    scratch = [
        *field(batch_all, lanes),
        pltpu.VMEM((taps, width, lanes), BF),
        act_field[0], *act_field,
        *field(samples, in_width),
        *field(samples, width),
        *field(samples, width),
        pltpu.VMEM(own, BF),
        pltpu.VMEM(own, F32),
        pltpu.VMEM(own, F32),
        pltpu.VMEM(w_first.shape, BF),
        pltpu.VMEM(w_second.shape, BF),
        pltpu.VMEM((n_lead,) + own, BF),
        pltpu.VMEM((n_lead,) + own, BF),
        pltpu.VMEM((2, batch_all * cols, width), F32),
        pltpu.VMEM((2, rows_two // 4, width), F32),
        pltpu.VMEM((rows_two, cells), BF),
        pltpu.VMEM((rows_one, cells), BF),
        pltpu.VMEM((2, rows_two // 4, cells), BF),
        pltpu.VMEM((2, rows_one // 4, cells), BF),
        pltpu.VMEM(own, BF),
        pltpu.VMEM(own, BF),
        *line_buffers(n_lon, 4),
        *line_buffers(4, n_lon),
        *[pltpu.VMEM((4, last_two * half // 4, width), BF)] * 2,
        *[pltpu.VMEM((n_lon, last_two * half // 4, width), BF)] * 2,
        *reduce_buffers(last_two),
        *[pltpu.VMEM((seats, last_one * half // 2, width), BF)] * 2,
        *reduce_buffers(last_one),
        pltpu.VMEM((rows, samples, cols, in_width), BF),
        pltpu.SemaphoreType.DMA((8,)),
        pltpu.SemaphoreType.DMA((5, 5)),
        pltpu.SemaphoreType.DMA((5, 5)),
        pltpu.SemaphoreType.DMA((1,)),
        pltpu.SemaphoreType.DMA((1,)),
        pltpu.SemaphoreType.DMA((4,)),
        pltpu.SemaphoreType.DMA((4,)),
        pltpu.SemaphoreType.DMA((4,)),
        pltpu.SemaphoreType.DMA((4,)),
        *[pltpu.SemaphoreType.DMA((2,)) for _ in range(6)],
        pltpu.SemaphoreType.REGULAR((14,)),
    ]
    anywhere = pl.BlockSpec(memory_space=pl.ANY)
    input_grad, grad_first, grad_second = pl.pallas_call(
        functools.partial(kernel, 1.0 / math.sqrt(cells_total)),
        out_shape=(
            jax.ShapeDtypeStruct(encoder_input.shape, BF),
            jax.ShapeDtypeStruct((last_one, width), F32),
            jax.ShapeDtypeStruct((last_two, width), F32),
        ),
        in_specs=[anywhere] * 7,
        out_specs=[anywhere] + [pl.BlockSpec(memory_space=pltpu.VMEM)] * 2,
        scratch_shapes=scratch,
        compiler_params=pltpu.CompilerParams(
            collective_id=0, has_side_effects=True, vmem_limit_bytes=55091 * 1024
        ),
    )(head_grads, head_weights, encoder_input, pre_first, pre_second, w_first, w_second)
    flat = [jax.ShapeDtypeStruct((grad.size,), F32) for grad in (grad_first, grad_second)]
    return pl.pallas_call(
        write_out,
        out_shape=(jax.ShapeDtypeStruct(input_grad.shape, BF), *flat),
        in_specs=[anywhere] + [pl.BlockSpec(memory_space=pltpu.VMEM)] * 2,
        out_specs=(anywhere, anywhere, anywhere),
        scratch_shapes=[
            pltpu.VMEM(flat[0].shape, F32),
            pltpu.VMEM(flat[1].shape, F32),
            pltpu.SemaphoreType.DMA((3,)),
        ],
        compiler_params=pltpu.CompilerParams(vmem_limit_bytes=2**20),
    )(input_grad, grad_first, grad_second)


def solution(mesh):
    tile = P("lead", "lat", "lon", None)
    in_specs = (P("lead", None, "lat", "lon", None), P("lead", None, None, None), tile, tile, tile, P(), P())
    out_specs = (tile, P(("lat", "lon")), P(("lat", "lon")))
    return jax.shard_map(
        per_device, mesh=mesh, in_specs=in_specs, out_specs=out_specs, check_vma=False
    )
```
